512 devices in a mesh: frame: 32 (over z_lo, y), chan: 16 (over x, z_hi, core).
Axes of the slice: x: 4, y: 4, z: 16 (z_hi: 2, z_lo: 8; z = z_hi * 8 + z_lo), core: 2. Of those that a mesh axis runs over, the one named last changes fastest.
Arguments:
- inputs: bfloat16 [1536, 12288], P('chan', 'frame'), may hold values from -6 to 6
- norm_gain: float32 [1536], replicated, may hold values from 0.5 to 2
- norm_bias: float32 [1536], replicated, may hold values from -3 to 3
- value_weight: bfloat16 [1536, 1536], P('chan'), may hold values from -0.15625 to 0.15625
- gate_weight: bfloat16 [1536, 1536], P('chan'), may hold values from -0.15625 to 0.15625
- conv_kernel: float32 [31, 1536], P(None, 'chan'), may hold values from -1 to 1
- project_weight: bfloat16 [1536, 1536], P('chan'), may hold values from -0.15625 to 0.15625
- frame_mask: int32 [12288], P('frame'), may hold values 0 or 1
- upstream: bfloat16 [1536, 12288], P('chan', 'frame'), may hold values from -6 to 6
Outputs:
- inputs_grad: bfloat16 [1536, 12288], P('chan', 'frame')
- value_grad: float32 [1536, 1536], P('chan', 'frame')
- gate_grad: float32 [1536, 1536], P('chan', 'frame')
- project_grad: float32 [1536, 1536], P('chan', 'frame')
- kernel_grad: float32 [31, 1536], P(None, 'chan')
- gain_grad: float32 [1536], P('chan')
- bias_grad: float32 [1536], P('chan')
The draws below stay inside these ranges and needn't reach their ends.
All inputs are finite; a program needn't handle non-finite values. No bound on the sum of `frame_mask` on one device may be relied on, other than what follows from the above.
Results may differ from the reference program's by a relative error of at most 0.025.
Values may be sent and summed in bfloat16 or wider, within the bound.
No kernel may reach another device: no remote copies, remote signals or barrier semaphores. Data moves between devices by JAX's collectives and lax.ppermute only.
A program may use at most 64 MiB of HBM per device.

```python
import math
import jax
import jax.numpy as jnp
from jax import lax

D = 1536
KW = 31
FRAMES = 12288
N_CHAN = 16


def set_ends(entries, rng, low, high):
    longest = entries.shape.index(max(entries.shape))
    spots = []
    for shift in (0, 1):
        where = [jax.random.randint(jax.random.fold_in(rng, axis), (), 0, length) for axis, length in enumerate(entries.shape)]
        where[longest] = (where[longest] + shift) % entries.shape[longest]
        spots.append(tuple(where))
    return entries.at[spots[0]].set(low).at[spots[1]].set(high)


def with_spikes(values, own_key, source, target, blocks, factor):
    def block_of(axis_at):
        return (jnp.arange(values.shape[axis_at]) // (values.shape[axis_at] // blocks)).reshape((-1,) + (1,) * (values.ndim - 1 - axis_at))

    first = jax.random.permutation(own_key, blocks)[block_of(target)]
    far = (block_of(target) + blocks // 2) % blocks
    return jnp.where((block_of(source) == first) | (block_of(source) == far), factor * values, values)


def block_levels(key, extent, pieces, smallest, high):
    factor_of = 1.0
    for position, shards_of in pieces:
        heights = jax.random.uniform(jax.random.fold_in(jax.random.fold_in(key, 6), position), (shards_of,), jnp.float32, smallest / len(pieces), high / len(pieces))
        factor_of = factor_of * jnp.repeat(jnp.exp(heights), extent[position] // shards_of).reshape((-1,) + (1,) * (len(extent) - 1 - position))
    return factor_of


def normal_values(own_key, shape, width, most, pieces=(), dtype=jnp.bfloat16):
    values = jax.random.normal(own_key, shape, jnp.float32) * width
    if len(pieces) > 0:
        values = block_levels(own_key, shape, pieces, -0.22, 0.18) * values
    return jnp.clip(values, min=-most, max=most).astype(dtype)


def bell_draw_with(stream_key, shape, width, most, split, heavy, held_as=jnp.bfloat16):
    entries = width * jax.random.normal(stream_key, shape, jnp.float32)
    if split:
        entries = entries * block_levels(stream_key, shape, split, -0.22, 0.18)
    return jnp.clip(with_spikes(entries, jax.random.fold_in(stream_key, 3), *heavy), -most, most).astype(held_as)


def setup_inputs(seed: int = 0) -> dict:
    key_list = jax.random.split(jax.random.key(seed), 10)
    inputs = normal_values(key_list[0], (D, FRAMES), 1.0, 6.0, ((0, 16), (1, 32)))
    norm_gain = jnp.clip(jnp.exp(jax.random.uniform(key_list[1], (D,), jnp.float32, math.log(0.5), math.log(2.0))), 0.5, 2.0)
    norm_bias = normal_values(key_list[2], (D,), 0.5, 3.0, (), jnp.float32)
    value_weight = normal_values(key_list[3], (D, D), D ** -0.5, 0.15625, ((0, 16),))
    gate_weight = normal_values(key_list[4], (D, D), D ** -0.5, 0.15625, ((0, 16),))
    conv_kernel = normal_values(key_list[5], (KW, D), KW ** -0.5, 1.0, ((1, 16),), jnp.float32)
    project_weight = normal_values(key_list[6], (D, D), D ** -0.5, 0.15625, ((0, 16),))
    frame_mask = set_ends((jax.random.randint(key_list[7], (FRAMES,), 0, 8) < 7).astype(jnp.int32), jax.random.fold_in(key_list[7], 1), 0, 1)
    upstream = bell_draw_with(key_list[8], (D, FRAMES), 1.0, 6.0, ((0, 16), (1, 32)), (1, 0, 32, 2.75))
    return dict(inputs=inputs, norm_gain=norm_gain, norm_bias=norm_bias, value_weight=value_weight, gate_weight=gate_weight, conv_kernel=conv_kernel, project_weight=project_weight, frame_mask=frame_mask, upstream=upstream)


eps = 1e-05

def reference(inputs, norm_gain, norm_bias, value_weight, gate_weight, conv_kernel, project_weight, frame_mask, upstream):
    model_width = inputs.shape[0]
    frames = inputs.shape[1]
    taps = conv_kernel.shape[0]
    reach = taps // 2
    x_float = inputs.astype(jnp.float32)
    row_mean = lax.optimization_barrier(jnp.mean(x_float, axis=0, keepdims=True))
    row_var = lax.optimization_barrier(jnp.mean(x_float * x_float, axis=0, keepdims=True)) - row_mean * row_mean
    inv_std = lax.rsqrt(row_var + eps)
    centred = (x_float - row_mean) * inv_std
    normed = (centred * norm_gain[:, None] + norm_bias[:, None]).astype(jnp.bfloat16)
    value_proj = jnp.dot(value_weight, normed, preferred_element_type=jnp.float32)
    gate_proj = jnp.dot(gate_weight, normed, preferred_element_type=jnp.float32)
    gate_sig = jax.nn.sigmoid(gate_proj)
    keep = frame_mask.astype(jnp.float32)[None, :]
    glu_out = (value_proj * gate_sig * keep).astype(jnp.bfloat16)
    padded = jnp.pad(glu_out, ((0, 0), (reach, reach)))
    conv_out = jnp.zeros((model_width, frames), jnp.float32)
    for k in range(taps):
        conv_out = conv_out + conv_kernel[k][:, None] * padded[:, k:k + frames].astype(jnp.float32)
    conv_sig = jax.nn.sigmoid(conv_out)
    activated = (conv_out * conv_sig).astype(jnp.bfloat16)
    act_grad = jnp.dot(project_weight, upstream, preferred_element_type=jnp.float32).astype(jnp.bfloat16)
    project_grad = lax.dot_general(activated, upstream, (((1,), (1,)), ((), ())), preferred_element_type=jnp.float32)
    conv_grad = (act_grad.astype(jnp.float32) * (conv_sig + conv_out * conv_sig * (1.0 - conv_sig))).astype(jnp.bfloat16)
    back_pad = jnp.pad(conv_grad, ((0, 0), (reach, reach)))
    grad_float = conv_grad.astype(jnp.float32)
    glu_grad = jnp.zeros((model_width, frames), jnp.float32)
    kernel_rows = []
    for k in range(taps):
        glu_grad = glu_grad + conv_kernel[k][:, None] * back_pad[:, 2 * reach - k:2 * reach - k + frames].astype(jnp.float32)
        kernel_rows.append(lax.optimization_barrier(jnp.sum(grad_float * padded[:, k:k + frames].astype(jnp.float32), axis=1)))
    kernel_grad = jnp.stack(kernel_rows)
    glu_grad = glu_grad * keep
    value_back = (glu_grad * gate_sig).astype(jnp.bfloat16)
    gate_back = (glu_grad * value_proj * gate_sig * (1.0 - gate_sig)).astype(jnp.bfloat16)
    block = model_width // N_CHAN
    normed_grad = jnp.zeros((model_width, frames), jnp.float32)
    for j in range(N_CHAN):
        lower = j * block
        partial_term = lax.dot_general(value_weight[lower:lower + block], value_back[lower:lower + block], (((0,), (0,)), ((), ())), preferred_element_type=jnp.float32)
        partial_term = partial_term + lax.dot_general(gate_weight[lower:lower + block], gate_back[lower:lower + block], (((0,), (0,)), ((), ())), preferred_element_type=jnp.float32)
        rounded = lax.optimization_barrier(partial_term.astype(jnp.bfloat16))
        normed_grad = normed_grad + rounded.astype(jnp.float32)
    value_grad = lax.dot_general(value_back, normed, (((1,), (1,)), ((), ())), preferred_element_type=jnp.float32)
    gate_grad = lax.dot_general(gate_back, normed, (((1,), (1,)), ((), ())), preferred_element_type=jnp.float32)
    gain_grad = lax.optimization_barrier(jnp.sum(normed_grad * centred, axis=1))
    bias_grad = lax.optimization_barrier(jnp.sum(normed_grad, axis=1))
    scaled = normed_grad * norm_gain[:, None]
    first_sum = lax.optimization_barrier(jnp.sum(scaled, axis=0, keepdims=True)) / model_width
    second_sum = lax.optimization_barrier(jnp.sum(scaled * centred, axis=0, keepdims=True)) / model_width
    inputs_grad = (upstream.astype(jnp.float32) + inv_std * (scaled - first_sum - centred * second_sum)).astype(jnp.bfloat16)
    return (inputs_grad, value_grad, gate_grad, project_grad, kernel_grad, gain_grad, bias_grad)
```

```python
import jax
import jax.numpy as jnp
from jax import lax
from jax.sharding import Mesh, PartitionSpec as P

eps = 1e-05
CHAN = ("x", "zh", "core")
FRAME = ("zl", "y")
SWAP = [(0, 1), (1, 0)]
f32 = jnp.float32
bf16 = jnp.bfloat16


def swap(value, axis):
    return lax.ppermute(value, axis, SWAP)


def ordered(own, other, index, axis):
    return jnp.where(
        index == 0, jnp.stack([own, other], axis), jnp.stack([other, own], axis)
    )


def halo(cells, width):
    count = 32
    head = cells[:, :width]
    tail = cells[:, cells.shape[1] - width :]
    left = lax.ppermute(tail, FRAME, [(i, i + 1) for i in range(count - 1)])
    right = lax.ppermute(head, FRAME, [(i + 1, i) for i in range(count - 1)])
    return jnp.concatenate([left, cells, right], axis=1)


def split_bf16(value):
    high = value.astype(bf16)
    return high, (value - high.astype(f32)).astype(bf16)


def on_device(
    inputs,
    norm_gain,
    norm_bias,
    value_weight,
    gate_weight,
    conv_kernel,
    project_weight,
    frame_mask,
    upstream,
):
    width, rows = inputs.shape
    model = value_weight.shape[1]
    taps = conv_kernel.shape[0]
    reach = taps // 2
    zh = lax.axis_index("zh")
    core = lax.axis_index("core")
    offset = lax.axis_index(CHAN) * width

    in_other = swap(inputs, "zh")
    in_pair = ordered(inputs, in_other, zh, 0)
    up_other = swap(lax.optimization_barrier((upstream, in_other))[0], "zh")
    in_x = lax.all_gather(in_pair, "x", axis=0, tiled=False)
    in_core = swap(in_x, "core")
    full_inputs = ordered(in_x, in_core, core, 2).reshape(model, rows)

    up_pair = ordered(upstream, up_other, zh, 0)
    up_pair = lax.optimization_barrier((up_pair, in_x))[0]
    up_x = lax.all_to_all(
        jnp.broadcast_to(up_pair[None], (4, 2, width, rows)), "x", 0, 0, tiled=True
    )
    up_core = swap(up_x, "core")
    full_grads = ordered(up_x, up_core, core, 2).reshape(model, rows)

    x_float = full_inputs.astype(f32)
    row_mean = jnp.mean(x_float, axis=0, keepdims=True)
    row_var = jnp.mean(x_float * x_float, axis=0, keepdims=True) - row_mean * row_mean
    inv_std = lax.rsqrt(row_var + eps)
    centred = (x_float - row_mean) * inv_std
    normed = (centred * norm_gain[:, None] + norm_bias[:, None]).astype(bf16)
    centred_local = (inputs.astype(f32) - row_mean) * inv_std
    gain_local = lax.dynamic_slice_in_dim(norm_gain, offset, width, 0)[:, None]

    value_proj = jnp.dot(value_weight, normed, preferred_element_type=f32)
    gate_proj = jnp.dot(gate_weight, normed, preferred_element_type=f32)
    gate_sig = jax.nn.sigmoid(gate_proj)
    keep = frame_mask.astype(f32)[None, :]
    glu_out = (value_proj * gate_sig * keep).astype(bf16)
    padded = halo(glu_out, reach)
    conv_out = jnp.zeros((width, rows), f32)
    for k in range(taps):
        conv_out = conv_out + conv_kernel[k][:, None] * padded[:, k : k + rows].astype(f32)
    conv_sig = jax.nn.sigmoid(conv_out)
    activated = (conv_out * conv_sig).astype(bf16)

    act_grad = jnp.dot(project_weight, full_grads, preferred_element_type=f32).astype(bf16)
    conv_grad = (
        act_grad.astype(f32) * (conv_sig + conv_out * conv_sig * (1.0 - conv_sig))
    ).astype(bf16)
    back_pad = halo(conv_grad, reach)
    grad_float = conv_grad.astype(f32)
    glu_grad = jnp.zeros((width, rows), f32)
    kernel_rows = []
    for k in range(taps):
        glu_grad = glu_grad + conv_kernel[k][:, None] * back_pad[
            :, 2 * reach - k : 2 * reach - k + rows
        ].astype(f32)
        kernel_rows.append(
            jnp.sum(grad_float * padded[:, k : k + rows].astype(f32), axis=1)
        )
    kernel_part = jnp.stack(kernel_rows)
    glu_grad = glu_grad * keep
    value_back = (glu_grad * gate_sig).astype(bf16)
    gate_back = (glu_grad * value_proj * gate_sig * (1.0 - gate_sig)).astype(bf16)

    across = (((0,), (0,)), ((), ()))
    partial = (
        lax.dot_general(value_weight, value_back, across, preferred_element_type=f32)
        + lax.dot_general(gate_weight, gate_back, across, preferred_element_type=f32)
    ).astype(bf16)
    scaled = partial.astype(f32) * norm_gain[:, None]
    sums = jnp.stack([jnp.sum(scaled, axis=0), jnp.sum(scaled * centred, axis=0)])
    sums_high, sums_low = split_bf16(sums)
    blocks = partial.reshape(4, 2, 2, width, rows)
    far = jnp.where(zh == 0, blocks[:, 1], blocks[:, 0]).reshape(8, width, rows)
    near = jnp.where(zh == 0, blocks[:, 0], blocks[:, 1]).reshape(8, width, rows)
    extra = jnp.concatenate([sums_high, sums_low, jnp.zeros((12, rows), bf16)])
    far = jnp.concatenate([far, jnp.broadcast_to(extra[None], (8, 16, rows))], axis=1)
    far = lax.all_to_all(far, ("x", "core"), 0, 0, tiled=True)
    far = jnp.sum(far.astype(f32), axis=0)
    far_sums = far[width : width + 2] + far[width + 2 : width + 4]
    sent_high, sent_low = split_bf16(far_sums)
    far = jnp.concatenate(
        [far[:width].astype(bf16), sent_high, sent_low, jnp.zeros((12, rows), bf16)]
    )
    came = swap(far, "zh").astype(f32)
    near = lax.optimization_barrier((near, far))[0]
    near = lax.all_to_all(near, ("x", "core"), 0, 0, tiled=True)
    normed_grad = jnp.sum(near.astype(f32), axis=0) + came[:width]
    sums = (far_sums + came[width : width + 2] + came[width + 2 : width + 4]) / model

    inputs_grad = (
        upstream.astype(f32)
        + inv_std * (normed_grad * gain_local - sums[0:1] - centred_local * sums[1:2])
    ).astype(bf16)
    tail = jnp.stack([jnp.sum(normed_grad * centred_local, axis=1), jnp.sum(normed_grad, axis=1)])
    tail = lax.all_to_all(
        jnp.broadcast_to(tail[None], (32, 2, width)), FRAME, 0, 0, tiled=True
    )
    tail = jnp.sum(tail, axis=0)

    over = (((1,), (1,)), ((), ()))
    zero = jnp.zeros((width, rows), bf16)
    grads = lax.dot_general(
        normed,
        jnp.concatenate([value_back, gate_back, zero, zero]),
        over,
        preferred_element_type=f32,
    ) + lax.dot_general(
        full_grads,
        jnp.concatenate([zero, zero, activated, zero]),
        over,
        preferred_element_type=f32,
    )
    piece = model // 32
    grads = grads.reshape(8, 4, piece, 4 * width).transpose(1, 0, 2, 3).astype(bf16)
    tap_high, tap_low = split_bf16(
        jnp.pad(kernel_part, ((0, piece - taps), (3 * width, 0)))
    )
    grads = jnp.concatenate(
        [
            grads[:, 0:1] + tap_high[None, None],
            grads[:, 1:2] + tap_low[None, None],
            grads[:, 2:],
        ],
        axis=1,
    )
    grads = lax.all_to_all(grads, "y", 0, 0, tiled=True)
    grads = jnp.sum(grads.astype(f32), axis=0)
    own_taps = (grads[0] + grads[1])[:, 3 * width :]
    grads = jnp.concatenate(
        [
            grads[:, :, : 3 * width].astype(bf16),
            jnp.broadcast_to(own_taps.astype(bf16)[None], (8, piece, width)),
        ],
        axis=2,
    )
    grads = lax.all_to_all(grads, "zl", 0, 0, tiled=True)
    grads = jnp.sum(grads.astype(f32), axis=0)
    value_grad = grads[:, :width].T
    gate_grad = grads[:, width : 2 * width].T
    project_grad = grads[:, 2 * width : 3 * width].T
    kernel_grad = grads[:taps, 3 * width :]
    return (inputs_grad, value_grad, gate_grad, project_grad, kernel_grad, tail[0], tail[1])


def solution(mesh):
    split = Mesh(mesh.devices.reshape(8, 4, 4, 2, 2), FRAME + CHAN)
    return jax.shard_map(
        on_device,
        mesh=split,
        in_specs=(
            P(CHAN, FRAME),
            P(),
            P(),
            P(CHAN, None),
            P(CHAN, None),
            P(None, CHAN),
            P(CHAN, None),
            P(FRAME),
            P(CHAN, FRAME),
        ),
        out_specs=(
            P(CHAN, FRAME),
            P(CHAN, FRAME),
            P(CHAN, FRAME),
            P(CHAN, FRAME),
            P(None, CHAN),
            P(CHAN),
            P(CHAN),
        ),
        check_vma=False,
    )
```

```python
import jax
import jax.numpy as jnp
from jax import lax
from jax.sharding import Mesh, PartitionSpec as P

eps = 1e-05
CHAN = ("x", "zh", "core")
FRAME = ("zl", "y")
SWAP = [(0, 1), (1, 0)]
f32 = jnp.float32
bf16 = jnp.bfloat16


def swap(value, axis):
    return lax.ppermute(value, axis, SWAP)


def ordered(own, other, index, axis):
    return jnp.where(
        index == 0, jnp.stack([own, other], axis), jnp.stack([other, own], axis)
    )


def over_x(pair):
    return lax.all_to_all(
        jnp.broadcast_to(pair[None], (4,) + pair.shape), "x", 0, 0, tiled=True
    )


def halo(cells, width):
    count = 32
    head = cells[:, :width]
    tail = cells[:, cells.shape[1] - width :]
    left = lax.ppermute(tail, FRAME, [(i, i + 1) for i in range(count - 1)])
    right = lax.ppermute(head, FRAME, [(i + 1, i) for i in range(count - 1)])
    return jnp.concatenate([left, cells, right], axis=1)


def split_bf16(value):
    high = value.astype(bf16)
    return high, (value - high.astype(f32)).astype(bf16)


def on_device(
    inputs,
    norm_gain,
    norm_bias,
    value_weight,
    gate_weight,
    conv_kernel,
    project_weight,
    frame_mask,
    upstream,
):
    width, rows = inputs.shape
    model = value_weight.shape[1]
    taps = conv_kernel.shape[0]
    reach = taps // 2
    zh = lax.axis_index("zh")
    core = lax.axis_index("core")
    offset = lax.axis_index(CHAN) * width

    in_other = swap(inputs, "zh")
    in_pair = ordered(inputs, in_other, zh, 0)
    upstream_late, in_pair = lax.optimization_barrier((upstream, in_pair))
    in_x = over_x(in_pair)
    up_other = swap(upstream_late, "zh")
    in_core = swap(in_x, "core")
    full_inputs = ordered(in_x, in_core, core, 2).reshape(model, rows)
    up_pair = ordered(upstream, up_other, zh, 0)
    up_x = over_x(up_pair)

    x_float = full_inputs.astype(f32)
    row_mean = jnp.mean(x_float, axis=0, keepdims=True)
    row_var = jnp.mean(x_float * x_float, axis=0, keepdims=True) - row_mean * row_mean
    inv_std = lax.rsqrt(row_var + eps)
    centred = (x_float - row_mean) * inv_std
    normed = (centred * norm_gain[:, None] + norm_bias[:, None]).astype(bf16)
    centred_local = (inputs.astype(f32) - row_mean) * inv_std
    gain_local = lax.dynamic_slice_in_dim(norm_gain, offset, width, 0)[:, None]

    value_proj = jnp.dot(value_weight, normed, preferred_element_type=f32)
    gate_proj = jnp.dot(gate_weight, normed, preferred_element_type=f32)
    gate_sig = jax.nn.sigmoid(gate_proj)
    keep = frame_mask.astype(f32)[None, :]
    glu_out = (value_proj * gate_sig * keep).astype(bf16)
    up_x, glu_out = lax.optimization_barrier((up_x, glu_out))
    padded = halo(glu_out, reach)
    up_core = swap(up_x, "core")
    full_grads = ordered(up_x, up_core, core, 2).reshape(model, rows)
    conv_out = jnp.zeros((width, rows), f32)
    for k in range(taps):
        conv_out = conv_out + conv_kernel[k][:, None] * padded[:, k : k + rows].astype(f32)
    conv_sig = jax.nn.sigmoid(conv_out)
    activated = (conv_out * conv_sig).astype(bf16)

    act_grad = jnp.dot(project_weight, full_grads, preferred_element_type=f32).astype(bf16)
    conv_grad = (
        act_grad.astype(f32) * (conv_sig + conv_out * conv_sig * (1.0 - conv_sig))
    ).astype(bf16)
    back_pad = halo(conv_grad, reach)
    grad_float = conv_grad.astype(f32)
    glu_grad = jnp.zeros((width, rows), f32)
    kernel_rows = []
    for k in range(taps):
        glu_grad = glu_grad + conv_kernel[k][:, None] * back_pad[
            :, 2 * reach - k : 2 * reach - k + rows
        ].astype(f32)
        kernel_rows.append(
            jnp.sum(grad_float * padded[:, k : k + rows].astype(f32), axis=1)
        )
    kernel_part = jnp.stack(kernel_rows)
    glu_grad = glu_grad * keep
    value_back = (glu_grad * gate_sig).astype(bf16)
    gate_back = (glu_grad * value_proj * gate_sig * (1.0 - gate_sig)).astype(bf16)

    both = jnp.concatenate([value_back, gate_back])
    weights = jnp.concatenate([value_weight, gate_weight])
    by_gain = jnp.sum(weights.astype(f32) * norm_gain[None, :], axis=1, keepdims=True)
    by_bias = jnp.sum(weights.astype(f32) * norm_bias[None, :], axis=1, keepdims=True)
    proj = jnp.concatenate([value_proj, gate_proj])
    sums = jnp.stack(
        [
            jnp.sum(both.astype(f32) * by_gain, axis=0),
            jnp.sum(both.astype(f32) * (proj - by_bias), axis=0),
        ]
    )
    sums_high, sums_low = split_bf16(sums)
    blocks = weights.reshape(2 * width, 4, 2, 2, width)
    far_w = jnp.where(zh == 0, blocks[:, :, 1], blocks[:, :, 0]).reshape(2 * width, -1)
    near_w = jnp.where(zh == 0, blocks[:, :, 0], blocks[:, :, 1]).reshape(2 * width, -1)
    across = (((0,), (0,)), ((), ()))
    far = lax.dot_general(far_w, both, across, preferred_element_type=f32).astype(bf16)
    near = lax.dot_general(near_w, both, across, preferred_element_type=f32).astype(bf16)
    extra = jnp.concatenate([sums_high, sums_low, jnp.zeros((12, rows), bf16)])
    far = jnp.concatenate(
        [far.reshape(8, width, rows), jnp.broadcast_to(extra[None], (8, 16, rows))], axis=1
    )
    far, both = lax.optimization_barrier((far, both))
    far = lax.all_to_all(far, ("x", "core"), 0, 0, tiled=True)
    over = (((1,), (1,)), ((), ()))
    zero = jnp.zeros((width, rows), bf16)
    grads = lax.dot_general(
        normed,
        jnp.concatenate([both, zero, zero]),
        over,
        preferred_element_type=f32,
    ) + lax.dot_general(
        full_grads,
        jnp.concatenate([zero, zero, activated, zero]),
        over,
        preferred_element_type=f32,
    )
    piece = model // 32
    grads = grads.reshape(8, 4, piece, 4 * width)
    taps_part = jnp.pad(kernel_part, ((0, piece - taps), (3 * width, 0)))
    y = lax.axis_index("y")
    zl = lax.axis_index("zl")

    def rows_for(step):
        index = (y + step) % 4
        return lax.dynamic_slice_in_dim(grads, index, 1, 1)[:, 0]

    total = rows_for(0) + taps_part
    for step in (1, 3, 2):
        sent = (rows_for(step) + taps_part).astype(bf16)
        total = total + lax.ppermute(sent, "y", [(i, (i + step) % 4) for i in range(4)]).astype(f32)
    near, far, total = lax.optimization_barrier((near, far, total))
    near = lax.all_to_all(near, ("x", "core"), 0, 0, tiled=True)
    far = jnp.sum(far.astype(f32), axis=0)
    far_sums = far[width : width + 2] + far[width + 2 : width + 4]
    sent_high, sent_low = split_bf16(far_sums)
    far = jnp.concatenate(
        [far[:width].astype(bf16), sent_high, sent_low, jnp.zeros((12, rows), bf16)]
    )
    came = swap(far, "zh").astype(f32)
    near = near.reshape(8, width, rows)
    normed_grad = jnp.sum(near.astype(f32), axis=0) + came[:width]
    sums = (far_sums + came[width : width + 2] + came[width + 2 : width + 4]) / model

    inputs_grad = (
        upstream.astype(f32)
        + inv_std * (normed_grad * gain_local - sums[0:1] - centred_local * sums[1:2])
    ).astype(bf16)
    tail = jnp.stack([jnp.sum(normed_grad * centred_local, axis=1), jnp.sum(normed_grad, axis=1)])
    tail = lax.all_to_all(
        jnp.broadcast_to(tail[None], (32, 2, width)), FRAME, 0, 0, tiled=True
    )
    tail = jnp.sum(tail, axis=0)

    for size in (4, 2, 1):
        side = (zl // size) % 2
        kept = lax.dynamic_slice_in_dim(total, side * size, size, 0)
        sent = lax.dynamic_slice_in_dim(total, (1 - side) * size, size, 0).astype(bf16)
        total = kept + lax.ppermute(sent, "zl", [(i, i ^ size) for i in range(8)]).astype(f32)
    grads = total[0]
    value_grad = grads[:, :width].T
    gate_grad = grads[:, width : 2 * width].T
    project_grad = grads[:, 2 * width : 3 * width].T
    kernel_grad = grads[:taps, 3 * width :]
    return (inputs_grad, value_grad, gate_grad, project_grad, kernel_grad, tail[0], tail[1])


def solution(mesh):
    split = Mesh(mesh.devices.reshape(8, 4, 4, 2, 2), FRAME + CHAN)
    return jax.shard_map(
        on_device,
        mesh=split,
        in_specs=(
            P(CHAN, FRAME),
            P(),
            P(),
            P(CHAN, None),
            P(CHAN, None),
            P(None, CHAN),
            P(CHAN, None),
            P(FRAME),
            P(CHAN, FRAME),
        ),
        out_specs=(
            P(CHAN, FRAME),
            P(CHAN, FRAME),
            P(CHAN, FRAME),
            P(CHAN, FRAME),
            P(None, CHAN),
            P(CHAN),
            P(CHAN),
        ),
        check_vma=False,
    )
```

```python
import jax
import jax.numpy as jnp
from jax import lax
from jax.experimental import pallas as pl
from jax.experimental.pallas import tpu as pltpu
from jax.sharding import Mesh, PartitionSpec as P

eps = 1e-05
CHAN = ("x", "zh", "core")
FRAME = ("zl", "y")
SWAP = [(0, 1), (1, 0)]
f32 = jnp.float32
bf16 = jnp.bfloat16
VMEM = pl.BlockSpec(memory_space=pltpu.VMEM)
SMEM = pl.BlockSpec(memory_space=pltpu.SMEM)
OVER = (((1,), (1,)), ((), ()))


def swap(value, axis):
    return lax.ppermute(value, axis, SWAP)


def over_x(pair):
    return lax.all_to_all(
        jnp.broadcast_to(pair[None], (4,) + pair.shape), "x", 0, 0, tiled=True
    )


def split_bf16(value):
    high = value.astype(bf16)
    return high, (value - high.astype(f32)).astype(bf16)


def shape(dims, dtype):
    return jax.ShapeDtypeStruct(dims, dtype)


def call(kernel, outs, scratch=(), specs=None):
    return pl.pallas_call(
        kernel,
        out_shape=outs,
        in_specs=specs,
        out_specs=tuple(VMEM for _ in outs),
        scratch_shapes=list(scratch),
        compiler_params=pltpu.CompilerParams(vmem_limit_bytes=48 << 20),
    )


def blocks_of(where_ref, own_ref, other_ref):
    zh, core = where_ref[0], where_ref[1]
    for x in range(4):
        for far in range(2):
            side = zh if far == 0 else 1 - zh
            yield x * 4 + side * 2 + core, own_ref.at[x, far]
            yield x * 4 + side * 2 + 1 - core, other_ref.at[x, far]


def forward(
    where_ref, own_ref, other_ref, gain_ref, bias_ref, weight_ref, taps_ref, mask_ref,
    normed_ref, stats_ref, proj_ref, glu_ref, conv_ref,
):
    model = weight_ref.shape[1]
    width = own_ref.shape[2]
    lanes = own_ref.shape[3]
    total = jnp.zeros((8, lanes), f32)
    square = jnp.zeros((8, lanes), f32)
    for _, block in blocks_of(where_ref, own_ref, other_ref):
        x = block[...].astype(f32).reshape(width // 8, 8, lanes)
        total = total + jnp.sum(x, axis=0)
        square = square + jnp.sum(x * x, axis=0)
    row_mean = jnp.sum(total, axis=0, keepdims=True) / model
    row_var = jnp.sum(square, axis=0, keepdims=True) / model - row_mean * row_mean
    inv_std = lax.rsqrt(row_var + eps)
    stats_ref[...] = jnp.concatenate(
        [row_mean, inv_std, jnp.zeros((6, lanes), f32)], axis=0
    )
    for place, block in blocks_of(where_ref, own_ref, other_ref):
        centred = (block[...].astype(f32) - row_mean) * inv_std
        normed_ref[place] = (centred * gain_ref[place] + bias_ref[place]).astype(bf16)
    proj = jnp.dot(
        weight_ref[...], normed_ref[...].reshape(model, lanes), preferred_element_type=f32
    )
    proj_ref[...] = proj
    glu = (proj[:width] * jax.nn.sigmoid(proj[width:]) * mask_ref[...]).astype(bf16)
    glu_ref[...] = glu
    glu = glu.astype(f32)
    taps = taps_ref.shape[0]
    conv = jnp.zeros((width, lanes), f32)
    for k in range(taps):
        conv = conv + taps_ref[k] * pltpu.roll(glu, (taps // 2 - k) % lanes, 1)
    conv_ref[...] = conv


def backward(
    where_ref, own_ref, other_ref, edge_own_ref, edge_other_ref, project_ref, flipped_ref,
    by_gain_ref, by_bias_ref, taps_ref, mask_ref, proj_ref, glu_ref, conv_ref,
    far_ref, near_ref, full_ref, both_ref, act_ref, kernel_ref,
    wide_ref, partial_ref,
):
    model = project_ref.shape[1]
    width, lanes = conv_ref.shape
    rows = own_ref.shape[3]
    taps = taps_ref.shape[0]
    reach = taps // 2
    for (place, block), (_, edge) in zip(
        blocks_of(where_ref, own_ref, other_ref),
        blocks_of(where_ref, edge_own_ref, edge_other_ref),
    ):
        full_ref[place] = block[...]
        wide_ref[place, :, :rows] = block[...]
        wide_ref[place, :, rows:] = pltpu.roll(edge[:, rows:].astype(f32), 64, 1).astype(bf16)
    act_grad = jnp.dot(
        project_ref[...], wide_ref[...].reshape(model, lanes), preferred_element_type=f32
    ).astype(bf16)
    conv = conv_ref[...]
    sig = jax.nn.sigmoid(conv)
    act_ref[...] = (conv * sig)[:, :rows].astype(bf16)
    grad = (act_grad.astype(f32) * (sig + conv * sig * (1.0 - sig))).astype(bf16).astype(f32)
    glu = glu_ref[...].astype(f32)
    inner = grad[:, :rows]
    glu_grad = jnp.zeros((width, rows), f32)
    lane = lax.broadcasted_iota(jnp.int32, (width, 128), 1)
    kernel = jnp.zeros((width, 128), f32)
    for k in range(taps):
        glu_grad = glu_grad + taps_ref[k] * pltpu.roll(grad, (k - reach) % lanes, 1)[:, :rows]
        seen = jnp.sum(
            inner * pltpu.roll(glu, (reach - k) % lanes, 1)[:, :rows], axis=1, keepdims=True
        )
        kernel = jnp.where(lane == k, seen, kernel)
    kernel_ref[...] = kernel
    glu_grad = glu_grad * mask_ref[:, :rows]
    proj = proj_ref[:, :rows]
    value = proj[:width]
    gate = jax.nn.sigmoid(proj[width:])
    both_ref[:width] = (glu_grad * gate).astype(bf16)
    both_ref[width:] = (glu_grad * value * gate * (1.0 - gate)).astype(bf16)
    both = both_ref[...]
    partial = jnp.dot(flipped_ref[...], both, preferred_element_type=f32).astype(bf16)
    partial_ref[...] = partial.reshape(partial_ref.shape)
    both = both.astype(f32)
    first = jnp.sum(both * by_gain_ref[...], axis=0, keepdims=True)
    second = jnp.sum(both * (proj - by_bias_ref[...]), axis=0, keepdims=True)
    first_high = first.astype(bf16).astype(f32)
    second_high = second.astype(bf16).astype(f32)
    row = lax.broadcasted_iota(jnp.int32, (16, rows), 0)
    extra = jnp.where(row == 0, first_high, 0.0)
    extra = jnp.where(row == 1, second_high, extra)
    extra = jnp.where(row == 2, first - first_high, extra)
    extra = jnp.where(row == 3, second - second_high, extra).astype(bf16)
    zh = where_ref[0]
    for x in range(4):
        for core in range(2):
            far_ref[x * 2 + core, :width] = partial_ref[x, 1 - zh, core]
            far_ref[x * 2 + core, width:] = extra
            near_ref[x * 2 + core] = partial_ref[x, zh, core]


def weights_of(normed_ref, full_ref, both_ref, act_ref, kernel_ref, grads_ref):
    rows = full_ref.shape[2]
    width = act_ref.shape[0]
    model = normed_ref.shape[0] * width
    zero = jnp.zeros((width, rows), bf16)
    grads = lax.dot_general(
        normed_ref[:, :, :rows].reshape(model, rows),
        jnp.concatenate([zero, both_ref[...], zero], axis=0),
        OVER,
        preferred_element_type=f32,
    ) + lax.dot_general(
        full_ref[...].reshape(model, rows),
        jnp.concatenate([zero, zero, zero, act_ref[...]], axis=0),
        OVER,
        preferred_element_type=f32,
    )
    grads_ref[...] = grads.astype(bf16).reshape(grads_ref.shape)
    piece = grads_ref.shape[2]
    kernel = jnp.transpose(kernel_ref[...])[:piece].astype(bf16)
    for zl in range(8):
        for y in range(4):
            grads_ref[zl, y, :, :width] = kernel


def on_device(
    inputs,
    norm_gain,
    norm_bias,
    value_weight,
    gate_weight,
    conv_kernel,
    project_weight,
    frame_mask,
    upstream,
):
    width, rows = inputs.shape
    model = value_weight.shape[1]
    taps = conv_kernel.shape[0]
    reach = taps // 2
    lanes = rows + 128
    piece = model // 32
    zh = lax.axis_index("zh")
    core = lax.axis_index("core")
    y = lax.axis_index("y")
    zl = lax.axis_index("zl")
    offset = lax.axis_index(CHAN) * width
    where = jnp.stack([zh, core]).astype(jnp.int32)

    def empty(height, count):
        return jnp.zeros((height, count), bf16)

    mask = frame_mask.astype(bf16)[None, :]
    up_reach, in_reach = reach, 2 * reach
    gap = 64 - in_reach
    to_right = jnp.concatenate(
        [
            jnp.concatenate(
                [
                    empty(width, 64 - up_reach),
                    upstream[:, rows - up_reach :],
                    empty(width, gap),
                    inputs[:, rows - in_reach :],
                ],
                axis=1,
            ),
            jnp.broadcast_to(
                jnp.concatenate([empty(1, 128 - in_reach), mask[:, rows - in_reach :]], axis=1),
                (16, 128),
            ),
        ]
    )
    to_left = jnp.concatenate(
        [
            jnp.concatenate(
                [
                    inputs[:, :in_reach],
                    empty(width, gap),
                    upstream[:, :up_reach],
                    empty(width, 64 - up_reach),
                ],
                axis=1,
            ),
            jnp.broadcast_to(
                jnp.concatenate([mask[:, :in_reach], empty(1, 128 - in_reach)], axis=1), (16, 128)
            ),
        ]
    )
    edge = lax.ppermute(to_right, FRAME, [(i, i + 1) for i in range(31)]) + lax.ppermute(
        to_left, FRAME, [(i + 1, i) for i in range(31)]
    )
    keep = jnp.concatenate([mask, edge[width : width + 1]], axis=1).astype(f32)

    held = jnp.concatenate([inputs, edge[:width], upstream], axis=1)
    came = swap(held, "zh")
    pair = jnp.stack([held, came])
    in_own = over_x(pair[:, :, :lanes])
    up_pair, in_own = lax.optimization_barrier((pair[:, :, lanes:], in_own))
    in_other = swap(in_own, "core")
    up_own = over_x(up_pair)

    weights = jnp.concatenate([value_weight, gate_weight])
    by_gain = jnp.sum(weights.astype(f32) * norm_gain[None, :], axis=1, keepdims=True)
    by_bias = jnp.sum(weights.astype(f32) * norm_bias[None, :], axis=1, keepdims=True)
    columns = conv_kernel.reshape(taps, width, 1)
    normed, stats, proj, glu, conv = call(
        forward,
        (
            shape((16, width, lanes), bf16),
            shape((8, lanes), f32),
            shape((2 * width, lanes), f32),
            shape((width, lanes), bf16),
            shape((width, lanes), f32),
        ),
        specs=[SMEM] + [VMEM] * 7,
    )(
        where, in_own, in_other, norm_gain.reshape(16, width, 1), norm_bias.reshape(16, width, 1),
        weights, columns, keep,
    )
    up_own, conv = lax.optimization_barrier((up_own, conv))
    up_other = swap(up_own, "core")
    far, near, full_grads, both, activated, kernel_part = call(
        backward,
        (
            shape((8, width + 16, rows), bf16),
            shape((8, width, rows), bf16),
            shape((16, width, rows), bf16),
            shape((2 * width, rows), bf16),
            shape((width, rows), bf16),
            shape((width, 128), f32),
        ),
        scratch=(
            pltpu.VMEM((16, width, lanes), bf16),
            pltpu.VMEM((4, 2, 2, width, rows), bf16),
        ),
        specs=[SMEM] + [VMEM] * 13,
    )(
        where, up_own, up_other, in_own, in_other, project_weight, weights.T,
        by_gain, by_bias, columns, keep, proj, glu, conv,
    )

    far, both = lax.optimization_barrier((far, both))
    far = lax.all_to_all(far, ("x", "core"), 0, 0, tiled=True)
    (grads,) = call(
        weights_of, (shape((8, 4, piece, 4 * width), bf16),), specs=[VMEM] * 5
    )(normed, full_grads, both, activated, kernel_part)

    def rows_for(step):
        return lax.dynamic_slice_in_dim(grads, (y + step) % 4, 1, 1)[:, 0]

    parts = [
        lax.ppermute(rows_for(step), "y", [(i, (i + step) % 4) for i in range(4)])
        for step in (1, 3, 2)
    ]
    near, far = lax.optimization_barrier((near, far))
    near = lax.all_to_all(near, ("x", "core"), 0, 0, tiled=True)
    far = jnp.sum(far.astype(f32), axis=0)
    far_sums = far[width : width + 2] + far[width + 2 : width + 4]
    sent_high, sent_low = split_bf16(far_sums)
    far = jnp.concatenate(
        [far[:width].astype(bf16), sent_high, sent_low, jnp.zeros((12, rows), bf16)]
    )
    came = swap(far, "zh").astype(f32)

    total = rows_for(0).astype(f32)
    for part in parts:
        total = total + part.astype(f32)

    def halve(total, size):
        side = (zl // size) % 2
        kept = lax.dynamic_slice_in_dim(total, side * size, size, 0)
        sent = lax.dynamic_slice_in_dim(total, (1 - side) * size, size, 0).astype(bf16)
        return kept + lax.ppermute(sent, "zl", [(i, i ^ size) for i in range(8)]).astype(f32)

    total = halve(total, 4)

    normed_grad = jnp.sum(near.astype(f32), axis=0) + came[:width]
    sums = (far_sums + came[width : width + 2] + came[width + 2 : width + 4]) / model
    gain_local = lax.dynamic_slice_in_dim(norm_gain, offset, width, 0)[:, None]
    inv_std = stats[1:2, :rows]
    centred = (inputs.astype(f32) - stats[0:1, :rows]) * inv_std
    tail = jnp.stack([jnp.sum(normed_grad * centred, axis=1), jnp.sum(normed_grad, axis=1)])
    tail, total = lax.optimization_barrier((tail, total))
    tail = lax.all_to_all(
        jnp.broadcast_to(tail[None], (32, 2, width)), FRAME, 0, 0, tiled=True
    )
    tail = jnp.sum(tail, axis=0)
    inputs_grad = (
        upstream.astype(f32)
        + inv_std * (normed_grad * gain_local - sums[0:1] - centred * sums[1:2])
    ).astype(bf16)

    grads = halve(halve(total, 2), 1)[0]
    kernel_grad = grads[:taps, :width]
    value_grad = grads[:, width : 2 * width].T
    gate_grad = grads[:, 2 * width : 3 * width].T
    project_grad = grads[:, 3 * width :].T
    return (inputs_grad, value_grad, gate_grad, project_grad, kernel_grad, tail[0], tail[1])


def solution(mesh):
    split = Mesh(mesh.devices.reshape(8, 4, 4, 2, 2), FRAME + CHAN)
    return jax.shard_map(
        on_device,
        mesh=split,
        in_specs=(
            P(CHAN, FRAME),
            P(),
            P(),
            P(CHAN, None),
            P(CHAN, None),
            P(None, CHAN),
            P(CHAN, None),
            P(FRAME),
            P(CHAN, FRAME),
        ),
        out_specs=(
            P(CHAN, FRAME),
            P(CHAN, FRAME),
            P(CHAN, FRAME),
            P(CHAN, FRAME),
            P(None, CHAN),
            P(CHAN),
            P(CHAN),
        ),
        check_vma=False,
    )
```

```python
import jax
import jax.numpy as jnp
from jax import lax
from jax.experimental import pallas as pl
from jax.experimental.pallas import tpu as pltpu
from jax.sharding import Mesh, PartitionSpec as P

eps = 1e-05
CHAN = ("x", "zh", "core")
FRAME = ("zl", "y")
SWAP = [(0, 1), (1, 0)]
f32 = jnp.float32
bf16 = jnp.bfloat16
VMEM = pl.BlockSpec(memory_space=pltpu.VMEM)
SMEM = pl.BlockSpec(memory_space=pltpu.SMEM)
OVER = (((1,), (1,)), ((), ()))


def swap(value, axis):
    return lax.ppermute(value, axis, SWAP)


def over_x(pair):
    return lax.all_to_all(
        jnp.broadcast_to(pair[None], (4,) + pair.shape), "x", 0, 0, tiled=True
    )


def split_bf16(value):
    high = value.astype(bf16)
    return high, (value - high.astype(f32)).astype(bf16)


def shape(dims, dtype):
    return jax.ShapeDtypeStruct(dims, dtype)


def call(kernel, outs, scratch=(), specs=None):
    return pl.pallas_call(
        kernel,
        out_shape=outs,
        in_specs=specs,
        out_specs=tuple(VMEM for _ in outs),
        scratch_shapes=list(scratch),
        compiler_params=pltpu.CompilerParams(vmem_limit_bytes=48 << 20),
    )


def blocks_of(where_ref, own_ref, other_ref):
    zh, core = where_ref[0], where_ref[1]
    for x in range(4):
        for far in range(2):
            side = zh if far == 0 else 1 - zh
            yield x * 4 + side * 2 + core, own_ref.at[x, far]
            yield x * 4 + side * 2 + 1 - core, other_ref.at[x, far]


def edges(inputs_ref, upstream_ref, mask_ref, right_ref, left_ref):
    width, rows = inputs_ref.shape
    lane = lax.broadcasted_iota(jnp.int32, (width, 128), 1)
    low = lax.broadcasted_iota(jnp.int32, (16, 128), 1)

    def pack(start, own, moved, ref):
        ends = inputs_ref[:, start : start + 128].astype(f32)
        up = pltpu.roll(upstream_ref[:, start : start + 128].astype(f32), 64, 1)
        ref[:width] = jnp.where(
            own(lane), ends, jnp.where(moved(lane), up, 0.0)
        ).astype(bf16)
        mask = jnp.broadcast_to(mask_ref[:, start : start + 128].astype(f32), (16, 128))
        ref[width:] = jnp.where(own(low), mask, 0.0).astype(bf16)

    pack(rows - 128, lambda i: i >= 98, lambda i: (i >= 49) & (i < 64), right_ref)
    pack(0, lambda i: i < 30, lambda i: (i >= 64) & (i < 79), left_ref)


def middle(
    where_ref, own_ref, other_ref, gain_ref, bias_ref, weight_ref, project_ref, flipped_ref,
    by_gain_ref, by_bias_ref, taps_ref, mask_ref,
    far_ref, near_ref, normed_ref, full_ref, stats_ref, both_ref, act_ref, kernel_ref,
    proj_ref, partial_ref, grad_ref, moved_ref,
):
    model = weight_ref.shape[1]
    width = own_ref.shape[2]
    lanes = normed_ref.shape[2]
    rows = near_ref.shape[2]
    taps = taps_ref.shape[0]
    reach = taps // 2
    total = jnp.zeros((8, lanes), f32)
    square = jnp.zeros((8, lanes), f32)
    for place, block in blocks_of(where_ref, own_ref, other_ref):
        x = block[:, :lanes].astype(f32).reshape(width // 8, 8, lanes)
        total = total + jnp.sum(x, axis=0)
        square = square + jnp.sum(x * x, axis=0)
        full_ref[place, :, :rows] = block[:, lanes:]
        full_ref[place, :, rows:] = pltpu.roll(
            block[:, rows:lanes].astype(f32), 64, 1
        ).astype(bf16)
    row_mean = jnp.sum(total, axis=0, keepdims=True) / model
    row_var = jnp.sum(square, axis=0, keepdims=True) / model - row_mean * row_mean
    inv_std = lax.rsqrt(row_var + eps)
    stats_ref[...] = jnp.concatenate(
        [row_mean, inv_std, jnp.zeros((6, lanes), f32)], axis=0
    )
    for place, block in blocks_of(where_ref, own_ref, other_ref):
        centred = (block[:, :lanes].astype(f32) - row_mean) * inv_std
        normed_ref[place] = (centred * gain_ref[place] + bias_ref[place]).astype(bf16)
    grad_ref[...] = jnp.dot(
        project_ref[...], full_ref[...].reshape(model, lanes), preferred_element_type=f32
    )
    proj_ref[...] = jnp.dot(
        weight_ref[...], normed_ref[...].reshape(model, lanes), preferred_element_type=f32
    )
    group = 16
    lane = lax.broadcasted_iota(jnp.int32, (group, 128), 1)

    def channels(step, carry):
        first = pl.multiple_of(step * group, group)
        mine = pl.ds(first, group)
        after = pl.ds(pl.multiple_of(width + first, group), group)
        value = proj_ref[mine, :]
        gate = jax.nn.sigmoid(proj_ref[after, :])
        keep = mask_ref[...]
        glu = (value * gate * keep).astype(bf16).astype(f32)
        conv = jnp.zeros((group, lanes), f32)
        for k in range(taps):
            moved = pltpu.roll(glu, (reach - k) % lanes, 1)
            moved_ref[k] = moved[:, :rows]
            conv = conv + taps_ref[k, mine, :] * moved
        sig = jax.nn.sigmoid(conv)
        act_ref[mine, :] = (conv * sig)[:, :rows].astype(bf16)
        act_grad = grad_ref[mine, :].astype(bf16).astype(f32)
        grad = (act_grad * (sig + conv * sig * (1.0 - sig))).astype(bf16).astype(f32)
        inner = grad[:, :rows]
        glu_grad = jnp.zeros((group, rows), f32)
        kernel = jnp.zeros((group, 128), f32)
        for k in range(taps):
            back = pltpu.roll(grad, (k - reach) % lanes, 1)[:, :rows]
            glu_grad = glu_grad + taps_ref[k, mine, :] * back
            seen = jnp.sum(inner * moved_ref[k], axis=1, keepdims=True)
            kernel = jnp.where(lane == k, seen, kernel)
        kernel_ref[mine, :] = kernel
        glu_grad = glu_grad * keep[:, :rows]
        gate = gate[:, :rows]
        both_ref[mine, :] = (glu_grad * gate).astype(bf16)
        both_ref[after, :] = (glu_grad * value[:, :rows] * gate * (1.0 - gate)).astype(bf16)
        return carry

    lax.fori_loop(0, width // group, channels, 0)
    both = both_ref[...]
    partial = jnp.dot(flipped_ref[...], both, preferred_element_type=f32).astype(bf16)
    partial_ref[...] = partial.reshape(partial_ref.shape)
    both = both.astype(f32)
    first = jnp.sum(both * by_gain_ref[...], axis=0, keepdims=True)
    second = jnp.sum(both * (proj_ref[:, :rows] - by_bias_ref[...]), axis=0, keepdims=True)
    first_high = first.astype(bf16).astype(f32)
    second_high = second.astype(bf16).astype(f32)
    row = lax.broadcasted_iota(jnp.int32, (16, rows), 0)
    extra = jnp.where(row == 0, first_high, 0.0)
    extra = jnp.where(row == 1, second_high, extra)
    extra = jnp.where(row == 2, first - first_high, extra)
    extra = jnp.where(row == 3, second - second_high, extra).astype(bf16)
    zh = where_ref[0]
    for x in range(4):
        for core in range(2):
            far_ref[x * 2 + core, :width] = partial_ref[x, 1 - zh, core]
            far_ref[x * 2 + core, width:] = extra
            near_ref[x * 2 + core] = partial_ref[x, zh, core]


def weights_of(normed_ref, full_ref, both_ref, act_ref, kernel_ref, grads_ref):
    width, rows = act_ref.shape
    model = normed_ref.shape[0] * width
    zero = jnp.zeros((width, rows), bf16)
    grads = lax.dot_general(
        normed_ref[:, :, :rows].reshape(model, rows),
        jnp.concatenate([zero, both_ref[...], zero], axis=0),
        OVER,
        preferred_element_type=f32,
    ) + lax.dot_general(
        full_ref[:, :, :rows].reshape(model, rows),
        jnp.concatenate([zero, zero, zero, act_ref[...]], axis=0),
        OVER,
        preferred_element_type=f32,
    )
    grads_ref[...] = grads.astype(bf16).reshape(grads_ref.shape)
    piece = grads_ref.shape[2]
    kernel = jnp.transpose(kernel_ref[...])[:piece].astype(bf16)
    for zl in range(8):
        for y in range(4):
            grads_ref[zl, y, :, :width] = kernel


def on_device(
    inputs,
    norm_gain,
    norm_bias,
    value_weight,
    gate_weight,
    conv_kernel,
    project_weight,
    frame_mask,
    upstream,
):
    width, rows = inputs.shape
    model = value_weight.shape[1]
    taps = conv_kernel.shape[0]
    lanes = rows + 128
    piece = model // 32
    zh = lax.axis_index("zh")
    core = lax.axis_index("core")
    y = lax.axis_index("y")
    zl = lax.axis_index("zl")
    offset = lax.axis_index(CHAN) * width
    where = jnp.stack([zh, core]).astype(jnp.int32)

    to_right, to_left = call(
        edges,
        (shape((width + 16, 128), bf16), shape((width + 16, 128), bf16)),
        specs=[VMEM] * 3,
    )(inputs, upstream, frame_mask.reshape(1, rows))
    edge = lax.ppermute(to_right, FRAME, [(i, i + 1) for i in range(31)]) + lax.ppermute(
        to_left, FRAME, [(i + 1, i) for i in range(31)]
    )

    weights = jnp.concatenate([value_weight, gate_weight])
    by_gain = jnp.sum(weights.astype(f32) * norm_gain[None, :], axis=1, keepdims=True)
    by_bias = jnp.sum(weights.astype(f32) * norm_bias[None, :], axis=1, keepdims=True)
    gain_local = lax.dynamic_slice_in_dim(norm_gain, offset, width, 0)[:, None]
    early = (
        weights, weights.T, by_gain, by_bias, conv_kernel.reshape(taps, width, 1),
        norm_gain.reshape(16, width, 1), norm_bias.reshape(16, width, 1), gain_local, where,
    )

    held = jnp.concatenate([inputs, edge[:width], upstream], axis=1)
    keep = jnp.concatenate([frame_mask.astype(f32)[None, :], edge[width : width + 1].astype(f32)], axis=1)
    came = swap(held, "zh")
    came, keep, early = lax.optimization_barrier((came, keep, early))
    weights, flipped, by_gain, by_bias, columns, gain, bias, gain_local, where = early
    own = over_x(jnp.stack([held, came]))
    other = swap(own, "core")
    far, near, normed, full_grads, stats, both, activated, kernel_part = call(
        middle,
        (
            shape((8, width + 16, rows), bf16),
            shape((8, width, rows), bf16),
            shape((16, width, lanes), bf16),
            shape((16, width, lanes), bf16),
            shape((8, lanes), f32),
            shape((2 * width, rows), bf16),
            shape((width, rows), bf16),
            shape((width, 128), f32),
        ),
        scratch=(
            pltpu.VMEM((2 * width, lanes), f32),
            pltpu.VMEM((4, 2, 2, width, rows), bf16),
            pltpu.VMEM((width, lanes), f32),
            pltpu.VMEM((taps, 16, rows), f32),
        ),
        specs=[SMEM] + [VMEM] * 11,
    )(
        where, own, other, gain, bias, weights, project_weight, flipped,
        by_gain, by_bias, columns, keep,
    )

    far, both = lax.optimization_barrier((far, both))
    far = lax.all_to_all(far, ("x", "core"), 0, 0, tiled=True)
    (grads,) = call(
        weights_of, (shape((8, 4, piece, 4 * width), bf16),), specs=[VMEM] * 5
    )(normed, full_grads, both, activated, kernel_part)

    def rows_for(step):
        return lax.dynamic_slice_in_dim(grads, (y + step) % 4, 1, 1)[:, 0]

    parts = [
        lax.ppermute(rows_for(step), "y", [(i, (i + step) % 4) for i in range(4)])
        for step in (1, 3, 2)
    ]
    near, far = lax.optimization_barrier((near, far))
    near = lax.all_to_all(near, ("x", "core"), 0, 0, tiled=True)
    far = jnp.sum(far.astype(f32), axis=0)
    far_sums = far[width : width + 2] + far[width + 2 : width + 4]
    sent_high, sent_low = split_bf16(far_sums)
    far = jnp.concatenate(
        [far[:width].astype(bf16), sent_high, sent_low, jnp.zeros((12, rows), bf16)]
    )
    came = swap(far, "zh").astype(f32)

    total, far_copy = lax.optimization_barrier((rows_for(0), far))
    total = total.astype(f32)
    for part in parts:
        total = total + part.astype(f32)

    def halve(total, size):
        side = (zl // size) % 2
        kept = lax.dynamic_slice_in_dim(total, side * size, size, 0)
        sent = lax.dynamic_slice_in_dim(total, (1 - side) * size, size, 0).astype(bf16)
        return kept + lax.ppermute(sent, "zl", [(i, i ^ size) for i in range(8)]).astype(f32)

    total = halve(total, 4)

    normed_grad = jnp.sum(near.astype(f32), axis=0) + came[:width]
    kept = far_copy[width : width + 4].astype(f32)
    sums = (kept[:2] + kept[2:] + came[width : width + 2] + came[width + 2 : width + 4]) / model
    inv_std = stats[1:2, :rows]
    centred = (inputs.astype(f32) - stats[0:1, :rows]) * inv_std
    tail = jnp.stack([jnp.sum(normed_grad * centred, axis=1), jnp.sum(normed_grad, axis=1)])
    tail, total = lax.optimization_barrier((tail, total))
    tail = lax.all_to_all(
        jnp.broadcast_to(tail[None], (32, 2, width)), FRAME, 0, 0, tiled=True
    )
    tail = jnp.sum(tail, axis=0)
    inputs_grad = (
        upstream.astype(f32)
        + inv_std * (normed_grad * gain_local - sums[0:1] - centred * sums[1:2])
    ).astype(bf16)

    grads = halve(halve(total, 2), 1)[0]
    kernel_grad = grads[:taps, :width]
    value_grad = grads[:, width : 2 * width].T
    gate_grad = grads[:, 2 * width : 3 * width].T
    project_grad = grads[:, 3 * width :].T
    return (inputs_grad, value_grad, gate_grad, project_grad, kernel_grad, tail[0], tail[1])


def solution(mesh):
    split = Mesh(mesh.devices.reshape(8, 4, 4, 2, 2), FRAME + CHAN)
    return jax.shard_map(
        on_device,
        mesh=split,
        in_specs=(
            P(CHAN, FRAME),
            P(),
            P(),
            P(CHAN, None),
            P(CHAN, None),
            P(None, CHAN),
            P(CHAN, None),
            P(FRAME),
            P(CHAN, FRAME),
        ),
        out_specs=(
            P(CHAN, FRAME),
            P(CHAN, FRAME),
            P(CHAN, FRAME),
            P(CHAN, FRAME),
            P(None, CHAN),
            P(CHAN),
            P(CHAN),
        ),
        check_vma=False,
    )
```

```python
import jax
import jax.numpy as jnp
from jax import lax
from jax.experimental import pallas as pl
from jax.experimental.pallas import tpu as pltpu
from jax.sharding import Mesh, PartitionSpec as P

eps = 1e-05
CHAN = ("x", "zh", "core")
FRAME = ("zl", "y")
SWAP = [(0, 1), (1, 0)]
f32 = jnp.float32
bf16 = jnp.bfloat16
VMEM = pl.BlockSpec(memory_space=pltpu.VMEM)
SMEM = pl.BlockSpec(memory_space=pltpu.SMEM)
OVER = (((1,), (1,)), ((), ()))


def swap(value, axis):
    return lax.ppermute(value, axis, SWAP)


def over_x(pair):
    return lax.all_to_all(
        jnp.broadcast_to(pair[None], (4,) + pair.shape), "x", 0, 0, tiled=True
    )


def split_bf16(value):
    high = value.astype(bf16)
    return high, (value - high.astype(f32)).astype(bf16)


def shape(dims, dtype):
    return jax.ShapeDtypeStruct(dims, dtype)


def call(kernel, outs, scratch=(), specs=None):
    return pl.pallas_call(
        kernel,
        out_shape=outs,
        in_specs=specs,
        out_specs=tuple(VMEM for _ in outs),
        scratch_shapes=list(scratch),
        compiler_params=pltpu.CompilerParams(vmem_limit_bytes=24 << 20),
    )


def blocks_of(where_ref, own_ref, other_ref):
    zh, core = where_ref[0], where_ref[1]
    for x in range(4):
        for far in range(2):
            side = zh if far == 0 else 1 - zh
            yield x * 4 + side * 2 + core, own_ref.at[x, far]
            yield x * 4 + side * 2 + 1 - core, other_ref.at[x, far]


def edges(inputs_ref, upstream_ref, mask_ref, main_ref, right_ref, left_ref):
    width, rows = inputs_ref.shape
    main_ref[:, :rows] = inputs_ref[...]
    main_ref[:, rows:] = upstream_ref[...]
    lane = lax.broadcasted_iota(jnp.int32, (width, 128), 1)
    low = lax.broadcasted_iota(jnp.int32, (16, 128), 1)

    def pack(start, own, moved, ref):
        ends = inputs_ref[:, start : start + 128].astype(f32)
        up = pltpu.roll(upstream_ref[:, start : start + 128].astype(f32), 64, 1)
        ref[:width] = jnp.where(
            own(lane), ends, jnp.where(moved(lane), up, 0.0)
        ).astype(bf16)
        mask = jnp.broadcast_to(mask_ref[:, start : start + 128].astype(f32), (16, 128))
        ref[width:] = jnp.where(own(low), mask, 0.0).astype(bf16)

    pack(rows - 128, lambda i: i >= 98, lambda i: (i >= 49) & (i < 64), right_ref)
    pack(0, lambda i: i < 30, lambda i: (i >= 64) & (i < 79), left_ref)


def middle(
    where_ref, own_ref, other_ref, gain_ref, bias_ref, weight_ref, project_ref, flipped_ref,
    by_gain_ref, by_bias_ref, taps_ref, mask_ref,
    mixed_ref, normed_ref, full_ref, stats_ref, both_ref, act_ref, kernel_ref,
    proj_ref, partial_ref, grad_ref, moved_ref,
):
    model = weight_ref.shape[1]
    width = own_ref.shape[2]
    lanes = normed_ref.shape[2]
    rows = mixed_ref.shape[2]
    taps = taps_ref.shape[1]
    reach = taps // 2
    total = jnp.zeros((8, lanes), f32)
    square = jnp.zeros((8, lanes), f32)
    for place, block in blocks_of(where_ref, own_ref, other_ref):
        x = block[:, :lanes].astype(f32).reshape(width // 8, 8, lanes)
        total = total + jnp.sum(x, axis=0)
        square = square + jnp.sum(x * x, axis=0)
        full_ref[place, :, :rows] = block[:, lanes:]
        full_ref[place, :, rows:] = pltpu.roll(
            block[:, rows:lanes].astype(f32), 64, 1
        ).astype(bf16)
    row_mean = jnp.sum(total, axis=0, keepdims=True) / model
    row_var = jnp.sum(square, axis=0, keepdims=True) / model - row_mean * row_mean
    inv_std = lax.rsqrt(row_var + eps)
    stats_ref[...] = jnp.concatenate(
        [row_mean, inv_std, jnp.zeros((6, lanes), f32)], axis=0
    )
    for i, (place, block) in enumerate(blocks_of(where_ref, own_ref, other_ref)):
        centred = (block[:, :lanes].astype(f32) - row_mean) * inv_std
        normed_ref[place] = (
            centred * gain_ref[:, i : i + 1] + bias_ref[:, i : i + 1]
        ).astype(bf16)
    grad_ref[...] = jnp.dot(
        project_ref[...], full_ref[...].reshape(model, lanes), preferred_element_type=f32
    )
    proj_ref[...] = jnp.dot(
        weight_ref[...], normed_ref[...].reshape(model, lanes), preferred_element_type=f32
    )
    group = 16
    lane = lax.broadcasted_iota(jnp.int32, (group, 128), 1)

    def channels(step, carry):
        first = pl.multiple_of(step * group, group)
        mine = pl.ds(first, group)
        after = pl.ds(pl.multiple_of(width + first, group), group)
        value = proj_ref[mine, :]
        gate = jax.nn.sigmoid(proj_ref[after, :])
        keep = mask_ref[...]
        glu = (value * gate * keep).astype(bf16).astype(f32)
        conv = jnp.zeros((group, lanes), f32)
        for k in range(taps):
            moved = pltpu.roll(glu, (reach - k) % lanes, 1)
            moved_ref[k] = moved[:, :rows]
            conv = conv + taps_ref[mine, k : k + 1] * moved
        sig = jax.nn.sigmoid(conv)
        act_ref[mine, :] = (conv * sig)[:, :rows].astype(bf16)
        act_grad = grad_ref[mine, :].astype(bf16).astype(f32)
        grad = (act_grad * (sig + conv * sig * (1.0 - sig))).astype(bf16).astype(f32)
        inner = grad[:, :rows]
        glu_grad = jnp.zeros((group, rows), f32)
        kernel = jnp.zeros((group, 128), f32)
        for k in range(taps):
            back = pltpu.roll(grad, (k - reach) % lanes, 1)[:, :rows]
            glu_grad = glu_grad + taps_ref[mine, k : k + 1] * back
            seen = jnp.sum(inner * moved_ref[k], axis=1, keepdims=True)
            kernel = jnp.where(lane == k, seen, kernel)
        kernel_ref[mine, :] = kernel
        glu_grad = glu_grad * keep[:, :rows]
        gate = gate[:, :rows]
        both_ref[mine, :] = (glu_grad * gate).astype(bf16)
        both_ref[after, :] = (glu_grad * value[:, :rows] * gate * (1.0 - gate)).astype(bf16)
        return carry

    lax.fori_loop(0, width // group, channels, 0)
    both = both_ref[...]
    partial = jnp.dot(flipped_ref[...], both, preferred_element_type=f32).astype(bf16)
    partial_ref[...] = partial.reshape(partial_ref.shape)
    both = both.astype(f32)
    first = jnp.sum(both * by_gain_ref[...], axis=0, keepdims=True)
    second = jnp.sum(both * (proj_ref[:, :rows] - by_bias_ref[...]), axis=0, keepdims=True)
    first_high = first.astype(bf16).astype(f32)
    second_high = second.astype(bf16).astype(f32)
    row = lax.broadcasted_iota(jnp.int32, (16, rows), 0)
    extra = jnp.where(row == 0, first_high, 0.0)
    extra = jnp.where(row == 1, second_high, extra)
    extra = jnp.where(row == 2, first - first_high, extra)
    extra = jnp.where(row == 3, second - second_high, extra).astype(bf16)
    zh = where_ref[0]
    for x in range(4):
        for core in range(2):
            mixed_ref[x * 2 + core, :width] = partial_ref[x, 1 - zh, core]
            mixed_ref[x * 2 + core, width : 2 * width] = partial_ref[x, zh, core]
            mixed_ref[x * 2 + core, 2 * width :] = extra


def weights_of(normed_ref, full_ref, both_ref, act_ref, kernel_ref, grads_ref):
    width, rows = act_ref.shape
    model = normed_ref.shape[0] * width
    zero = jnp.zeros((width, rows), bf16)
    grads = lax.dot_general(
        normed_ref[:, :, :rows].reshape(model, rows),
        jnp.concatenate([zero, both_ref[...], zero], axis=0),
        OVER,
        preferred_element_type=f32,
    ) + lax.dot_general(
        full_ref[:, :, :rows].reshape(model, rows),
        jnp.concatenate([zero, zero, zero, act_ref[...]], axis=0),
        OVER,
        preferred_element_type=f32,
    )
    grads_ref[...] = grads.astype(bf16).reshape(grads_ref.shape)
    piece = grads_ref.shape[2]
    kernel = jnp.transpose(kernel_ref[...])[:piece].astype(bf16)
    for zl in range(8):
        for y in range(4):
            grads_ref[zl, y, :, :width] = kernel


def on_device(
    inputs,
    norm_gain,
    norm_bias,
    value_weight,
    gate_weight,
    conv_kernel,
    project_weight,
    frame_mask,
    upstream,
):
    width, rows = inputs.shape
    model = value_weight.shape[1]
    taps = conv_kernel.shape[0]
    lanes = rows + 128
    piece = model // 32
    zh = lax.axis_index("zh")
    core = lax.axis_index("core")
    y = lax.axis_index("y")
    zl = lax.axis_index("zl")
    offset = lax.axis_index(CHAN) * width
    where = jnp.stack([zh, core]).astype(jnp.int32)

    main, to_right, to_left = call(
        edges,
        (
            shape((width, 2 * rows), bf16),
            shape((width + 16, 128), bf16),
            shape((width + 16, 128), bf16),
        ),
        specs=[VMEM] * 3,
    )(inputs, upstream, frame_mask.reshape(1, rows))
    came = swap(main, "zh")
    edge = lax.ppermute(to_right, FRAME, [(i, i + 1) for i in range(31)]) + lax.ppermute(
        to_left, FRAME, [(i + 1, i) for i in range(31)]
    )
    across = FRAME + ("zh",)
    pairs = [(i, i + 1, z) for i in range(31) for z in range(2)]
    edge_came = lax.ppermute(
        to_right[:width], across, [(2 * i + z, 2 * j + 1 - z) for i, j, z in pairs]
    ) + lax.ppermute(to_left[:width], across, [(2 * j + z, 2 * i + 1 - z) for i, j, z in pairs])

    weights = jnp.concatenate([value_weight, gate_weight])
    by_gain = jnp.sum(weights.astype(f32) * norm_gain[None, :], axis=1, keepdims=True)
    by_bias = jnp.sum(weights.astype(f32) * norm_bias[None, :], axis=1, keepdims=True)
    gain_local = lax.dynamic_slice_in_dim(norm_gain, offset, width, 0)[:, None]

    def columns_of(parameter):
        parameter = parameter.reshape(4, 2, 2, width)
        parameter = jnp.where(zh == 0, parameter, parameter[:, ::-1])
        parameter = jnp.where(core == 0, parameter, parameter[:, :, ::-1])
        return parameter.reshape(16, width).T

    early = (
        weights, weights.T, by_gain, by_bias, conv_kernel.T,
        columns_of(norm_gain), columns_of(norm_bias), gain_local, where,
    )

    keep = jnp.concatenate([frame_mask.astype(f32)[None, :], edge[width : width + 1].astype(f32)], axis=1)
    came, keep, early = lax.optimization_barrier((came, keep, early))
    weights, flipped, by_gain, by_bias, columns, gain, bias, gain_local, where = early
    own = over_x(
        jnp.stack(
            [
                jnp.concatenate([inputs, edge[:width], upstream], axis=1),
                jnp.concatenate([came[:, :rows], edge_came, came[:, rows:]], axis=1),
            ]
        )
    )
    other = swap(own, "core")
    mixed, normed, full_grads, stats, both, activated, kernel_part = call(
        middle,
        (
            shape((8, 2 * width + 16, rows), bf16),
            shape((16, width, lanes), bf16),
            shape((16, width, lanes), bf16),
            shape((8, lanes), f32),
            shape((2 * width, rows), bf16),
            shape((width, rows), bf16),
            shape((width, 128), f32),
        ),
        scratch=(
            pltpu.VMEM((2 * width, lanes), f32),
            pltpu.VMEM((4, 2, 2, width, rows), bf16),
            pltpu.VMEM((width, lanes), f32),
            pltpu.VMEM((taps, 16, rows), f32),
        ),
        specs=[SMEM] + [VMEM] * 11,
    )(
        where, own, other, gain, bias, weights, project_weight, flipped,
        by_gain, by_bias, columns, keep,
    )

    mixed, both = lax.optimization_barrier((mixed, both))
    mixed = lax.all_to_all(mixed, ("x", "core"), 0, 0, tiled=True)
    (grads,) = call(
        weights_of, (shape((8, 4, piece, 4 * width), bf16),), specs=[VMEM] * 5
    )(normed, full_grads, both, activated, kernel_part)

    def rows_for(step):
        return lax.dynamic_slice_in_dim(grads, (y + step) % 4, 1, 1)[:, 0]

    parts = [
        lax.ppermute(rows_for(step), "y", [(i, (i + step) % 4) for i in range(4)])
        for step in (1, 3, 2)
    ]
    mixed = jnp.sum(mixed.astype(f32), axis=0)
    far_sums = mixed[2 * width : 2 * width + 2] + mixed[2 * width + 2 : 2 * width + 4]
    sent_high, sent_low = split_bf16(far_sums)
    far = jnp.concatenate(
        [mixed[:width].astype(bf16), sent_high, sent_low, jnp.zeros((12, rows), bf16)]
    )
    came = swap(far, "zh").astype(f32)

    total, far_copy = lax.optimization_barrier((rows_for(0), far))
    total = total.astype(f32)
    for part in parts:
        total = total + part.astype(f32)

    def halve(total, size):
        side = (zl // size) % 2
        kept = lax.dynamic_slice_in_dim(total, side * size, size, 0)
        sent = lax.dynamic_slice_in_dim(total, (1 - side) * size, size, 0).astype(bf16)
        return kept + lax.ppermute(sent, "zl", [(i, i ^ size) for i in range(8)]).astype(f32)

    total = halve(total, 4)

    normed_grad = mixed[width : 2 * width] + came[:width]
    kept = far_copy[width : width + 4].astype(f32)
    sums = (kept[:2] + kept[2:] + came[width : width + 2] + came[width + 2 : width + 4]) / model
    inv_std = stats[1:2, :rows]
    centred = (inputs.astype(f32) - stats[0:1, :rows]) * inv_std
    tail = jnp.stack([jnp.sum(normed_grad * centred, axis=1), jnp.sum(normed_grad, axis=1)])
    tail, total = lax.optimization_barrier((tail, total))
    tail = lax.all_to_all(
        jnp.broadcast_to(tail[None], (32, 2, width)), FRAME, 0, 0, tiled=True
    )
    tail = jnp.sum(tail, axis=0)
    inputs_grad = (
        upstream.astype(f32)
        + inv_std * (normed_grad * gain_local - sums[0:1] - centred * sums[1:2])
    ).astype(bf16)

    grads = halve(halve(total, 2), 1)[0]
    kernel_grad = grads[:taps, :width]
    value_grad = grads[:, width : 2 * width].T
    gate_grad = grads[:, 2 * width : 3 * width].T
    project_grad = grads[:, 3 * width :].T
    return (inputs_grad, value_grad, gate_grad, project_grad, kernel_grad, tail[0], tail[1])


def solution(mesh):
    split = Mesh(mesh.devices.reshape(8, 4, 4, 2, 2), FRAME + CHAN)
    return jax.shard_map(
        on_device,
        mesh=split,
        in_specs=(
            P(CHAN, FRAME),
            P(),
            P(),
            P(CHAN, None),
            P(CHAN, None),
            P(None, CHAN),
            P(CHAN, None),
            P(FRAME),
            P(CHAN, FRAME),
        ),
        out_specs=(
            P(CHAN, FRAME),
            P(CHAN, FRAME),
            P(CHAN, FRAME),
            P(CHAN, FRAME),
            P(None, CHAN),
            P(CHAN),
            P(CHAN),
        ),
        check_vma=False,
    )
```

```python
import jax
import jax.numpy as jnp
from jax import lax
from jax.experimental import pallas as pl
from jax.experimental.pallas import tpu as pltpu
from jax.sharding import Mesh, PartitionSpec as P

eps = 1e-05
CHAN = ("x", "zh", "core")
FRAME = ("zl", "y")
SWAP = [(0, 1), (1, 0)]
f32 = jnp.float32
bf16 = jnp.bfloat16
VMEM = pl.BlockSpec(memory_space=pltpu.VMEM)
SMEM = pl.BlockSpec(memory_space=pltpu.SMEM)
OVER = (((1,), (1,)), ((), ()))


def swap(value, axis):
    return lax.ppermute(value, axis, SWAP)


def over_x(pair):
    return lax.all_to_all(
        jnp.broadcast_to(pair[None], (4,) + pair.shape), "x", 0, 0, tiled=True
    )


def split_bf16(value):
    high = value.astype(bf16)
    return high, (value - high.astype(f32)).astype(bf16)


def shape(dims, dtype):
    return jax.ShapeDtypeStruct(dims, dtype)


def call(kernel, outs, scratch=(), specs=None):
    return pl.pallas_call(
        kernel,
        out_shape=outs,
        in_specs=specs,
        out_specs=tuple(VMEM for _ in outs),
        scratch_shapes=list(scratch),
        compiler_params=pltpu.CompilerParams(vmem_limit_bytes=24 << 20),
    )


def blocks_of(where_ref, own_ref, other_ref):
    zh, core = where_ref[0], where_ref[1]
    for x in range(4):
        for far in range(2):
            side = zh if far == 0 else 1 - zh
            yield x * 4 + side * 2 + core, own_ref.at[x, far]
            yield x * 4 + side * 2 + 1 - core, other_ref.at[x, far]


def edges(inputs_ref, upstream_ref, mask_ref, right_ref, left_ref):
    width, rows = inputs_ref.shape
    lane = lax.broadcasted_iota(jnp.int32, (width, 128), 1)
    low = lax.broadcasted_iota(jnp.int32, (16, 128), 1)

    def pack(start, own, moved, ref):
        ends = inputs_ref[:, start : start + 128].astype(f32)
        up = pltpu.roll(upstream_ref[:, start : start + 128].astype(f32), 64, 1)
        ref[:width] = jnp.where(
            own(lane), ends, jnp.where(moved(lane), up, 0.0)
        ).astype(bf16)
        mask = jnp.broadcast_to(mask_ref[:, start : start + 128].astype(f32), (16, 128))
        ref[width:] = jnp.where(own(low), mask, 0.0).astype(bf16)

    pack(rows - 128, lambda i: i >= 98, lambda i: (i >= 49) & (i < 64), right_ref)
    pack(0, lambda i: i < 30, lambda i: (i >= 64) & (i < 79), left_ref)


def middle(
    where_ref, own_ref, other_ref, gain_ref, bias_ref, weight_ref, project_ref, flipped_ref,
    by_gain_ref, by_bias_ref, taps_ref, mask_ref,
    mixed_out, grads_ref, stats_ref,
    mixed_ref, normed_ref, full_ref, both_ref, act_ref, kernel_ref,
    proj_ref, grad_ref, moved_ref, back_ref, sem,
):
    model = weight_ref.shape[1]
    width = own_ref.shape[2]
    lanes = normed_ref.shape[2]
    rows = mixed_ref.shape[2]
    taps = taps_ref.shape[0]
    total = jnp.zeros((8, lanes), f32)
    square = jnp.zeros((8, lanes), f32)
    for place, block in blocks_of(where_ref, own_ref, other_ref):
        x = block[:, :lanes].astype(f32).reshape(width // 8, 8, lanes)
        total = total + jnp.sum(x, axis=0)
        square = square + jnp.sum(x * x, axis=0)
        full_ref[place, :, :rows] = block[:, lanes:]
        full_ref[place, :, rows:] = pltpu.roll(
            block[:, rows:lanes].astype(f32), 64, 1
        ).astype(bf16)
    row_mean = jnp.sum(total, axis=0, keepdims=True) / model
    row_var = jnp.sum(square, axis=0, keepdims=True) / model - row_mean * row_mean
    inv_std = lax.rsqrt(row_var + eps)
    stats_ref[...] = jnp.concatenate(
        [row_mean, inv_std, jnp.zeros((6, lanes), f32)], axis=0
    )
    for i, (place, block) in enumerate(blocks_of(where_ref, own_ref, other_ref)):
        centred = (block[:, :lanes].astype(f32) - row_mean) * inv_std
        normed_ref[place] = (
            centred * gain_ref[:, i : i + 1] + bias_ref[:, i : i + 1]
        ).astype(bf16)
    grad_ref[...] = jnp.dot(
        project_ref[...], full_ref[...].reshape(model, lanes), preferred_element_type=f32
    )
    proj_ref[...] = jnp.dot(
        weight_ref[...], normed_ref[...].reshape(model, lanes), preferred_element_type=f32
    )
    group = 16
    lane = lax.broadcasted_iota(jnp.int32, (group, 128), 1)
    inside = lax.broadcasted_iota(jnp.int32, (group, lanes), 1) < rows

    def channels(step, carry):
        first = pl.multiple_of(step * group, group)
        mine = pl.ds(first, group)
        after = pl.ds(pl.multiple_of(width + first, group), group)
        value = proj_ref[mine, :]
        gate = jax.nn.sigmoid(proj_ref[after, :])
        keep = mask_ref[...]
        glu = (value * gate * keep).astype(bf16).astype(f32)

        def shifted(x, by):
            return pltpu.roll(x, by % lanes, 1) if by % lanes else x

        def tap(k):
            return jnp.concatenate([taps_ref[k, mine, :]] * (lanes // 128), axis=1)

        def spread(fine, sign):
            result = None
            for a in range(4):
                part = None
                for b in range(8):
                    if 8 * a + b < taps:
                        term = tap(8 * a + b) * fine[b]
                        part = term if part is None else part + term
                part = shifted(part, sign * (8 * a - 8))
                result = part if result is None else result + part
            return result

        for b in range(8):
            moved_ref[b] = shifted(glu, 7 - b)
        conv = spread(moved_ref, -1)
        sig = jax.nn.sigmoid(conv)
        act_ref[mine, :] = (conv * sig)[:, :rows].astype(bf16)
        act_grad = grad_ref[mine, :].astype(bf16).astype(f32)
        grad = (act_grad * (sig + conv * sig * (1.0 - sig))).astype(bf16).astype(f32)
        for b in range(8):
            back_ref[b] = shifted(grad, b - 7)
        glu_grad = spread(back_ref, 1)[:, :rows]
        inner = jnp.where(inside, grad, 0.0)
        kernel = jnp.zeros((group, 128), f32)
        for a in range(4):
            here = shifted(inner, 8 * a - 8)
            for b in range(8):
                if 8 * a + b < taps:
                    seen = jnp.sum(here * moved_ref[b], axis=1, keepdims=True)
                    kernel = jnp.where(lane == 8 * a + b, seen, kernel)
        kernel_ref[mine, :] = kernel
        glu_grad = glu_grad * keep[:, :rows]
        gate = gate[:, :rows]
        both_ref[mine, :] = (glu_grad * gate).astype(bf16)
        both_ref[after, :] = (glu_grad * value[:, :rows] * gate * (1.0 - gate)).astype(bf16)
        return carry

    lax.fori_loop(0, width // group, channels, 0)
    both = both_ref[...]
    partial = jnp.dot(flipped_ref[...], both, preferred_element_type=f32).astype(bf16)
    partial = partial.reshape(4, 2, 2, width, rows)
    both = both.astype(f32)
    first = jnp.sum(both * by_gain_ref[...], axis=0, keepdims=True)
    second = jnp.sum(both * (proj_ref[:, :rows] - by_bias_ref[...]), axis=0, keepdims=True)
    first_high = first.astype(bf16).astype(f32)
    second_high = second.astype(bf16).astype(f32)
    row = lax.broadcasted_iota(jnp.int32, (16, rows), 0)
    extra = jnp.where(row == 0, first_high, 0.0)
    extra = jnp.where(row == 1, second_high, extra)
    extra = jnp.where(row == 2, first - first_high, extra)
    extra = jnp.where(row == 3, second - second_high, extra).astype(bf16)
    zh = where_ref[0]
    for x in range(4):
        for core in range(2):
            for side in range(2):
                start = pl.multiple_of(jnp.where(side == zh, width, 0), width)
                mixed_ref[x * 2 + core, pl.ds(start, width)] = partial[x, side, core]
            mixed_ref[x * 2 + core, 2 * width :] = extra
    copy = pltpu.make_async_copy(mixed_ref, mixed_out, sem)
    copy.start()

    zero = jnp.zeros((width, rows), bf16)
    grads = lax.dot_general(
        normed_ref[:, :, :rows].reshape(model, rows),
        jnp.concatenate([zero, both_ref[...], zero], axis=0),
        OVER,
        preferred_element_type=f32,
    ) + lax.dot_general(
        full_ref[:, :, :rows].reshape(model, rows),
        jnp.concatenate([zero, zero, zero, act_ref[...]], axis=0),
        OVER,
        preferred_element_type=f32,
    )
    grads_ref[...] = grads.astype(bf16).reshape(grads_ref.shape)
    kernel = jnp.transpose(kernel_ref[...])[: grads_ref.shape[2]].astype(bf16)
    for zl in range(8):
        for y in range(4):
            grads_ref[zl, y, :, :width] = kernel
    copy.wait()


def on_device(
    inputs,
    norm_gain,
    norm_bias,
    value_weight,
    gate_weight,
    conv_kernel,
    project_weight,
    frame_mask,
    upstream,
):
    width, rows = inputs.shape
    model = value_weight.shape[1]
    taps = conv_kernel.shape[0]
    lanes = rows + 128
    piece = model // 32
    zh = lax.axis_index("zh")
    core = lax.axis_index("core")
    y = lax.axis_index("y")
    zl = lax.axis_index("zl")
    offset = lax.axis_index(CHAN) * width
    where = jnp.stack([zh, core]).astype(jnp.int32)

    to_right, to_left = call(
        edges,
        (shape((width + 16, 128), bf16), shape((width + 16, 128), bf16)),
        specs=[VMEM] * 3,
    )(inputs, upstream, frame_mask.reshape(1, rows))
    edge = lax.ppermute(to_right, FRAME, [(i, i + 1) for i in range(31)]) + lax.ppermute(
        to_left, FRAME, [(i + 1, i) for i in range(31)]
    )

    weights = jnp.concatenate([value_weight, gate_weight])
    by_gain = jnp.sum(weights.astype(f32) * norm_gain[None, :], axis=1, keepdims=True)
    by_bias = jnp.sum(weights.astype(f32) * norm_bias[None, :], axis=1, keepdims=True)
    gain_local = lax.dynamic_slice_in_dim(norm_gain, offset, width, 0)[:, None]

    def columns_of(parameter):
        parameter = parameter.reshape(4, 2, 2, width)
        parameter = jnp.where(zh == 0, parameter, parameter[:, ::-1])
        parameter = jnp.where(core == 0, parameter, parameter[:, :, ::-1])
        return parameter.reshape(16, width).T

    early = (
        weights, weights.T, by_gain, by_bias,
        jnp.broadcast_to(conv_kernel[:, :, None], (taps, width, 128)),
        columns_of(norm_gain), columns_of(norm_bias), gain_local, where,
    )

    held = jnp.concatenate([inputs, edge[:width], upstream], axis=1)
    keep = jnp.concatenate([frame_mask.astype(f32)[None, :], edge[width : width + 1].astype(f32)], axis=1)
    came = swap(held, "zh")
    came, keep, early = lax.optimization_barrier((came, keep, early))
    weights, flipped, by_gain, by_bias, columns, gain, bias, gain_local, where = early
    own = over_x(jnp.stack([held, came]))
    other = swap(own, "core")
    mixed, grads, stats = pl.pallas_call(
        middle,
        out_shape=(
            shape((8, 2 * width + 16, rows), bf16),
            shape((8, 4, piece, 4 * width), bf16),
            shape((8, lanes), f32),
        ),
        in_specs=[SMEM] + [VMEM] * 11,
        out_specs=(pl.BlockSpec(memory_space=pltpu.HBM), VMEM, VMEM),
        scratch_shapes=[
            pltpu.VMEM((8, 2 * width + 16, rows), bf16),
            pltpu.VMEM((16, width, lanes), bf16),
            pltpu.VMEM((16, width, lanes), bf16),
            pltpu.VMEM((2 * width, rows), bf16),
            pltpu.VMEM((width, rows), bf16),
            pltpu.VMEM((width, 128), f32),
            pltpu.VMEM((2 * width, lanes), f32),
            pltpu.VMEM((width, lanes), f32),
            pltpu.VMEM((8, 16, lanes), f32),
            pltpu.VMEM((8, 16, lanes), f32),
            pltpu.SemaphoreType.DMA,
        ],
        compiler_params=pltpu.CompilerParams(vmem_limit_bytes=30 << 20),
    )(
        where, own, other, gain, bias, weights, project_weight, flipped,
        by_gain, by_bias, columns, keep,
    )

    mixed = lax.all_to_all(mixed, ("x", "core"), 0, 0, tiled=True)

    def rows_for(step):
        return lax.dynamic_slice_in_dim(grads, (y + step) % 4, 1, 1)[:, 0]

    parts = [
        lax.ppermute(rows_for(step), "y", [(i, (i + step) % 4) for i in range(4)])
        for step in (1, 3, 2)
    ]
    mixed = jnp.sum(mixed.astype(f32), axis=0)
    far_sums = mixed[2 * width : 2 * width + 2] + mixed[2 * width + 2 : 2 * width + 4]
    sent_high, sent_low = split_bf16(far_sums)
    far = jnp.concatenate(
        [mixed[:width].astype(bf16), sent_high, sent_low, jnp.zeros((12, rows), bf16)]
    )
    came = swap(far, "zh").astype(f32)

    total, far_copy = lax.optimization_barrier((rows_for(0), far))
    total = total.astype(f32)
    for part in parts:
        total = total + part.astype(f32)

    def halve(total, size):
        side = (zl // size) % 2
        half = total.shape[0] // 2
        total = total.reshape(half, 2, piece, 4 * width)
        kept = lax.dynamic_slice_in_dim(total, side, 1, 1)[:, 0]
        sent = lax.dynamic_slice_in_dim(total, 1 - side, 1, 1)[:, 0].astype(bf16)
        return kept + lax.ppermute(sent, "zl", [(i, i ^ size) for i in range(8)]).astype(f32)

    total = halve(total, 1)

    normed_grad = mixed[width : 2 * width] + came[:width]
    kept = far_copy[width : width + 4].astype(f32)
    sums = (kept[:2] + kept[2:] + came[width : width + 2] + came[width + 2 : width + 4]) / model
    inv_std = stats[1:2, :rows]
    centred = (inputs.astype(f32) - stats[0:1, :rows]) * inv_std
    tail = jnp.stack([jnp.sum(normed_grad * centred, axis=1), jnp.sum(normed_grad, axis=1)])
    total, normed_grad = lax.optimization_barrier((total, normed_grad))
    tail = lax.all_to_all(
        jnp.broadcast_to(tail[None], (32, 2, width)), FRAME, 0, 0, tiled=True
    )
    inputs_grad = (
        upstream.astype(f32)
        + inv_std * (normed_grad * gain_local - sums[0:1] - centred * sums[1:2])
    ).astype(bf16)

    grads = halve(halve(total, 2), 4)[0]
    tail, grads = lax.optimization_barrier((tail, grads))
    tail = jnp.sum(tail, axis=0)
    kernel_grad = grads[:taps, :width]
    value_grad = grads[:, width : 2 * width].T
    gate_grad = grads[:, 2 * width : 3 * width].T
    project_grad = grads[:, 3 * width :].T
    return (inputs_grad, value_grad, gate_grad, project_grad, kernel_grad, tail[0], tail[1])


def solution(mesh):
    split = Mesh(mesh.devices.reshape(8, 4, 4, 2, 2), FRAME + CHAN)
    return jax.shard_map(
        on_device,
        mesh=split,
        in_specs=(
            P(CHAN, FRAME),
            P(),
            P(),
            P(CHAN, None),
            P(CHAN, None),
            P(None, CHAN),
            P(CHAN, None),
            P(FRAME),
            P(CHAN, FRAME),
        ),
        out_specs=(
            P(CHAN, FRAME),
            P(CHAN, FRAME),
            P(CHAN, FRAME),
            P(CHAN, FRAME),
            P(None, CHAN),
            P(CHAN),
            P(CHAN),
        ),
        check_vma=False,
    )
```

```python
import jax
import jax.numpy as jnp
from jax import lax
from jax.experimental import pallas as pl
from jax.experimental.pallas import tpu as pltpu
from jax.sharding import Mesh, PartitionSpec as P

eps = 1e-05
CHAN = ("x", "zh", "core")
FRAME = ("zl", "y")
SWAP = [(0, 1), (1, 0)]
f32 = jnp.float32
bf16 = jnp.bfloat16
VMEM = pl.BlockSpec(memory_space=pltpu.VMEM)
SMEM = pl.BlockSpec(memory_space=pltpu.SMEM)
OVER = (((1,), (1,)), ((), ()))


def swap(value, axis):
    return lax.ppermute(value, axis, SWAP)


def over_x(pair):
    return lax.all_to_all(
        jnp.broadcast_to(pair[None], (4,) + pair.shape), "x", 0, 0, tiled=True
    )


def split_bf16(value):
    high = value.astype(bf16)
    return high, (value - high.astype(f32)).astype(bf16)


def shape(dims, dtype):
    return jax.ShapeDtypeStruct(dims, dtype)


def call(kernel, outs, scratch=(), specs=None):
    return pl.pallas_call(
        kernel,
        out_shape=outs,
        in_specs=specs,
        out_specs=tuple(VMEM for _ in outs),
        scratch_shapes=list(scratch),
        compiler_params=pltpu.CompilerParams(vmem_limit_bytes=24 << 20),
    )


def blocks_of(where_ref, own_ref, other_ref):
    zh, core = where_ref[0], where_ref[1]
    for x in range(4):
        for far in range(2):
            side = zh if far == 0 else 1 - zh
            yield x * 4 + side * 2 + core, own_ref.at[x, far]
            yield x * 4 + side * 2 + 1 - core, other_ref.at[x, far]


def edges(inputs_ref, upstream_ref, mask_ref, right_ref, left_ref):
    width, rows = inputs_ref.shape
    lane = lax.broadcasted_iota(jnp.int32, (width, 128), 1)
    low = lax.broadcasted_iota(jnp.int32, (16, 128), 1)

    def pack(start, own, moved, ref):
        ends = inputs_ref[:, start : start + 128].astype(f32)
        up = pltpu.roll(upstream_ref[:, start : start + 128].astype(f32), 64, 1)
        ref[:width] = jnp.where(
            own(lane), ends, jnp.where(moved(lane), up, 0.0)
        ).astype(bf16)
        mask = jnp.broadcast_to(mask_ref[:, start : start + 128].astype(f32), (16, 128))
        ref[width:] = jnp.where(own(low), mask, 0.0).astype(bf16)

    pack(rows - 128, lambda i: i >= 98, lambda i: (i >= 49) & (i < 64), right_ref)
    pack(0, lambda i: i < 30, lambda i: (i >= 64) & (i < 79), left_ref)


def middle(
    where_ref, own_hbm, other_hbm, small_hbm, weight_hbm, project_hbm, flipped_hbm, taps_hbm, mask_hbm,
    mixed_out, part0_out, part1_out, part2_out, part3_out, stats_out,
    own_ref, other_ref, small_ref, weight_ref, project_ref, flipped_ref, taps_ref, mask_ref,
    mixed_ref, grads_ref, stats_ref, normed_ref, full_ref, both_ref, act_ref, kernel_ref,
    proj_ref, grad_ref, moved_ref, back_ref, sems,
):
    model = weight_ref.shape[1]
    width = own_ref.shape[2]
    lanes = normed_ref.shape[2]
    rows = mixed_ref.shape[2]
    taps = taps_ref.shape[0]
    count = 0

    def copy(source, target):
        nonlocal count
        started = pltpu.make_async_copy(source, target, sems.at[count])
        started.start()
        count += 1
        return started

    blocks = [
        copy(source.at[x], target.at[x])
        for x in range(4)
        for source, target in ((own_hbm, own_ref), (other_hbm, other_ref))
    ]
    small_copy = copy(small_hbm, small_ref)
    mask_copy = copy(mask_hbm, mask_ref)
    project_copy = copy(project_hbm, project_ref)
    weight_copy = copy(weight_hbm, weight_ref)
    taps_copy = copy(taps_hbm, taps_ref)
    flipped_copy = copy(flipped_hbm, flipped_ref)
    total = jnp.zeros((8, lanes), f32)
    square = jnp.zeros((8, lanes), f32)
    for i, (place, block) in enumerate(blocks_of(where_ref, own_ref, other_ref)):
        if i % 4 == 0:
            blocks[i // 2].wait()
            blocks[i // 2 + 1].wait()
        x = block[:, :lanes].astype(f32).reshape(width // 8, 8, lanes)
        total = total + jnp.sum(x, axis=0)
        square = square + jnp.sum(x * x, axis=0)
        full_ref[place, :, :rows] = block[:, lanes:]
        full_ref[place, :, rows:] = pltpu.roll(
            block[:, rows:lanes].astype(f32), 64, 1
        ).astype(bf16)
    row_mean = jnp.sum(total, axis=0, keepdims=True) / model
    row_var = jnp.sum(square, axis=0, keepdims=True) / model - row_mean * row_mean
    inv_std = lax.rsqrt(row_var + eps)
    stats_ref[...] = jnp.concatenate(
        [row_mean, inv_std, jnp.zeros((6, lanes), f32)], axis=0
    )
    finished = [copy(stats_ref, stats_out)]
    small_copy.wait()
    for i, (place, block) in enumerate(blocks_of(where_ref, own_ref, other_ref)):
        centred = (block[:, :lanes].astype(f32) - row_mean) * inv_std
        normed_ref[place] = (
            centred * small_ref[:width, i : i + 1] + small_ref[:width, 16 + i : 17 + i]
        ).astype(bf16)
    project_copy.wait()
    grad_ref[...] = jnp.dot(
        project_ref[...], full_ref[...].reshape(model, lanes), preferred_element_type=f32
    )
    weight_copy.wait()
    proj_ref[...] = jnp.dot(
        weight_ref[...], normed_ref[...].reshape(model, lanes), preferred_element_type=f32
    )
    mask_copy.wait()
    taps_copy.wait()
    group = 16
    lane = lax.broadcasted_iota(jnp.int32, (group, 128), 1)
    inside = lax.broadcasted_iota(jnp.int32, (group, lanes), 1) < rows

    def channels(step, carry):
        first = pl.multiple_of(step * group, group)
        mine = pl.ds(first, group)
        after = pl.ds(pl.multiple_of(width + first, group), group)
        value = proj_ref[mine, :]
        gate = jax.nn.sigmoid(proj_ref[after, :])
        keep = mask_ref[...]
        glu = (value * gate * keep).astype(bf16).astype(f32)

        def shifted(x, by):
            return pltpu.roll(x, by % lanes, 1) if by % lanes else x

        def tap(k):
            return jnp.concatenate([taps_ref[k, mine, :]] * (lanes // 128), axis=1)

        def spread(fine, sign):
            result = None
            for a in range(4):
                part = None
                for b in range(8):
                    if 8 * a + b < taps:
                        term = tap(8 * a + b) * fine[b]
                        part = term if part is None else part + term
                part = shifted(part, sign * (8 * a - 8))
                result = part if result is None else result + part
            return result

        for b in range(8):
            moved_ref[b] = shifted(glu, 7 - b)
        conv = spread(moved_ref, -1)
        sig = jax.nn.sigmoid(conv)
        act_ref[mine, :] = (conv * sig)[:, :rows].astype(bf16)
        act_grad = grad_ref[mine, :].astype(bf16).astype(f32)
        grad = (act_grad * (sig + conv * sig * (1.0 - sig))).astype(bf16).astype(f32)
        for b in range(8):
            back_ref[b] = shifted(grad, b - 7)
        glu_grad = spread(back_ref, 1)[:, :rows]
        inner = jnp.where(inside, grad, 0.0)
        kernel = jnp.zeros((group, 128), f32)
        for a in range(4):
            here = shifted(inner, 8 * a - 8)
            for b in range(8):
                if 8 * a + b < taps:
                    seen = jnp.sum(here * moved_ref[b], axis=1, keepdims=True)
                    kernel = jnp.where(lane == 8 * a + b, seen, kernel)
        kernel_ref[mine, :] = kernel
        glu_grad = glu_grad * keep[:, :rows]
        gate = gate[:, :rows]
        both_ref[mine, :] = (glu_grad * gate).astype(bf16)
        both_ref[after, :] = (glu_grad * value[:, :rows] * gate * (1.0 - gate)).astype(bf16)
        return carry

    lax.fori_loop(0, width // group, channels, 0)
    both = both_ref[...]
    flipped_copy.wait()
    partial = jnp.dot(flipped_ref[...], both, preferred_element_type=f32).astype(bf16)
    partial = partial.reshape(4, 2, 2, width, rows)
    both = both.astype(f32)
    first = jnp.sum(both * small_ref[:, 32:33], axis=0, keepdims=True)
    second = jnp.sum(both * (proj_ref[:, :rows] - small_ref[:, 33:34]), axis=0, keepdims=True)
    first_high = first.astype(bf16).astype(f32)
    second_high = second.astype(bf16).astype(f32)
    row = lax.broadcasted_iota(jnp.int32, (16, rows), 0)
    extra = jnp.where(row == 0, first_high, 0.0)
    extra = jnp.where(row == 1, second_high, extra)
    extra = jnp.where(row == 2, first - first_high, extra)
    extra = jnp.where(row == 3, second - second_high, extra).astype(bf16)
    zh = where_ref[0]
    for x in range(4):
        for core in range(2):
            for side in range(2):
                start = pl.multiple_of(jnp.where(side == zh, width, 0), width)
                mixed_ref[x * 2 + core, pl.ds(start, width)] = partial[x, side, core]
            mixed_ref[x * 2 + core, 2 * width :] = extra
    finished.append(copy(mixed_ref, mixed_out))

    zero = jnp.zeros((width, rows), bf16)
    grads = lax.dot_general(
        normed_ref[:, :, :rows].reshape(model, rows),
        jnp.concatenate([zero, both_ref[...], zero], axis=0),
        OVER,
        preferred_element_type=f32,
    ) + lax.dot_general(
        full_ref[:, :, :rows].reshape(model, rows),
        jnp.concatenate([zero, zero, zero, act_ref[...]], axis=0),
        OVER,
        preferred_element_type=f32,
    )
    grads_ref[...] = grads.astype(bf16).reshape(grads_ref.shape)
    kernel = jnp.transpose(kernel_ref[...])[: grads_ref.shape[2]].astype(bf16)
    for zl in range(8):
        for y in range(4):
            grads_ref[zl, y, :, :width] = kernel
    for step, out in zip((0, 1, 3, 2), (part0_out, part1_out, part2_out, part3_out)):
        out[...] = grads_ref[:, lax.rem(where_ref[2] + step, 4)]
    for started in finished:
        started.wait()


def on_device(
    inputs,
    norm_gain,
    norm_bias,
    value_weight,
    gate_weight,
    conv_kernel,
    project_weight,
    frame_mask,
    upstream,
):
    width, rows = inputs.shape
    model = value_weight.shape[1]
    taps = conv_kernel.shape[0]
    lanes = rows + 128
    piece = model // 32
    zh = lax.axis_index("zh")
    core = lax.axis_index("core")
    y = lax.axis_index("y")
    zl = lax.axis_index("zl")
    offset = lax.axis_index(CHAN) * width
    where = jnp.stack([zh, core, y]).astype(jnp.int32)

    to_right, to_left = call(
        edges,
        (shape((width + 16, 128), bf16), shape((width + 16, 128), bf16)),
        specs=[VMEM] * 3,
    )(inputs, upstream, frame_mask.reshape(1, rows))
    edge = lax.ppermute(to_right, FRAME, [(i, i + 1) for i in range(31)]) + lax.ppermute(
        to_left, FRAME, [(i + 1, i) for i in range(31)]
    )

    weights = jnp.concatenate([value_weight, gate_weight])
    by_gain = jnp.sum(weights.astype(f32) * norm_gain[None, :], axis=1, keepdims=True)
    by_bias = jnp.sum(weights.astype(f32) * norm_bias[None, :], axis=1, keepdims=True)
    gain_local = lax.dynamic_slice_in_dim(norm_gain, offset, width, 0)[:, None]

    def columns_of(parameter):
        parameter = parameter.reshape(4, 2, 2, width)
        parameter = jnp.where(zh == 0, parameter, parameter[:, ::-1])
        parameter = jnp.where(core == 0, parameter, parameter[:, :, ::-1])
        return parameter.reshape(16, width).T

    small = jnp.concatenate([columns_of(norm_gain), columns_of(norm_bias)], axis=1)
    small = jnp.concatenate([jnp.pad(small, ((0, width), (0, 0))), by_gain, by_bias], axis=1)
    small = jnp.pad(small, ((0, 0), (0, 128 - small.shape[1])))
    wide_taps = jnp.broadcast_to(conv_kernel[:, :, None], (taps, width, 128))
    early = (weights, weights.T, small, wide_taps, gain_local, where)

    held = jnp.concatenate([inputs, edge[:width], upstream], axis=1)
    keep = jnp.concatenate([frame_mask.astype(f32)[None, :], edge[width : width + 1].astype(f32)], axis=1)
    came = swap(held, "zh")
    came, keep, early = lax.optimization_barrier((came, keep, early))
    weights, flipped, small, wide_taps, gain_local, where = early
    own = over_x(jnp.stack([held, came]))
    other = swap(own, "core")
    piece_shape = (8, piece, 4 * width)
    operands = (own, other, small, weights, project_weight, flipped, wide_taps, keep)
    mixed, *pieces, stats = pl.pallas_call(
        middle,
        out_shape=(
            pltpu.HBM((8, 2 * width + 16, rows), bf16),
            *(pltpu.VMEM(piece_shape, bf16) for _ in range(4)),
            pltpu.HBM((8, lanes), f32),
        ),
        in_specs=[SMEM] + [pl.BlockSpec(memory_space=pltpu.HBM)] * len(operands),
        out_specs=tuple(pl.BlockSpec(memory_space=pltpu.HBM if i in (0, 5) else pltpu.VMEM) for i in range(6)),
        scratch_shapes=[pltpu.VMEM(operand.shape, operand.dtype) for operand in operands]
        + [
            pltpu.VMEM((8, 2 * width + 16, rows), bf16),
            pltpu.VMEM((8, 4, piece, 4 * width), bf16),
            pltpu.VMEM((8, lanes), f32),
            pltpu.VMEM((16, width, lanes), bf16),
            pltpu.VMEM((16, width, lanes), bf16),
            pltpu.VMEM((2 * width, rows), bf16),
            pltpu.VMEM((width, rows), bf16),
            pltpu.VMEM((width, 128), f32),
            pltpu.VMEM((2 * width, lanes), f32),
            pltpu.VMEM((width, lanes), f32),
            pltpu.VMEM((8, 16, lanes), f32),
            pltpu.VMEM((8, 16, lanes), f32),
            pltpu.SemaphoreType.DMA((20,)),
        ],
        compiler_params=pltpu.CompilerParams(vmem_limit_bytes=40 << 20),
    )(where, *(pltpu.with_memory_space_constraint(operand, pltpu.HBM) for operand in operands))

    mixed = lax.all_to_all(mixed, ("x", "core"), 0, 0, tiled=True)

    parts = [
        lax.ppermute(sent, "y", [(i, (i + step) % 4) for i in range(4)])
        for step, sent in zip((1, 3, 2), pieces[1:])
    ]
    mixed = jnp.sum(mixed.astype(f32), axis=0)
    far_sums = mixed[2 * width : 2 * width + 2] + mixed[2 * width + 2 : 2 * width + 4]
    sent_high, sent_low = split_bf16(far_sums)
    far = jnp.concatenate(
        [mixed[:width].astype(bf16), sent_high, sent_low, jnp.zeros((12, rows), bf16)]
    )
    came = swap(far, "zh").astype(f32)

    total, far_copy = lax.optimization_barrier((pieces[0], far))
    total = total.astype(f32)
    for part in parts:
        total = total + part.astype(f32)

    def block(index):
        return lax.dynamic_slice_in_dim(total, index, 1, 0)[0]

    side = zl % 2
    total = total.reshape(4, 2, piece, 4 * width)
    sent = lax.dynamic_slice_in_dim(total, 1 - side, 1, 1)[:, 0].astype(bf16)
    total = lax.dynamic_slice_in_dim(total, side, 1, 1)[:, 0]
    total = total + lax.ppermute(sent, "zl", [(i, i ^ 1) for i in range(8)]).astype(f32)

    normed_grad = mixed[width : 2 * width] + came[:width]
    kept = far_copy[width : width + 4].astype(f32)
    sums = (kept[:2] + kept[2:] + came[width : width + 2] + came[width + 2 : width + 4]) / model
    inv_std = stats[1:2, :rows]
    centred = (inputs.astype(f32) - stats[0:1, :rows]) * inv_std
    tail = jnp.stack([jnp.sum(normed_grad * centred, axis=1), jnp.sum(normed_grad, axis=1)])
    tail = lax.all_to_all(
        jnp.broadcast_to(tail[None], (32, 2, width)), FRAME, 0, 0, tiled=True
    )
    inputs_grad = (
        upstream.astype(f32)
        + inv_std * (normed_grad * gain_local - sums[0:1] - centred * sums[1:2])
    ).astype(bf16)

    grads = block(zl // 2)
    for step in (3, 2, 1):
        sent = block((zl // 2) ^ step).astype(bf16)
        grads = grads + lax.ppermute(sent, "zl", [(i, i ^ (2 * step)) for i in range(8)]).astype(f32)
    tail, grads = lax.optimization_barrier((tail, grads))
    tail = jnp.sum(tail, axis=0)
    kernel_grad = grads[:taps, :width]
    value_grad = grads[:, width : 2 * width].T
    gate_grad = grads[:, 2 * width : 3 * width].T
    project_grad = grads[:, 3 * width :].T
    return (inputs_grad, value_grad, gate_grad, project_grad, kernel_grad, tail[0], tail[1])


def solution(mesh):
    split = Mesh(mesh.devices.reshape(8, 4, 4, 2, 2), FRAME + CHAN)
    return jax.shard_map(
        on_device,
        mesh=split,
        in_specs=(
            P(CHAN, FRAME),
            P(),
            P(),
            P(CHAN, None),
            P(CHAN, None),
            P(None, CHAN),
            P(CHAN, None),
            P(FRAME),
            P(CHAN, FRAME),
        ),
        out_specs=(
            P(CHAN, FRAME),
            P(CHAN, FRAME),
            P(CHAN, FRAME),
            P(CHAN, FRAME),
            P(None, CHAN),
            P(CHAN),
            P(CHAN),
        ),
        check_vma=False,
    )
```

```python
import jax
import jax.numpy as jnp
from jax import lax
from jax.experimental import pallas as pl
from jax.experimental.pallas import tpu as pltpu
from jax.sharding import Mesh, PartitionSpec as P

eps = 1e-05
CHAN = ("x", "zh", "core")
FRAME = ("zl", "y")
SWAP = [(0, 1), (1, 0)]
f32 = jnp.float32
bf16 = jnp.bfloat16
VMEM = pl.BlockSpec(memory_space=pltpu.VMEM)
SMEM = pl.BlockSpec(memory_space=pltpu.SMEM)
OVER = (((1,), (1,)), ((), ()))


def swap(value, axis):
    return lax.ppermute(value, axis, SWAP)


def over_x(pair):
    return lax.all_to_all(
        jnp.broadcast_to(pair[None], (4,) + pair.shape), "x", 0, 0, tiled=True
    )


def split_bf16(value):
    high = value.astype(bf16)
    return high, (value - high.astype(f32)).astype(bf16)


def shape(dims, dtype):
    return jax.ShapeDtypeStruct(dims, dtype)


def call(kernel, outs, scratch=(), specs=None):
    return pl.pallas_call(
        kernel,
        out_shape=outs,
        in_specs=specs,
        out_specs=tuple(VMEM for _ in outs),
        scratch_shapes=list(scratch),
        compiler_params=pltpu.CompilerParams(vmem_limit_bytes=24 << 20),
    )


def blocks_of(where_ref, own_ref, other_ref):
    zh, core = where_ref[0], where_ref[1]
    for x in range(4):
        for far in range(2):
            side = zh if far == 0 else 1 - zh
            yield x * 4 + side * 2 + core, own_ref.at[x, far]
            yield x * 4 + side * 2 + 1 - core, other_ref.at[x, far]


def edges(inputs_ref, upstream_ref, mask_ref, right_ref, left_ref):
    width, rows = inputs_ref.shape
    lane = lax.broadcasted_iota(jnp.int32, (width, 128), 1)
    low = lax.broadcasted_iota(jnp.int32, (16, 128), 1)

    def pack(start, own, moved, ref):
        ends = inputs_ref[:, start : start + 128].astype(f32)
        up = pltpu.roll(upstream_ref[:, start : start + 128].astype(f32), 64, 1)
        ref[:width] = jnp.where(
            own(lane), ends, jnp.where(moved(lane), up, 0.0)
        ).astype(bf16)
        mask = jnp.broadcast_to(mask_ref[:, start : start + 128].astype(f32), (16, 128))
        ref[width:] = jnp.where(own(low), mask, 0.0).astype(bf16)

    pack(rows - 128, lambda i: i >= 98, lambda i: (i >= 49) & (i < 64), right_ref)
    pack(0, lambda i: i < 30, lambda i: (i >= 64) & (i < 79), left_ref)


def middle(
    where_ref, own_hbm, other_hbm, small_hbm, weight_hbm, project_hbm, flipped_hbm, mask_hbm,
    mixed_out, part0_out, part1_out, part2_out, part3_out, stats_out,
    own_ref, other_ref, small_ref, weight_ref, project_ref, flipped_ref, mask_ref,
    taps_ref, mixed_ref, grads_ref, stats_ref, normed_ref, full_ref, both_ref, act_ref, kernel_ref,
    proj_ref, grad_ref, moved_ref, back_ref, sems,
):
    model = weight_ref.shape[1]
    width = own_ref.shape[2]
    lanes = normed_ref.shape[2]
    rows = mixed_ref.shape[2]
    taps = taps_ref.shape[0]
    count = 0

    def copy(source, target):
        nonlocal count
        started = pltpu.make_async_copy(source, target, sems.at[count])
        started.start()
        count += 1
        return started

    small_copy = copy(small_hbm, small_ref)
    blocks = [
        copy(source.at[x], target.at[x])
        for x in range(4)
        for source, target in ((own_hbm, own_ref), (other_hbm, other_ref))
    ]
    mask_copy = copy(mask_hbm, mask_ref)
    project_copy = copy(project_hbm, project_ref)
    weight_copy = copy(weight_hbm, weight_ref)
    flipped_copy = copy(flipped_hbm, flipped_ref)
    small_copy.wait()
    for k in range(taps):
        taps_ref[k] = jnp.broadcast_to(small_ref[:width, 34 + k : 35 + k], (width, 128))
    total = jnp.zeros((8, lanes), f32)
    square = jnp.zeros((8, lanes), f32)
    for i, (place, block) in enumerate(blocks_of(where_ref, own_ref, other_ref)):
        if i % 4 == 0:
            blocks[i // 2].wait()
            blocks[i // 2 + 1].wait()
        x = block[:, :lanes].astype(f32).reshape(width // 8, 8, lanes)
        total = total + jnp.sum(x, axis=0)
        square = square + jnp.sum(x * x, axis=0)
        full_ref[place, :, :rows] = block[:, lanes:]
        full_ref[place, :, rows:] = pltpu.roll(
            block[:, rows:lanes].astype(f32), 64, 1
        ).astype(bf16)
    row_mean = jnp.sum(total, axis=0, keepdims=True) / model
    row_var = jnp.sum(square, axis=0, keepdims=True) / model - row_mean * row_mean
    inv_std = lax.rsqrt(row_var + eps)
    stats_ref[...] = jnp.concatenate(
        [row_mean, inv_std, jnp.zeros((6, lanes), f32)], axis=0
    )
    finished = [copy(stats_ref, stats_out)]
    for i, (place, block) in enumerate(blocks_of(where_ref, own_ref, other_ref)):
        centred = (block[:, :lanes].astype(f32) - row_mean) * inv_std
        normed_ref[place] = (
            centred * small_ref[:width, i : i + 1] + small_ref[:width, 16 + i : 17 + i]
        ).astype(bf16)
    project_copy.wait()
    grad_ref[...] = jnp.dot(
        project_ref[...], full_ref[...].reshape(model, lanes), preferred_element_type=f32
    )
    weight_copy.wait()
    proj_ref[...] = jnp.dot(
        weight_ref[...], normed_ref[...].reshape(model, lanes), preferred_element_type=f32
    )
    mask_copy.wait()
    group = 16
    lane = lax.broadcasted_iota(jnp.int32, (group, 128), 1)
    inside = lax.broadcasted_iota(jnp.int32, (group, lanes), 1) < rows

    def channels(step, carry):
        first = pl.multiple_of(step * group, group)
        mine = pl.ds(first, group)
        after = pl.ds(pl.multiple_of(width + first, group), group)
        value = proj_ref[mine, :]
        gate = jax.nn.sigmoid(proj_ref[after, :])
        keep = mask_ref[...]
        glu = (value * gate * keep).astype(bf16).astype(f32)

        def shifted(x, by):
            return pltpu.roll(x, by % lanes, 1) if by % lanes else x

        def tap(k):
            return jnp.concatenate([taps_ref[k, mine, :]] * (lanes // 128), axis=1)

        def spread(fine, sign):
            result = None
            for a in range(4):
                part = None
                for b in range(8):
                    if 8 * a + b < taps:
                        term = tap(8 * a + b) * fine[b]
                        part = term if part is None else part + term
                part = shifted(part, sign * (8 * a - 8))
                result = part if result is None else result + part
            return result

        for b in range(8):
            moved_ref[b] = shifted(glu, 7 - b)
        conv = spread(moved_ref, -1)
        sig = jax.nn.sigmoid(conv)
        act_ref[mine, :] = (conv * sig)[:, :rows].astype(bf16)
        act_grad = grad_ref[mine, :].astype(bf16).astype(f32)
        grad = (act_grad * (sig + conv * sig * (1.0 - sig))).astype(bf16).astype(f32)
        for b in range(8):
            back_ref[b] = shifted(grad, b - 7)
        glu_grad = spread(back_ref, 1)[:, :rows]
        inner = jnp.where(inside, grad, 0.0)
        kernel = jnp.zeros((group, 128), f32)
        for a in range(4):
            here = shifted(inner, 8 * a - 8)
            for b in range(8):
                if 8 * a + b < taps:
                    seen = jnp.sum(here * moved_ref[b], axis=1, keepdims=True)
                    kernel = jnp.where(lane == 8 * a + b, seen, kernel)
        kernel_ref[mine, :] = kernel
        glu_grad = glu_grad * keep[:, :rows]
        gate = gate[:, :rows]
        both_ref[mine, :] = (glu_grad * gate).astype(bf16)
        both_ref[after, :] = (glu_grad * value[:, :rows] * gate * (1.0 - gate)).astype(bf16)
        return carry

    lax.fori_loop(0, width // group, channels, 0)
    both = both_ref[...]
    flipped_copy.wait()
    partial = jnp.dot(flipped_ref[...], both, preferred_element_type=f32).astype(bf16)
    partial = partial.reshape(4, 2, 2, width, rows)
    both = both.astype(f32)
    first = jnp.sum(both * small_ref[:, 32:33], axis=0, keepdims=True)
    second = jnp.sum(both * (proj_ref[:, :rows] - small_ref[:, 33:34]), axis=0, keepdims=True)
    first_high = first.astype(bf16).astype(f32)
    second_high = second.astype(bf16).astype(f32)
    row = lax.broadcasted_iota(jnp.int32, (16, rows), 0)
    extra = jnp.where(row == 0, first_high, 0.0)
    extra = jnp.where(row == 1, second_high, extra)
    extra = jnp.where(row == 2, first - first_high, extra)
    extra = jnp.where(row == 3, second - second_high, extra).astype(bf16)
    zh = where_ref[0]
    for x in range(4):
        for core in range(2):
            for side in range(2):
                start = pl.multiple_of(jnp.where(side == zh, width, 0), width)
                mixed_ref[x * 2 + core, pl.ds(start, width)] = partial[x, side, core]
            mixed_ref[x * 2 + core, 2 * width :] = extra
    finished.append(copy(mixed_ref, mixed_out))

    zero = jnp.zeros((width, rows), bf16)
    grads = lax.dot_general(
        normed_ref[:, :, :rows].reshape(model, rows),
        jnp.concatenate([zero, both_ref[...], zero], axis=0),
        OVER,
        preferred_element_type=f32,
    ) + lax.dot_general(
        full_ref[:, :, :rows].reshape(model, rows),
        jnp.concatenate([zero, zero, zero, act_ref[...]], axis=0),
        OVER,
        preferred_element_type=f32,
    )
    grads_ref[...] = grads.astype(bf16).reshape(grads_ref.shape)
    kernel = jnp.transpose(kernel_ref[...])[: grads_ref.shape[2]].astype(bf16)
    for zl in range(8):
        for y in range(4):
            grads_ref[zl, y, :, :width] = kernel
    for step, out in zip((0, 1, 3, 2), (part0_out, part1_out, part2_out, part3_out)):
        out[...] = grads_ref[:, lax.rem(where_ref[2] + step, 4)]
    for started in finished:
        started.wait()


def on_device(
    inputs,
    norm_gain,
    norm_bias,
    value_weight,
    gate_weight,
    conv_kernel,
    project_weight,
    frame_mask,
    upstream,
):
    width, rows = inputs.shape
    model = value_weight.shape[1]
    taps = conv_kernel.shape[0]
    lanes = rows + 128
    piece = model // 32
    zh = lax.axis_index("zh")
    core = lax.axis_index("core")
    y = lax.axis_index("y")
    zl = lax.axis_index("zl")
    offset = lax.axis_index(CHAN) * width
    where = jnp.stack([zh, core, y]).astype(jnp.int32)

    to_right, to_left = call(
        edges,
        (shape((width + 16, 128), bf16), shape((width + 16, 128), bf16)),
        specs=[VMEM] * 3,
    )(inputs, upstream, frame_mask.reshape(1, rows))
    edge = lax.ppermute(to_right, FRAME, [(i, i + 1) for i in range(31)]) + lax.ppermute(
        to_left, FRAME, [(i + 1, i) for i in range(31)]
    )

    weights = jnp.concatenate([value_weight, gate_weight])
    by_gain = jnp.sum(weights.astype(f32) * norm_gain[None, :], axis=1, keepdims=True)
    by_bias = jnp.sum(weights.astype(f32) * norm_bias[None, :], axis=1, keepdims=True)
    gain_local = lax.dynamic_slice_in_dim(norm_gain, offset, width, 0)[:, None]

    def columns_of(parameter):
        parameter = parameter.reshape(4, 2, 2, width)
        parameter = jnp.where(zh == 0, parameter, parameter[:, ::-1])
        parameter = jnp.where(core == 0, parameter, parameter[:, :, ::-1])
        return parameter.reshape(16, width).T

    small = jnp.concatenate([columns_of(norm_gain), columns_of(norm_bias)], axis=1)
    small = jnp.concatenate(
        [
            jnp.pad(small, ((0, width), (0, 0))),
            by_gain,
            by_bias,
            jnp.pad(conv_kernel.T, ((0, width), (0, 128 - 34 - taps))),
        ],
        axis=1,
    )
    early = (weights, weights.T, small, gain_local, where)

    held = jnp.concatenate([inputs, edge[:width], upstream], axis=1)
    keep = jnp.concatenate([frame_mask.astype(f32)[None, :], edge[width : width + 1].astype(f32)], axis=1)
    came = swap(held, "zh")
    came, keep, early = lax.optimization_barrier((came, keep, early))
    weights, flipped, small, gain_local, where = early
    own = over_x(jnp.stack([held, came]))
    other = swap(own, "core")
    piece_shape = (8, piece, 4 * width)
    operands = (own, other, small, weights, project_weight, flipped, keep)
    mixed, *pieces, stats = pl.pallas_call(
        middle,
        out_shape=(
            pltpu.HBM((8, 2 * width + 16, rows), bf16),
            *(pltpu.VMEM(piece_shape, bf16) for _ in range(4)),
            pltpu.HBM((8, lanes), f32),
        ),
        in_specs=[SMEM] + [pl.BlockSpec(memory_space=pltpu.HBM)] * len(operands),
        out_specs=tuple(pl.BlockSpec(memory_space=pltpu.HBM if i in (0, 5) else pltpu.VMEM) for i in range(6)),
        scratch_shapes=[pltpu.VMEM(operand.shape, operand.dtype) for operand in operands]
        + [
            pltpu.VMEM((taps, width, 128), f32),
            pltpu.VMEM((8, 2 * width + 16, rows), bf16),
            pltpu.VMEM((8, 4, piece, 4 * width), bf16),
            pltpu.VMEM((8, lanes), f32),
            pltpu.VMEM((16, width, lanes), bf16),
            pltpu.VMEM((16, width, lanes), bf16),
            pltpu.VMEM((2 * width, rows), bf16),
            pltpu.VMEM((width, rows), bf16),
            pltpu.VMEM((width, 128), f32),
            pltpu.VMEM((2 * width, lanes), f32),
            pltpu.VMEM((width, lanes), f32),
            pltpu.VMEM((8, 16, lanes), f32),
            pltpu.VMEM((8, 16, lanes), f32),
            pltpu.SemaphoreType.DMA((20,)),
        ],
        compiler_params=pltpu.CompilerParams(vmem_limit_bytes=40 << 20),
    )(where, *(pltpu.with_memory_space_constraint(operand, pltpu.HBM) for operand in operands))

    mixed = lax.all_to_all(mixed, ("x", "core"), 0, 0, tiled=True)

    parts = [
        lax.ppermute(sent, "y", [(i, (i + step) % 4) for i in range(4)])
        for step, sent in zip((1, 3, 2), pieces[1:])
    ]
    mixed = jnp.sum(mixed.astype(f32), axis=0)
    far_sums = mixed[2 * width : 2 * width + 2] + mixed[2 * width + 2 : 2 * width + 4]
    sent_high, sent_low = split_bf16(far_sums)
    far = jnp.concatenate(
        [mixed[:width].astype(bf16), sent_high, sent_low, jnp.zeros((12, rows), bf16)]
    )
    came = swap(far, "zh").astype(f32)

    total, far_copy = lax.optimization_barrier((pieces[0], far))
    total = total.astype(f32)
    for part in parts:
        total = total + part.astype(f32)

    def block(index):
        return lax.dynamic_slice_in_dim(total, index, 1, 0)[0]

    side = zl % 2
    total = total.reshape(4, 2, piece, 4 * width)
    sent = lax.dynamic_slice_in_dim(total, 1 - side, 1, 1)[:, 0].astype(bf16)
    total = lax.dynamic_slice_in_dim(total, side, 1, 1)[:, 0]
    total = total + lax.ppermute(sent, "zl", [(i, i ^ 1) for i in range(8)]).astype(f32)

    normed_grad = mixed[width : 2 * width] + came[:width]
    kept = far_copy[width : width + 4].astype(f32)
    sums = (kept[:2] + kept[2:] + came[width : width + 2] + came[width + 2 : width + 4]) / model
    inv_std = stats[1:2, :rows]
    centred = (inputs.astype(f32) - stats[0:1, :rows]) * inv_std
    tail = jnp.stack([jnp.sum(normed_grad * centred, axis=1), jnp.sum(normed_grad, axis=1)])
    total, normed_grad = lax.optimization_barrier((total, normed_grad))
    tail = lax.all_to_all(
        jnp.broadcast_to(tail[None], (32, 2, width)), FRAME, 0, 0, tiled=True
    )
    inputs_grad = (
        upstream.astype(f32)
        + inv_std * (normed_grad * gain_local - sums[0:1] - centred * sums[1:2])
    ).astype(bf16)

    grads = block(zl // 2)
    for step in (3, 2, 1):
        sent = block((zl // 2) ^ step).astype(bf16)
        grads = grads + lax.ppermute(sent, "zl", [(i, i ^ (2 * step)) for i in range(8)]).astype(f32)
    tail, grads = lax.optimization_barrier((tail, grads))
    tail = jnp.sum(tail, axis=0)
    kernel_grad = grads[:taps, :width]
    value_grad = grads[:, width : 2 * width].T
    gate_grad = grads[:, 2 * width : 3 * width].T
    project_grad = grads[:, 3 * width :].T
    return (inputs_grad, value_grad, gate_grad, project_grad, kernel_grad, tail[0], tail[1])


def solution(mesh):
    split = Mesh(mesh.devices.reshape(8, 4, 4, 2, 2), FRAME + CHAN)
    return jax.shard_map(
        on_device,
        mesh=split,
        in_specs=(
            P(CHAN, FRAME),
            P(),
            P(),
            P(CHAN, None),
            P(CHAN, None),
            P(None, CHAN),
            P(CHAN, None),
            P(FRAME),
            P(CHAN, FRAME),
        ),
        out_specs=(
            P(CHAN, FRAME),
            P(CHAN, FRAME),
            P(CHAN, FRAME),
            P(CHAN, FRAME),
            P(None, CHAN),
            P(CHAN),
            P(CHAN),
        ),
        check_vma=False,
    )
```

```python
import jax
import jax.numpy as jnp
from jax import lax
from jax.experimental import pallas as pl
from jax.experimental.pallas import tpu as pltpu
from jax.sharding import Mesh, PartitionSpec as P

eps = 1e-05
CHAN = ("x", "zh", "core")
FRAME = ("zl", "y")
SWAP = [(0, 1), (1, 0)]
f32 = jnp.float32
bf16 = jnp.bfloat16
VMEM = pl.BlockSpec(memory_space=pltpu.VMEM)
SMEM = pl.BlockSpec(memory_space=pltpu.SMEM)
OVER = (((1,), (1,)), ((), ()))


def swap(value, axis):
    return lax.ppermute(value, axis, SWAP)


def over_x(pair):
    return lax.all_to_all(
        jnp.broadcast_to(pair[None], (4,) + pair.shape), "x", 0, 0, tiled=True
    )


def ordered(own, other, index, axis):
    return jnp.where(
        index == 0, jnp.stack([own, other], axis), jnp.stack([other, own], axis)
    )


def split_bf16(value):
    high = value.astype(bf16)
    return high, (value - high.astype(f32)).astype(bf16)


def shape(dims, dtype):
    return jax.ShapeDtypeStruct(dims, dtype)


def call(kernel, outs, scratch=(), specs=None):
    return pl.pallas_call(
        kernel,
        out_shape=outs,
        in_specs=specs,
        out_specs=tuple(VMEM for _ in outs),
        scratch_shapes=list(scratch),
        compiler_params=pltpu.CompilerParams(vmem_limit_bytes=24 << 20),
    )


def blocks_of(where_ref, own_ref, other_ref):
    zh, core = where_ref[0], where_ref[1]
    for x in range(4):
        for far in range(2):
            side = zh if far == 0 else 1 - zh
            yield x * 4 + side * 2 + core, own_ref.at[x, far]
            yield x * 4 + side * 2 + 1 - core, other_ref.at[x, far]


def edges(inputs_hbm, upstream_hbm, mask_ref, right_ref, left_ref, ends_ref, sems):
    width, rows = inputs_hbm.shape
    starts = (rows - 128, 0)
    copies = []
    for i, start in enumerate(starts):
        for j, source in enumerate((inputs_hbm, upstream_hbm)):
            copies.append(
                pltpu.make_async_copy(
                    source.at[:, start : start + 128], ends_ref.at[i, j], sems.at[2 * i + j]
                )
            )
            copies[-1].start()
    for started in copies:
        started.wait()
    lane = lax.broadcasted_iota(jnp.int32, (width, 128), 1)
    low = lax.broadcasted_iota(jnp.int32, (16, 128), 1)

    def pack(i, own, moved, ref):
        up = pltpu.roll(ends_ref[i, 1].astype(f32), 64, 1)
        ref[:width] = jnp.where(
            own(lane), ends_ref[i, 0].astype(f32), jnp.where(moved(lane), up, 0.0)
        ).astype(bf16)
        mask = mask_ref[:, starts[i] : starts[i] + 128].astype(f32)
        ref[width:] = jnp.where(own(low), jnp.broadcast_to(mask, (16, 128)), 0.0).astype(bf16)

    pack(0, lambda i: i >= 98, lambda i: (i >= 49) & (i < 64), right_ref)
    pack(1, lambda i: i < 30, lambda i: (i >= 64) & (i < 79), left_ref)


def middle(
    where_ref, own_hbm, other_hbm, small_hbm, weight_hbm, project_hbm, flipped_hbm, mask_hbm,
    mixed_out, part0_out, part1_out, part2_out, part3_out, stats_out,
    own_ref, other_ref, small_ref, weight_ref, project_ref, flipped_ref, mask_ref,
    taps_ref, mixed_ref, grads_ref, stats_ref, normed_ref, full_ref, both_ref, act_ref, kernel_ref,
    proj_ref, grad_ref, moved_ref, back_ref, sems,
):
    model = weight_ref.shape[1]
    width = own_ref.shape[2]
    lanes = normed_ref.shape[2]
    rows = mixed_ref.shape[2]
    taps = taps_ref.shape[0]
    count = 0

    def copy(source, target):
        nonlocal count
        started = pltpu.make_async_copy(source, target, sems.at[count])
        started.start()
        count += 1
        return started

    small_copy = copy(small_hbm, small_ref)
    blocks = [
        copy(source.at[x], target.at[x])
        for x in range(4)
        for source, target in ((own_hbm, own_ref), (other_hbm, other_ref))
    ]
    mask_copy = copy(mask_hbm, mask_ref)
    project_copy = copy(project_hbm, project_ref)
    weight_copy = copy(weight_hbm, weight_ref)
    flipped_copy = copy(flipped_hbm, flipped_ref)
    small_copy.wait()
    for k in range(taps):
        taps_ref[k] = jnp.broadcast_to(small_ref[:width, 34 + k : 35 + k], (width, 128))
    total = jnp.zeros((8, lanes), f32)
    square = jnp.zeros((8, lanes), f32)
    for i, (place, block) in enumerate(blocks_of(where_ref, own_ref, other_ref)):
        if i % 4 == 0:
            blocks[i // 2].wait()
            blocks[i // 2 + 1].wait()
        x = block[:, :lanes].astype(f32).reshape(width // 8, 8, lanes)
        total = total + jnp.sum(x, axis=0)
        square = square + jnp.sum(x * x, axis=0)
        full_ref[place, :, :rows] = block[:, lanes:]
        full_ref[place, :, rows:] = pltpu.roll(
            block[:, rows:lanes].astype(f32), 64, 1
        ).astype(bf16)
    row_mean = jnp.sum(total, axis=0, keepdims=True) / model
    row_var = jnp.sum(square, axis=0, keepdims=True) / model - row_mean * row_mean
    inv_std = lax.rsqrt(row_var + eps)
    stats_ref[...] = jnp.concatenate(
        [row_mean, inv_std, jnp.zeros((6, lanes), f32)], axis=0
    )
    finished = [copy(stats_ref, stats_out)]
    for i, (place, block) in enumerate(blocks_of(where_ref, own_ref, other_ref)):
        centred = (block[:, :lanes].astype(f32) - row_mean) * inv_std
        normed_ref[place] = (
            centred * small_ref[:width, i : i + 1] + small_ref[:width, 16 + i : 17 + i]
        ).astype(bf16)
    project_copy.wait()
    grad_ref[...] = jnp.dot(
        project_ref[...], full_ref[...].reshape(model, lanes), preferred_element_type=f32
    )
    weight_copy.wait()
    proj_ref[...] = jnp.dot(
        weight_ref[...], normed_ref[...].reshape(model, lanes), preferred_element_type=f32
    )
    mask_copy.wait()
    group = 16
    lane = lax.broadcasted_iota(jnp.int32, (group, 128), 1)
    inside = lax.broadcasted_iota(jnp.int32, (group, lanes), 1) < rows

    def channels(step, carry):
        first = pl.multiple_of(step * group, group)
        mine = pl.ds(first, group)
        after = pl.ds(pl.multiple_of(width + first, group), group)
        value = proj_ref[mine, :]
        gate = jax.nn.sigmoid(proj_ref[after, :])
        keep = mask_ref[...]
        glu = (value * gate * keep).astype(bf16).astype(f32)

        def shifted(x, by):
            return pltpu.roll(x, by % lanes, 1) if by % lanes else x

        def tap(k):
            return jnp.concatenate([taps_ref[k, mine, :]] * (lanes // 128), axis=1)

        def spread(fine, sign):
            result = None
            for a in range(4):
                part = None
                for b in range(8):
                    if 8 * a + b < taps:
                        term = tap(8 * a + b) * fine[b]
                        part = term if part is None else part + term
                part = shifted(part, sign * (8 * a - 8))
                result = part if result is None else result + part
            return result

        for b in range(8):
            moved_ref[b] = shifted(glu, 7 - b)
        conv = spread(moved_ref, -1)
        sig = jax.nn.sigmoid(conv)
        act_ref[mine, :] = (conv * sig)[:, :rows].astype(bf16)
        act_grad = grad_ref[mine, :].astype(bf16).astype(f32)
        grad = (act_grad * (sig + conv * sig * (1.0 - sig))).astype(bf16).astype(f32)
        for b in range(8):
            back_ref[b] = shifted(grad, b - 7)
        glu_grad = spread(back_ref, 1)[:, :rows]
        inner = jnp.where(inside, grad, 0.0)
        kernel = jnp.zeros((group, 128), f32)
        for a in range(4):
            here = shifted(inner, 8 * a - 8)
            for b in range(8):
                if 8 * a + b < taps:
                    seen = jnp.sum(here * moved_ref[b], axis=1, keepdims=True)
                    kernel = jnp.where(lane == 8 * a + b, seen, kernel)
        kernel_ref[mine, :] = kernel
        glu_grad = glu_grad * keep[:, :rows]
        gate = gate[:, :rows]
        both_ref[mine, :] = (glu_grad * gate).astype(bf16)
        both_ref[after, :] = (glu_grad * value[:, :rows] * gate * (1.0 - gate)).astype(bf16)
        return carry

    lax.fori_loop(0, width // group, channels, 0)
    both = both_ref[...]
    flipped_copy.wait()
    partial = jnp.dot(flipped_ref[...], both, preferred_element_type=f32).astype(bf16)
    partial = partial.reshape(4, 2, 2, width, rows)
    both = both.astype(f32)
    first = jnp.sum(both * small_ref[:, 32:33], axis=0, keepdims=True)
    second = jnp.sum(both * (proj_ref[:, :rows] - small_ref[:, 33:34]), axis=0, keepdims=True)
    first_high = first.astype(bf16).astype(f32)
    second_high = second.astype(bf16).astype(f32)
    row = lax.broadcasted_iota(jnp.int32, (16, rows), 0)
    extra = jnp.where(row == 0, first_high, 0.0)
    extra = jnp.where(row == 1, second_high, extra)
    extra = jnp.where(row == 2, first - first_high, extra)
    extra = jnp.where(row == 3, second - second_high, extra).astype(bf16)
    zh = where_ref[0]
    for x in range(4):
        for core in range(2):
            for side in range(2):
                start = pl.multiple_of(jnp.where(side == zh, width, 0), width)
                mixed_ref[x * 2 + core, pl.ds(start, width)] = partial[x, side, core]
            mixed_ref[x * 2 + core, 2 * width :] = extra
    finished.append(copy(mixed_ref, mixed_out))

    zero = jnp.zeros((width, rows), bf16)
    grads = lax.dot_general(
        normed_ref[:, :, :rows].reshape(model, rows),
        jnp.concatenate([zero, both_ref[...], zero], axis=0),
        OVER,
        preferred_element_type=f32,
    ) + lax.dot_general(
        full_ref[:, :, :rows].reshape(model, rows),
        jnp.concatenate([zero, zero, zero, act_ref[...]], axis=0),
        OVER,
        preferred_element_type=f32,
    )
    grads_ref[...] = grads.astype(bf16).reshape(grads_ref.shape)
    kernel = jnp.transpose(kernel_ref[...])[: grads_ref.shape[2]].astype(bf16)
    for zl in range(8):
        for y in range(4):
            grads_ref[zl, y, :, :width] = kernel
    for step, out in zip((0, 1, 3, 2), (part0_out, part1_out, part2_out, part3_out)):
        out[...] = grads_ref[:, lax.rem(where_ref[2] + step, 4)]
    for started in finished:
        started.wait()


def on_device(
    inputs,
    norm_gain,
    norm_bias,
    value_weight,
    gate_weight,
    conv_kernel,
    project_weight,
    frame_mask,
    upstream,
):
    width, rows = inputs.shape
    model = value_weight.shape[1]
    taps = conv_kernel.shape[0]
    lanes = rows + 128
    piece = model // 32
    zh = lax.axis_index("zh")
    core = lax.axis_index("core")
    y = lax.axis_index("y")
    zl = lax.axis_index("zl")
    offset = lax.axis_index(CHAN) * width
    where = jnp.stack([zh, core, y]).astype(jnp.int32)

    to_right, to_left = call(
        edges,
        (shape((width + 16, 128), bf16), shape((width + 16, 128), bf16)),
        scratch=(pltpu.VMEM((2, 2, width, 128), bf16), pltpu.SemaphoreType.DMA((4,))),
        specs=[pl.BlockSpec(memory_space=pltpu.HBM)] * 2 + [VMEM],
    )(
        pltpu.with_memory_space_constraint(inputs, pltpu.HBM),
        pltpu.with_memory_space_constraint(upstream, pltpu.HBM),
        frame_mask.reshape(1, rows),
    )
    edge = lax.ppermute(to_right, FRAME, [(i, i + 1) for i in range(31)]) + lax.ppermute(
        to_left, FRAME, [(i + 1, i) for i in range(31)]
    )

    weights = jnp.concatenate([value_weight, gate_weight])
    by_gain = jnp.sum(weights.astype(f32) * norm_gain[None, :], axis=1, keepdims=True)
    by_bias = jnp.sum(weights.astype(f32) * norm_bias[None, :], axis=1, keepdims=True)
    gain_local = lax.dynamic_slice_in_dim(norm_gain, offset, width, 0)[:, None]

    def columns_of(parameter):
        parameter = parameter.reshape(4, 2, 2, width)
        parameter = jnp.where(zh == 0, parameter, parameter[:, ::-1])
        parameter = jnp.where(core == 0, parameter, parameter[:, :, ::-1])
        return parameter.reshape(16, width).T

    small = jnp.concatenate([columns_of(norm_gain), columns_of(norm_bias)], axis=1)
    small = jnp.concatenate(
        [
            jnp.pad(small, ((0, width), (0, 0))),
            by_gain,
            by_bias,
            jnp.pad(conv_kernel.T, ((0, width), (0, 128 - 34 - taps))),
        ],
        axis=1,
    )
    early = (weights, weights.T, small, gain_local, where)

    held = jnp.concatenate([inputs, edge[:width], upstream], axis=1)
    keep = jnp.concatenate([frame_mask.astype(f32)[None, :], edge[width : width + 1].astype(f32)], axis=1)
    came = swap(held, "zh")
    came, keep, early = lax.optimization_barrier((came, keep, early))
    weights, flipped, small, gain_local, where = early
    far_inputs = came[:, :rows]
    own = over_x(jnp.stack([held, came]))
    other = swap(own, "core")
    piece_shape = (8, piece, 4 * width)
    operands = (own, other, small, weights, project_weight, flipped, keep)
    mixed, *pieces, stats = pl.pallas_call(
        middle,
        out_shape=(
            pltpu.HBM((8, 2 * width + 16, rows), bf16),
            *(pltpu.VMEM(piece_shape, bf16) for _ in range(4)),
            pltpu.HBM((8, lanes), f32),
        ),
        in_specs=[SMEM] + [pl.BlockSpec(memory_space=pltpu.HBM)] * len(operands),
        out_specs=tuple(pl.BlockSpec(memory_space=pltpu.HBM if i in (0, 5) else pltpu.VMEM) for i in range(6)),
        scratch_shapes=[pltpu.VMEM(operand.shape, operand.dtype) for operand in operands]
        + [
            pltpu.VMEM((taps, width, 128), f32),
            pltpu.VMEM((8, 2 * width + 16, rows), bf16),
            pltpu.VMEM((8, 4, piece, 4 * width), bf16),
            pltpu.VMEM((8, lanes), f32),
            pltpu.VMEM((16, width, lanes), bf16),
            pltpu.VMEM((16, width, lanes), bf16),
            pltpu.VMEM((2 * width, rows), bf16),
            pltpu.VMEM((width, rows), bf16),
            pltpu.VMEM((width, 128), f32),
            pltpu.VMEM((2 * width, lanes), f32),
            pltpu.VMEM((width, lanes), f32),
            pltpu.VMEM((8, 16, lanes), f32),
            pltpu.VMEM((8, 16, lanes), f32),
            pltpu.SemaphoreType.DMA((20,)),
        ],
        compiler_params=pltpu.CompilerParams(vmem_limit_bytes=40 << 20),
    )(where, *(pltpu.with_memory_space_constraint(operand, pltpu.HBM) for operand in operands))

    mixed = lax.all_to_all(mixed, ("x", "core"), 0, 0, tiled=True)

    parts = [
        lax.ppermute(sent, "y", [(i, (i + step) % 4) for i in range(4)])
        for step, sent in zip((1, 3, 2), pieces[1:])
    ]
    mixed = jnp.sum(mixed.astype(f32), axis=0)
    near = mixed[width : 2 * width]
    inv_std = stats[1:2, :rows]
    centred = (inputs.astype(f32) - stats[0:1, :rows]) * inv_std
    centred_far = (far_inputs.astype(f32) - stats[0:1, :rows]) * inv_std
    near_tail = jnp.stack([jnp.sum(near * centred, axis=1), jnp.sum(near, axis=1)])
    far_tail = jnp.stack([jnp.sum(mixed[:width] * centred_far, axis=1), jnp.sum(mixed[:width], axis=1)])
    tail, near = lax.optimization_barrier((ordered(near_tail, far_tail, zh, 0), near))
    far_sums = mixed[2 * width : 2 * width + 2] + mixed[2 * width + 2 : 2 * width + 4]
    sent_high, sent_low = split_bf16(far_sums)
    far = jnp.concatenate(
        [mixed[:width].astype(bf16), sent_high, sent_low, jnp.zeros((12, rows), bf16)]
    )
    came = swap(far, "zh").astype(f32)

    tail = lax.all_to_all(
        jnp.broadcast_to(tail[None], (32, 2, 2, width)).reshape(64, 2, width),
        FRAME + ("zh",), 0, 0, tiled=True,
    )

    total, far_copy = lax.optimization_barrier((pieces[0], far))
    total = total.astype(f32)
    for part in parts:
        total = total + part.astype(f32)

    def block(index):
        return lax.dynamic_slice_in_dim(total, index, 1, 0)[0]

    side = zl % 2
    total = total.reshape(4, 2, piece, 4 * width)
    sent = lax.dynamic_slice_in_dim(total, 1 - side, 1, 1)[:, 0].astype(bf16)
    total = lax.dynamic_slice_in_dim(total, side, 1, 1)[:, 0]
    total = total + lax.ppermute(sent, "zl", [(i, i ^ 1) for i in range(8)]).astype(f32)

    normed_grad = near + came[:width]
    kept = far_copy[width : width + 4].astype(f32)
    sums = (kept[:2] + kept[2:] + came[width : width + 2] + came[width + 2 : width + 4]) / model
    total, normed_grad = lax.optimization_barrier((total, normed_grad))
    inputs_grad = (
        upstream.astype(f32)
        + inv_std * (normed_grad * gain_local - sums[0:1] - centred * sums[1:2])
    ).astype(bf16)

    grads = block(zl // 2)
    for step in (3, 2, 1):
        sent = block((zl // 2) ^ step).astype(bf16)
        grads = grads + lax.ppermute(sent, "zl", [(i, i ^ (2 * step)) for i in range(8)]).astype(f32)
    tail, grads = lax.optimization_barrier((tail, grads))
    tail = jnp.sum(tail, axis=0)
    kernel_grad = grads[:taps, :width]
    value_grad = grads[:, width : 2 * width].T
    gate_grad = grads[:, 2 * width : 3 * width].T
    project_grad = grads[:, 3 * width :].T
    return (inputs_grad, value_grad, gate_grad, project_grad, kernel_grad, tail[0], tail[1])


def solution(mesh):
    split = Mesh(mesh.devices.reshape(8, 4, 4, 2, 2), FRAME + CHAN)
    return jax.shard_map(
        on_device,
        mesh=split,
        in_specs=(
            P(CHAN, FRAME),
            P(),
            P(),
            P(CHAN, None),
            P(CHAN, None),
            P(None, CHAN),
            P(CHAN, None),
            P(FRAME),
            P(CHAN, FRAME),
        ),
        out_specs=(
            P(CHAN, FRAME),
            P(CHAN, FRAME),
            P(CHAN, FRAME),
            P(CHAN, FRAME),
            P(None, CHAN),
            P(CHAN),
            P(CHAN),
        ),
        check_vma=False,
    )
```

```python
import jax
import jax.numpy as jnp
from jax import lax
from jax.experimental import pallas as pl
from jax.experimental.pallas import tpu as pltpu
from jax.sharding import Mesh, PartitionSpec as P

eps = 1e-05
CHAN = ("x", "zh", "core")
FRAME = ("zl", "y")
SWAP = [(0, 1), (1, 0)]
f32 = jnp.float32
bf16 = jnp.bfloat16
VMEM = pl.BlockSpec(memory_space=pltpu.VMEM)
SMEM = pl.BlockSpec(memory_space=pltpu.SMEM)
OVER = (((1,), (1,)), ((), ()))


def swap(value, axis):
    return lax.ppermute(value, axis, SWAP)


def over_x(pair):
    return lax.all_to_all(
        jnp.broadcast_to(pair[None], (4,) + pair.shape), "x", 0, 0, tiled=True
    )


def ordered(own, other, index, axis):
    return jnp.where(
        index == 0, jnp.stack([own, other], axis), jnp.stack([other, own], axis)
    )


def split_bf16(value):
    high = value.astype(bf16)
    return high, (value - high.astype(f32)).astype(bf16)


def shape(dims, dtype):
    return jax.ShapeDtypeStruct(dims, dtype)


def call(kernel, outs, scratch=(), specs=None):
    return pl.pallas_call(
        kernel,
        out_shape=outs,
        in_specs=specs,
        out_specs=tuple(VMEM for _ in outs),
        scratch_shapes=list(scratch),
        compiler_params=pltpu.CompilerParams(vmem_limit_bytes=24 << 20),
    )


def blocks_of(where_ref, own_ref, other_ref):
    zh, core = where_ref[0], where_ref[1]
    for x in range(4):
        for far in range(2):
            side = zh if far == 0 else 1 - zh
            yield x * 4 + side * 2 + core, own_ref.at[x, far]
            yield x * 4 + side * 2 + 1 - core, other_ref.at[x, far]


def edges(inputs_hbm, upstream_hbm, mask_ref, right_ref, left_ref, ends_ref, sems):
    width, rows = inputs_hbm.shape
    starts = (rows - 128, 0)
    copies = []
    for i, start in enumerate(starts):
        for j, source in enumerate((inputs_hbm, upstream_hbm)):
            copies.append(
                pltpu.make_async_copy(
                    source.at[:, start : start + 128], ends_ref.at[i, j], sems.at[2 * i + j]
                )
            )
            copies[-1].start()
    for started in copies:
        started.wait()
    lane = lax.broadcasted_iota(jnp.int32, (width, 128), 1)
    low = lax.broadcasted_iota(jnp.int32, (16, 128), 1)

    def pack(i, own, moved, ref):
        up = pltpu.roll(ends_ref[i, 1].astype(f32), 64, 1)
        ref[:width] = jnp.where(
            own(lane), ends_ref[i, 0].astype(f32), jnp.where(moved(lane), up, 0.0)
        ).astype(bf16)
        mask = mask_ref[:, starts[i] : starts[i] + 128].astype(f32)
        ref[width:] = jnp.where(own(low), jnp.broadcast_to(mask, (16, 128)), 0.0).astype(bf16)

    pack(0, lambda i: i >= 98, lambda i: (i >= 49) & (i < 64), right_ref)
    pack(1, lambda i: i < 30, lambda i: (i >= 64) & (i < 79), left_ref)


def middle(
    where_ref, own_hbm, other_hbm, small_hbm, weight_hbm, project_hbm, flipped_hbm, mask_hbm,
    mixed_out, part0_out, part1_out, part2_out, part3_out, stats_out,
    own_ref, other_ref, small_ref, weight_ref, project_ref, flipped_ref, mask_ref,
    taps_ref, mixed_ref, grads_ref, stats_ref, normed_ref, full_ref, both_ref, act_ref, kernel_ref,
    proj_ref, grad_ref, moved_ref, back_ref, sems,
):
    model = weight_ref.shape[1]
    width = own_ref.shape[2]
    lanes = normed_ref.shape[2]
    rows = mixed_ref.shape[2]
    taps = taps_ref.shape[0]
    count = 0

    def copy(source, target):
        nonlocal count
        started = pltpu.make_async_copy(source, target, sems.at[count])
        started.start()
        count += 1
        return started

    small_copy = copy(small_hbm, small_ref)
    blocks = [
        copy(source.at[x], target.at[x])
        for x in range(4)
        for source, target in ((own_hbm, own_ref), (other_hbm, other_ref))
    ]
    mask_copy = copy(mask_hbm, mask_ref)
    project_copy = copy(project_hbm, project_ref)
    weight_copy = copy(weight_hbm, weight_ref)
    flipped_copy = copy(flipped_hbm, flipped_ref)
    small_copy.wait()
    for k in range(taps):
        taps_ref[k] = jnp.broadcast_to(small_ref[:width, 34 + k : 35 + k], (width, 128))
    total = jnp.zeros((8, lanes), f32)
    square = jnp.zeros((8, lanes), f32)
    for i, (place, block) in enumerate(blocks_of(where_ref, own_ref, other_ref)):
        if i % 4 == 0:
            blocks[i // 2].wait()
            blocks[i // 2 + 1].wait()
        x = block[:, :lanes].astype(f32).reshape(width // 8, 8, lanes)
        total = total + jnp.sum(x, axis=0)
        square = square + jnp.sum(x * x, axis=0)
        full_ref[place, :, :rows] = block[:, lanes:]
        full_ref[place, :, rows:] = pltpu.roll(
            block[:, rows:lanes].astype(f32), 64, 1
        ).astype(bf16)
    row_mean = jnp.sum(total, axis=0, keepdims=True) / model
    row_var = jnp.sum(square, axis=0, keepdims=True) / model - row_mean * row_mean
    inv_std = lax.rsqrt(row_var + eps)
    stats_ref[...] = jnp.concatenate(
        [row_mean, inv_std, jnp.zeros((6, lanes), f32)], axis=0
    )
    finished = [copy(stats_ref, stats_out)]
    for i, (place, block) in enumerate(blocks_of(where_ref, own_ref, other_ref)):
        centred = (block[:, :lanes].astype(f32) - row_mean) * inv_std
        normed_ref[place] = (
            centred * small_ref[:width, i : i + 1] + small_ref[:width, 16 + i : 17 + i]
        ).astype(bf16)
    project_copy.wait()
    grad_ref[...] = jnp.dot(
        project_ref[...], full_ref[...].reshape(model, lanes), preferred_element_type=f32
    )
    weight_copy.wait()
    proj_ref[...] = jnp.dot(
        weight_ref[...], normed_ref[...].reshape(model, lanes), preferred_element_type=f32
    )
    mask_copy.wait()
    group = 16
    lane = lax.broadcasted_iota(jnp.int32, (group, 128), 1)
    inside = lax.broadcasted_iota(jnp.int32, (group, lanes), 1) < rows

    def channels(step, carry):
        first = pl.multiple_of(step * group, group)
        mine = pl.ds(first, group)
        after = pl.ds(pl.multiple_of(width + first, group), group)
        value = proj_ref[mine, :]
        gate = jax.nn.sigmoid(proj_ref[after, :])
        keep = mask_ref[...]
        glu = (value * gate * keep).astype(bf16).astype(f32)

        def shifted(x, by):
            return pltpu.roll(x, by % lanes, 1) if by % lanes else x

        def tap(k):
            return jnp.concatenate([taps_ref[k, mine, :]] * (lanes // 128), axis=1)

        def spread(fine, sign):
            result = None
            for a in range(4):
                part = None
                for b in range(8):
                    if 8 * a + b < taps:
                        term = tap(8 * a + b) * fine[b]
                        part = term if part is None else part + term
                part = shifted(part, sign * (8 * a - 8))
                result = part if result is None else result + part
            return result

        for b in range(8):
            moved_ref[b] = shifted(glu, 7 - b)
        conv = spread(moved_ref, -1)
        sig = jax.nn.sigmoid(conv)
        act_ref[mine, :] = (conv * sig)[:, :rows].astype(bf16)
        act_grad = grad_ref[mine, :].astype(bf16).astype(f32)
        grad = (act_grad * (sig + conv * sig * (1.0 - sig))).astype(bf16).astype(f32)
        for b in range(8):
            back_ref[b] = shifted(grad, b - 7)
        glu_grad = spread(back_ref, 1)[:, :rows]
        inner = jnp.where(inside, grad, 0.0)
        kernel = jnp.zeros((group, 128), f32)
        for a in range(4):
            here = shifted(inner, 8 * a - 8)
            for b in range(8):
                if 8 * a + b < taps:
                    seen = jnp.sum(here * moved_ref[b], axis=1, keepdims=True)
                    kernel = jnp.where(lane == 8 * a + b, seen, kernel)
        kernel_ref[mine, :] = kernel
        glu_grad = glu_grad * keep[:, :rows]
        gate = gate[:, :rows]
        both_ref[mine, :] = (glu_grad * gate).astype(bf16)
        both_ref[after, :] = (glu_grad * value[:, :rows] * gate * (1.0 - gate)).astype(bf16)
        return carry

    lax.fori_loop(0, width // group, channels, 0)
    both = both_ref[...]
    flipped_copy.wait()
    partial = jnp.dot(flipped_ref[...], both, preferred_element_type=f32).astype(bf16)
    partial = partial.reshape(4, 2, 2, width, rows)
    both = both.astype(f32)
    first = jnp.sum(both * small_ref[:, 32:33], axis=0, keepdims=True)
    second = jnp.sum(both * (proj_ref[:, :rows] - small_ref[:, 33:34]), axis=0, keepdims=True)
    first_high = first.astype(bf16).astype(f32)
    second_high = second.astype(bf16).astype(f32)
    row = lax.broadcasted_iota(jnp.int32, (16, rows), 0)
    extra = jnp.where(row == 0, first_high, 0.0)
    extra = jnp.where(row == 1, second_high, extra)
    extra = jnp.where(row == 2, first - first_high, extra)
    extra = jnp.where(row == 3, second - second_high, extra).astype(bf16)
    zh = where_ref[0]
    for x in range(4):
        for core in range(2):
            for side in range(2):
                start = pl.multiple_of(jnp.where(side == zh, width, 0), width)
                mixed_ref[x * 2 + core, pl.ds(start, width)] = partial[x, side, core]
            mixed_ref[x * 2 + core, 2 * width :] = extra
    finished.append(copy(mixed_ref, mixed_out))

    zero = jnp.zeros((width, rows), bf16)
    grads = lax.dot_general(
        normed_ref[:, :, :rows].reshape(model, rows),
        jnp.concatenate([zero, both_ref[...], zero], axis=0),
        OVER,
        preferred_element_type=f32,
    ) + lax.dot_general(
        full_ref[:, :, :rows].reshape(model, rows),
        jnp.concatenate([zero, zero, zero, act_ref[...]], axis=0),
        OVER,
        preferred_element_type=f32,
    )
    grads_ref[...] = grads.astype(bf16).reshape(grads_ref.shape)
    kernel = jnp.transpose(kernel_ref[...])[: grads_ref.shape[2]].astype(bf16)
    for zl in range(8):
        for y in range(4):
            grads_ref[zl, y, :, :width] = kernel
    for step, out in zip((0, 1, 3, 2), (part0_out, part1_out, part2_out, part3_out)):
        out[...] = grads_ref[:, lax.rem(where_ref[2] + step, 4)]
    for started in finished:
        started.wait()


def on_device(
    inputs,
    norm_gain,
    norm_bias,
    value_weight,
    gate_weight,
    conv_kernel,
    project_weight,
    frame_mask,
    upstream,
):
    width, rows = inputs.shape
    model = value_weight.shape[1]
    taps = conv_kernel.shape[0]
    lanes = rows + 128
    piece = model // 32
    zh = lax.axis_index("zh")
    core = lax.axis_index("core")
    y = lax.axis_index("y")
    zl = lax.axis_index("zl")
    offset = lax.axis_index(CHAN) * width
    where = jnp.stack([zh, core, y]).astype(jnp.int32)

    to_right, to_left = call(
        edges,
        (shape((width + 16, 128), bf16), shape((width + 16, 128), bf16)),
        scratch=(pltpu.VMEM((2, 2, width, 128), bf16), pltpu.SemaphoreType.DMA((4,))),
        specs=[pl.BlockSpec(memory_space=pltpu.HBM)] * 2 + [VMEM],
    )(
        pltpu.with_memory_space_constraint(inputs, pltpu.HBM),
        pltpu.with_memory_space_constraint(upstream, pltpu.HBM),
        frame_mask.reshape(1, rows),
    )
    edge = lax.ppermute(to_right, FRAME, [(i, i + 1) for i in range(31)]) + lax.ppermute(
        to_left, FRAME, [(i + 1, i) for i in range(31)]
    )

    weights = jnp.concatenate([value_weight, gate_weight])
    by_gain = jnp.sum(weights.astype(f32) * norm_gain[None, :], axis=1, keepdims=True)
    by_bias = jnp.sum(weights.astype(f32) * norm_bias[None, :], axis=1, keepdims=True)
    gain_local = lax.dynamic_slice_in_dim(norm_gain, offset, width, 0)[:, None]

    def columns_of(parameter):
        parameter = parameter.reshape(4, 2, 2, width)
        parameter = jnp.where(zh == 0, parameter, parameter[:, ::-1])
        parameter = jnp.where(core == 0, parameter, parameter[:, :, ::-1])
        return parameter.reshape(16, width).T

    small = jnp.concatenate([columns_of(norm_gain), columns_of(norm_bias)], axis=1)
    small = jnp.concatenate(
        [
            jnp.pad(small, ((0, width), (0, 0))),
            by_gain,
            by_bias,
            jnp.pad(conv_kernel.T, ((0, width), (0, 128 - 34 - taps))),
        ],
        axis=1,
    )
    early = (weights, weights.T, small, gain_local, where)

    held = jnp.concatenate([inputs, edge[:width], upstream], axis=1)
    keep = jnp.concatenate([frame_mask.astype(f32)[None, :], edge[width : width + 1].astype(f32)], axis=1)
    came = swap(held, "zh")
    came, keep, early = lax.optimization_barrier((came, keep, early))
    weights, flipped, small, gain_local, where = early
    far_inputs = came[:, :rows]
    own = over_x(jnp.stack([held, came]))
    other = swap(own, "core")
    piece_shape = (8, piece, 4 * width)
    operands = (own, other, small, weights, project_weight, flipped, keep)
    mixed, *pieces, stats = pl.pallas_call(
        middle,
        out_shape=(
            pltpu.HBM((8, 2 * width + 16, rows), bf16),
            *(pltpu.VMEM(piece_shape, bf16) for _ in range(4)),
            pltpu.HBM((8, lanes), f32),
        ),
        in_specs=[SMEM] + [pl.BlockSpec(memory_space=pltpu.HBM)] * len(operands),
        out_specs=tuple(pl.BlockSpec(memory_space=pltpu.HBM if i in (0, 5) else pltpu.VMEM) for i in range(6)),
        scratch_shapes=[pltpu.VMEM(operand.shape, operand.dtype) for operand in operands]
        + [
            pltpu.VMEM((taps, width, 128), f32),
            pltpu.VMEM((8, 2 * width + 16, rows), bf16),
            pltpu.VMEM((8, 4, piece, 4 * width), bf16),
            pltpu.VMEM((8, lanes), f32),
            pltpu.VMEM((16, width, lanes), bf16),
            pltpu.VMEM((16, width, lanes), bf16),
            pltpu.VMEM((2 * width, rows), bf16),
            pltpu.VMEM((width, rows), bf16),
            pltpu.VMEM((width, 128), f32),
            pltpu.VMEM((2 * width, lanes), f32),
            pltpu.VMEM((width, lanes), f32),
            pltpu.VMEM((8, 16, lanes), f32),
            pltpu.VMEM((8, 16, lanes), f32),
            pltpu.SemaphoreType.DMA((20,)),
        ],
        compiler_params=pltpu.CompilerParams(vmem_limit_bytes=40 << 20),
    )(where, *(pltpu.with_memory_space_constraint(operand, pltpu.HBM) for operand in operands))

    mixed = lax.all_to_all(mixed, ("x", "core"), 0, 0, tiled=True)

    parts = [
        lax.ppermute(sent, "y", [(i, (i + step) % 4) for i in range(4)])
        for step, sent in zip((1, 3, 2), pieces[1:])
    ]
    total = pieces[0].astype(f32)
    for part in parts:
        total = total + part.astype(f32)

    side = zl % 2
    total = total.reshape(4, 2, piece, 4 * width)
    sent = lax.dynamic_slice_in_dim(total, 1 - side, 1, 1)[:, 0].astype(bf16)
    total = lax.dynamic_slice_in_dim(total, side, 1, 1)[:, 0]
    sent, mixed = lax.optimization_barrier((sent, mixed))
    total = total + lax.ppermute(sent, "zl", [(i, i ^ 1) for i in range(8)]).astype(f32)

    mixed = jnp.sum(mixed.astype(f32), axis=0)
    near = mixed[width : 2 * width]
    inv_std = stats[1:2, :rows]
    centred = (inputs.astype(f32) - stats[0:1, :rows]) * inv_std
    centred_far = (far_inputs.astype(f32) - stats[0:1, :rows]) * inv_std
    near_tail = jnp.stack([jnp.sum(near * centred, axis=1), jnp.sum(near, axis=1)])
    far_tail = jnp.stack([jnp.sum(mixed[:width] * centred_far, axis=1), jnp.sum(mixed[:width], axis=1)])
    tail, near = lax.optimization_barrier((ordered(near_tail, far_tail, zh, 0), near))
    far_sums = mixed[2 * width : 2 * width + 2] + mixed[2 * width + 2 : 2 * width + 4]
    sent_high, sent_low = split_bf16(far_sums)
    far = jnp.concatenate(
        [mixed[:width].astype(bf16), sent_high, sent_low, jnp.zeros((12, rows), bf16)]
    )
    came = swap(far, "zh").astype(f32)

    tail = lax.all_to_all(
        jnp.broadcast_to(tail[None], (32, 2, 2, width)).reshape(64, 2, width),
        FRAME + ("zh",), 0, 0, tiled=True,
    )

    normed_grad = near + came[:width]
    kept = far[width : width + 4].astype(f32)
    sums = (kept[:2] + kept[2:] + came[width : width + 2] + came[width + 2 : width + 4]) / model
    total, normed_grad = lax.optimization_barrier((total, normed_grad))
    inputs_grad = (
        upstream.astype(f32)
        + inv_std * (normed_grad * gain_local - sums[0:1] - centred * sums[1:2])
    ).astype(bf16)

    for size in (2, 4):
        side = (zl // size) % 2
        total = total.reshape(4 // size, 2, piece, 4 * width)
        sent = lax.dynamic_slice_in_dim(total, 1 - side, 1, 1)[:, 0].astype(bf16)
        total = lax.dynamic_slice_in_dim(total, side, 1, 1)[:, 0]
        total = total + lax.ppermute(sent, "zl", [(i, i ^ size) for i in range(8)]).astype(f32)
    grads = total[0]
    tail, grads = lax.optimization_barrier((tail, grads))
    tail = jnp.sum(tail, axis=0)
    kernel_grad = grads[:taps, :width]
    value_grad = grads[:, width : 2 * width].T
    gate_grad = grads[:, 2 * width : 3 * width].T
    project_grad = grads[:, 3 * width :].T
    return (inputs_grad, value_grad, gate_grad, project_grad, kernel_grad, tail[0], tail[1])


def solution(mesh):
    split = Mesh(mesh.devices.reshape(8, 4, 4, 2, 2), FRAME + CHAN)
    return jax.shard_map(
        on_device,
        mesh=split,
        in_specs=(
            P(CHAN, FRAME),
            P(),
            P(),
            P(CHAN, None),
            P(CHAN, None),
            P(None, CHAN),
            P(CHAN, None),
            P(FRAME),
            P(CHAN, FRAME),
        ),
        out_specs=(
            P(CHAN, FRAME),
            P(CHAN, FRAME),
            P(CHAN, FRAME),
            P(CHAN, FRAME),
            P(None, CHAN),
            P(CHAN),
            P(CHAN),
        ),
        check_vma=False,
    )
```

```python
import jax
import jax.numpy as jnp
from jax import lax
from jax.experimental import pallas as pl
from jax.experimental.pallas import tpu as pltpu
from jax.sharding import Mesh, PartitionSpec as P

eps = 1e-05
CHAN = ("x", "zh", "core")
FRAME = ("zl", "y")
SWAP = [(0, 1), (1, 0)]
f32 = jnp.float32
bf16 = jnp.bfloat16
VMEM = pl.BlockSpec(memory_space=pltpu.VMEM)
SMEM = pl.BlockSpec(memory_space=pltpu.SMEM)
OVER = (((1,), (1,)), ((), ()))


def swap(value, axis):
    return lax.ppermute(value, axis, SWAP)


def over_x(pair):
    return lax.all_to_all(
        jnp.broadcast_to(pair[None], (4,) + pair.shape), "x", 0, 0, tiled=True
    )


def ordered(own, other, index, axis):
    return jnp.where(
        index == 0, jnp.stack([own, other], axis), jnp.stack([other, own], axis)
    )


def split_bf16(value):
    high = value.astype(bf16)
    return high, (value - high.astype(f32)).astype(bf16)


def shape(dims, dtype):
    return jax.ShapeDtypeStruct(dims, dtype)


def call(kernel, outs, scratch=(), specs=None):
    return pl.pallas_call(
        kernel,
        out_shape=outs,
        in_specs=specs,
        out_specs=tuple(VMEM for _ in outs),
        scratch_shapes=list(scratch),
        compiler_params=pltpu.CompilerParams(vmem_limit_bytes=24 << 20),
    )


def blocks_of(where_ref, own_ref, other_ref):
    zh, core = where_ref[0], where_ref[1]
    for x in range(4):
        for far in range(2):
            side = zh if far == 0 else 1 - zh
            yield x * 4 + side * 2 + core, own_ref.at[x, far]
            yield x * 4 + side * 2 + 1 - core, other_ref.at[x, far]


def edges(inputs_hbm, upstream_hbm, mask_ref, right_ref, left_ref, ends_ref, sems):
    width, rows = inputs_hbm.shape
    starts = (rows - 128, 0)
    copies = []
    for i, start in enumerate(starts):
        for j, source in enumerate((inputs_hbm, upstream_hbm)):
            copies.append(
                pltpu.make_async_copy(
                    source.at[:, start : start + 128], ends_ref.at[i, j], sems.at[2 * i + j]
                )
            )
            copies[-1].start()
    for started in copies:
        started.wait()
    lane = lax.broadcasted_iota(jnp.int32, (width, 128), 1)
    low = lax.broadcasted_iota(jnp.int32, (16, 128), 1)

    def pack(i, own, moved, ref):
        up = pltpu.roll(ends_ref[i, 1].astype(f32), 64, 1)
        ref[:width] = jnp.where(
            own(lane), ends_ref[i, 0].astype(f32), jnp.where(moved(lane), up, 0.0)
        ).astype(bf16)
        mask = mask_ref[:, starts[i] : starts[i] + 128].astype(f32)
        ref[width:] = jnp.where(own(low), jnp.broadcast_to(mask, (16, 128)), 0.0).astype(bf16)

    pack(0, lambda i: i >= 98, lambda i: (i >= 49) & (i < 64), right_ref)
    pack(1, lambda i: i < 30, lambda i: (i >= 64) & (i < 79), left_ref)


def middle(
    where_ref, own_hbm, other_hbm, small_hbm, weight_hbm, project_hbm, flipped_hbm, mask_hbm,
    mixed_out, part0_out, part1_out, part2_out, part3_out, stats_out,
    own_ref, other_ref, small_ref, weight_ref, project_ref, flipped_ref, mask_ref,
    taps_ref, mixed_ref, grads_ref, stats_ref, normed_ref, full_ref, both_ref, act_ref, kernel_ref,
    proj_ref, grad_ref, moved_ref, back_ref, sems,
):
    model = weight_ref.shape[1]
    width = own_ref.shape[2]
    lanes = normed_ref.shape[2]
    rows = mixed_ref.shape[2]
    taps = taps_ref.shape[0]
    count = 0

    def copy(source, target):
        nonlocal count
        started = pltpu.make_async_copy(source, target, sems.at[count])
        started.start()
        count += 1
        return started

    small_copy = copy(small_hbm, small_ref)
    blocks = [
        copy(source.at[x], target.at[x])
        for x in range(4)
        for source, target in ((own_hbm, own_ref), (other_hbm, other_ref))
    ]
    mask_copy = copy(mask_hbm, mask_ref)
    project_copy = copy(project_hbm, project_ref)
    weight_copy = copy(weight_hbm, weight_ref)
    flipped_copy = copy(flipped_hbm, flipped_ref)
    small_copy.wait()
    for k in range(taps):
        taps_ref[k] = jnp.broadcast_to(small_ref[:width, 34 + k : 35 + k], (width, 128))
    total = jnp.zeros((8, lanes), f32)
    square = jnp.zeros((8, lanes), f32)
    for i, (place, block) in enumerate(blocks_of(where_ref, own_ref, other_ref)):
        if i % 4 == 0:
            blocks[i // 2].wait()
            blocks[i // 2 + 1].wait()
        x = block[:, :lanes].astype(f32).reshape(width // 8, 8, lanes)
        total = total + jnp.sum(x, axis=0)
        square = square + jnp.sum(x * x, axis=0)
        full_ref[place, :, :rows] = block[:, lanes:]
        full_ref[place, :, rows:] = pltpu.roll(
            block[:, rows:lanes].astype(f32), 64, 1
        ).astype(bf16)
    row_mean = jnp.sum(total, axis=0, keepdims=True) / model
    row_var = jnp.sum(square, axis=0, keepdims=True) / model - row_mean * row_mean
    inv_std = lax.rsqrt(row_var + eps)
    stats_ref[...] = jnp.concatenate(
        [row_mean, inv_std, jnp.zeros((6, lanes), f32)], axis=0
    )
    finished = [copy(stats_ref, stats_out)]
    for i, (place, block) in enumerate(blocks_of(where_ref, own_ref, other_ref)):
        centred = (block[:, :lanes].astype(f32) - row_mean) * inv_std
        normed_ref[place] = (
            centred * small_ref[:width, i : i + 1] + small_ref[:width, 16 + i : 17 + i]
        ).astype(bf16)
    project_copy.wait()
    grad_ref[...] = jnp.dot(
        project_ref[...], full_ref[...].reshape(model, lanes), preferred_element_type=f32
    )
    weight_copy.wait()
    proj_ref[...] = jnp.dot(
        weight_ref[...], normed_ref[...].reshape(model, lanes), preferred_element_type=f32
    )
    mask_copy.wait()
    group = 16
    lane = lax.broadcasted_iota(jnp.int32, (group, 128), 1)
    inside = lax.broadcasted_iota(jnp.int32, (group, lanes), 1) < rows

    def channels(step, carry):
        first = pl.multiple_of(step * group, group)
        mine = pl.ds(first, group)
        after = pl.ds(pl.multiple_of(width + first, group), group)
        value = proj_ref[mine, :]
        gate = jax.nn.sigmoid(proj_ref[after, :])
        keep = mask_ref[...]
        glu = (value * gate * keep).astype(bf16).astype(f32)

        def shifted(x, by):
            return pltpu.roll(x, by % lanes, 1) if by % lanes else x

        def tap(k):
            return jnp.concatenate([taps_ref[k, mine, :]] * (lanes // 128), axis=1)

        def spread(fine, sign):
            result = None
            for a in range(4):
                part = None
                for b in range(8):
                    if 8 * a + b < taps:
                        term = tap(8 * a + b) * fine[b]
                        part = term if part is None else part + term
                part = shifted(part, sign * (8 * a - 8))
                result = part if result is None else result + part
            return result

        for b in range(8):
            moved_ref[b] = shifted(glu, 7 - b)
        conv = spread(moved_ref, -1)
        sig = jax.nn.sigmoid(conv)
        act_ref[mine, :] = (conv * sig)[:, :rows].astype(bf16)
        act_grad = grad_ref[mine, :].astype(bf16).astype(f32)
        grad = (act_grad * (sig + conv * sig * (1.0 - sig))).astype(bf16).astype(f32)
        for b in range(8):
            back_ref[b] = shifted(grad, b - 7)
        glu_grad = spread(back_ref, 1)[:, :rows]
        inner = jnp.where(inside, grad, 0.0)
        kernel = jnp.zeros((group, 128), f32)
        for a in range(4):
            here = shifted(inner, 8 * a - 8)
            for b in range(8):
                if 8 * a + b < taps:
                    seen = jnp.sum(here * moved_ref[b], axis=1, keepdims=True)
                    kernel = jnp.where(lane == 8 * a + b, seen, kernel)
        kernel_ref[mine, :] = kernel
        glu_grad = glu_grad * keep[:, :rows]
        gate = gate[:, :rows]
        both_ref[mine, :] = (glu_grad * gate).astype(bf16)
        both_ref[after, :] = (glu_grad * value[:, :rows] * gate * (1.0 - gate)).astype(bf16)
        return carry

    lax.fori_loop(0, width // group, channels, 0)
    both = both_ref[...]
    flipped_copy.wait()
    partial = jnp.dot(flipped_ref[...], both, preferred_element_type=f32).astype(bf16)
    partial = partial.reshape(4, 2, 2, width, rows)
    both = both.astype(f32)
    first = jnp.sum(both * small_ref[:, 32:33], axis=0, keepdims=True)
    second = jnp.sum(both * (proj_ref[:, :rows] - small_ref[:, 33:34]), axis=0, keepdims=True)
    first_high = first.astype(bf16).astype(f32)
    second_high = second.astype(bf16).astype(f32)
    row = lax.broadcasted_iota(jnp.int32, (16, rows), 0)
    extra = jnp.where(row == 0, first_high, 0.0)
    extra = jnp.where(row == 1, second_high, extra)
    extra = jnp.where(row == 2, first - first_high, extra)
    extra = jnp.where(row == 3, second - second_high, extra).astype(bf16)
    zh = where_ref[0]
    for x in range(4):
        for core in range(2):
            for side in range(2):
                start = pl.multiple_of(jnp.where(side == zh, width, 0), width)
                mixed_ref[x * 2 + core, pl.ds(start, width)] = partial[x, side, core]
            mixed_ref[x * 2 + core, 2 * width :] = extra
    finished.append(copy(mixed_ref, mixed_out))

    zero = jnp.zeros((width, rows), bf16)
    grads = lax.dot_general(
        normed_ref[:, :, :rows].reshape(model, rows),
        jnp.concatenate([zero, both_ref[...], zero], axis=0),
        OVER,
        preferred_element_type=f32,
    ) + lax.dot_general(
        full_ref[:, :, :rows].reshape(model, rows),
        jnp.concatenate([zero, zero, zero, act_ref[...]], axis=0),
        OVER,
        preferred_element_type=f32,
    )
    grads_ref[...] = grads.astype(bf16).reshape(grads_ref.shape)
    kernel = jnp.transpose(kernel_ref[...])[: grads_ref.shape[2]].astype(bf16)
    for zl in range(8):
        for y in range(4):
            grads_ref[zl, y, :, :width] = kernel
    for step, out in zip((0, 1, 3, 2), (part0_out, part1_out, part2_out, part3_out)):
        out[...] = grads_ref[:, lax.rem(where_ref[2] + step, 4)]
    for started in finished:
        started.wait()


def unpack(total_ref, part_ref, value_ref, gate_ref, project_ref, kernel_ref):
    taps, width = kernel_ref.shape
    total = total_ref[...] + part_ref[...].astype(f32)
    kernel_ref[...] = total[:taps, :width]
    turned = jnp.transpose(total)
    for i, ref in enumerate((value_ref, gate_ref, project_ref)):
        ref[...] = turned[(i + 1) * width : (i + 2) * width]


def on_device(
    inputs,
    norm_gain,
    norm_bias,
    value_weight,
    gate_weight,
    conv_kernel,
    project_weight,
    frame_mask,
    upstream,
):
    width, rows = inputs.shape
    model = value_weight.shape[1]
    taps = conv_kernel.shape[0]
    lanes = rows + 128
    piece = model // 32
    zh = lax.axis_index("zh")
    core = lax.axis_index("core")
    y = lax.axis_index("y")
    zl = lax.axis_index("zl")
    offset = lax.axis_index(CHAN) * width
    where = jnp.stack([zh, core, y]).astype(jnp.int32)

    to_right, to_left = call(
        edges,
        (shape((width + 16, 128), bf16), shape((width + 16, 128), bf16)),
        scratch=(pltpu.VMEM((2, 2, width, 128), bf16), pltpu.SemaphoreType.DMA((4,))),
        specs=[pl.BlockSpec(memory_space=pltpu.HBM)] * 2 + [VMEM],
    )(
        pltpu.with_memory_space_constraint(inputs, pltpu.HBM),
        pltpu.with_memory_space_constraint(upstream, pltpu.HBM),
        frame_mask.reshape(1, rows),
    )
    edge = lax.ppermute(to_right, FRAME, [(i, i + 1) for i in range(31)]) + lax.ppermute(
        to_left, FRAME, [(i + 1, i) for i in range(31)]
    )

    weights = jnp.concatenate([value_weight, gate_weight])
    by_gain = jnp.sum(weights.astype(f32) * norm_gain[None, :], axis=1, keepdims=True)
    by_bias = jnp.sum(weights.astype(f32) * norm_bias[None, :], axis=1, keepdims=True)
    gain_local = lax.dynamic_slice_in_dim(norm_gain, offset, width, 0)[:, None]

    def columns_of(parameter):
        parameter = parameter.reshape(4, 2, 2, width)
        parameter = jnp.where(zh == 0, parameter, parameter[:, ::-1])
        parameter = jnp.where(core == 0, parameter, parameter[:, :, ::-1])
        return parameter.reshape(16, width).T

    small = jnp.concatenate([columns_of(norm_gain), columns_of(norm_bias)], axis=1)
    small = jnp.concatenate(
        [
            jnp.pad(small, ((0, width), (0, 0))),
            by_gain,
            by_bias,
            jnp.pad(conv_kernel.T, ((0, width), (0, 128 - 34 - taps))),
        ],
        axis=1,
    )
    early = (weights, weights.T, small, gain_local, where)

    held = jnp.concatenate([inputs, edge[:width], upstream], axis=1)
    keep = jnp.concatenate([frame_mask.astype(f32)[None, :], edge[width : width + 1].astype(f32)], axis=1)
    came = swap(held, "zh")
    came, keep, early = lax.optimization_barrier((came, keep, early))
    weights, flipped, small, gain_local, where = early
    far_inputs = came[:, :rows]
    own = over_x(jnp.stack([held, came]))
    other = swap(own, "core")
    piece_shape = (8, piece, 4 * width)
    operands = (own, other, small, weights, project_weight, flipped, keep)
    mixed, *pieces, stats = pl.pallas_call(
        middle,
        out_shape=(
            pltpu.HBM((8, 2 * width + 16, rows), bf16),
            *(pltpu.VMEM(piece_shape, bf16) for _ in range(4)),
            pltpu.HBM((8, lanes), f32),
        ),
        in_specs=[SMEM] + [pl.BlockSpec(memory_space=pltpu.HBM)] * len(operands),
        out_specs=tuple(pl.BlockSpec(memory_space=pltpu.HBM if i in (0, 5) else pltpu.VMEM) for i in range(6)),
        scratch_shapes=[pltpu.VMEM(operand.shape, operand.dtype) for operand in operands]
        + [
            pltpu.VMEM((taps, width, 128), f32),
            pltpu.VMEM((8, 2 * width + 16, rows), bf16),
            pltpu.VMEM((8, 4, piece, 4 * width), bf16),
            pltpu.VMEM((8, lanes), f32),
            pltpu.VMEM((16, width, lanes), bf16),
            pltpu.VMEM((16, width, lanes), bf16),
            pltpu.VMEM((2 * width, rows), bf16),
            pltpu.VMEM((width, rows), bf16),
            pltpu.VMEM((width, 128), f32),
            pltpu.VMEM((2 * width, lanes), f32),
            pltpu.VMEM((width, lanes), f32),
            pltpu.VMEM((8, 16, lanes), f32),
            pltpu.VMEM((8, 16, lanes), f32),
            pltpu.SemaphoreType.DMA((20,)),
        ],
        compiler_params=pltpu.CompilerParams(vmem_limit_bytes=40 << 20),
    )(where, *(pltpu.with_memory_space_constraint(operand, pltpu.HBM) for operand in operands))

    mixed = lax.all_to_all(mixed, ("x", "core"), 0, 0, tiled=True)

    parts = [
        lax.ppermute(sent, "y", [(i, (i + step) % 4) for i in range(4)])
        for step, sent in zip((1, 3, 2), pieces[1:])
    ]
    total = pieces[0].astype(f32)
    for part in parts:
        total = total + part.astype(f32)

    side = zl % 2
    total = total.reshape(4, 2, piece, 4 * width)
    sent = lax.dynamic_slice_in_dim(total, 1 - side, 1, 1)[:, 0].astype(bf16)
    total = lax.dynamic_slice_in_dim(total, side, 1, 1)[:, 0]
    sent, mixed = lax.optimization_barrier((sent, mixed))
    total = total + lax.ppermute(sent, "zl", [(i, i ^ 1) for i in range(8)]).astype(f32)

    mixed = jnp.sum(mixed.astype(f32), axis=0)
    near = mixed[width : 2 * width]
    inv_std = stats[1:2, :rows]
    centred = (inputs.astype(f32) - stats[0:1, :rows]) * inv_std
    centred_far = (far_inputs.astype(f32) - stats[0:1, :rows]) * inv_std
    near_tail = jnp.stack([jnp.sum(near * centred, axis=1), jnp.sum(near, axis=1)])
    far_tail = jnp.stack([jnp.sum(mixed[:width] * centred_far, axis=1), jnp.sum(mixed[:width], axis=1)])
    tail, near = lax.optimization_barrier((ordered(near_tail, far_tail, zh, 0), near))
    far_sums = mixed[2 * width : 2 * width + 2] + mixed[2 * width + 2 : 2 * width + 4]
    sent_high, sent_low = split_bf16(far_sums)
    far = jnp.concatenate(
        [mixed[:width].astype(bf16), sent_high, sent_low, jnp.zeros((12, rows), bf16)]
    )
    tail = lax.all_to_all(
        jnp.broadcast_to(tail[None], (32, 2, 2, width)).reshape(64, 2, width),
        FRAME + ("zh",), 0, 0, tiled=True,
    )

    side = (zl // 2) % 2
    total = total.reshape(2, 2, piece, 4 * width)
    sent = lax.dynamic_slice_in_dim(total, 1 - side, 1, 1)[:, 0].astype(bf16)
    total = lax.dynamic_slice_in_dim(total, side, 1, 1)[:, 0]
    far, sent = lax.optimization_barrier((far, sent))
    total = total + lax.ppermute(sent, "zl", [(i, i ^ 2) for i in range(8)]).astype(f32)
    came = swap(far, "zh").astype(f32)

    normed_grad = near + came[:width]
    kept = far[width : width + 4].astype(f32)
    sums = (kept[:2] + kept[2:] + came[width : width + 2] + came[width + 2 : width + 4]) / model
    inputs_grad = (
        upstream.astype(f32)
        + inv_std * (normed_grad * gain_local - sums[0:1] - centred * sums[1:2])
    ).astype(bf16)

    side = zl // 4
    sent = lax.dynamic_slice_in_dim(total, 1 - side, 1, 0)[0].astype(bf16)
    total = lax.dynamic_slice_in_dim(total, side, 1, 0)[0]
    part = lax.ppermute(sent, "zl", [(i, i ^ 4) for i in range(8)])
    tail, part = lax.optimization_barrier((tail, part))
    value_grad, gate_grad, project_grad, kernel_grad = call(
        unpack,
        tuple(shape((width, piece), f32) for _ in range(3)) + (shape((taps, width), f32),),
        specs=[VMEM] * 2,
    )(total, part)
    tail = jnp.sum(tail, axis=0)
    return (inputs_grad, value_grad, gate_grad, project_grad, kernel_grad, tail[0], tail[1])


def solution(mesh):
    split = Mesh(mesh.devices.reshape(8, 4, 4, 2, 2), FRAME + CHAN)
    return jax.shard_map(
        on_device,
        mesh=split,
        in_specs=(
            P(CHAN, FRAME),
            P(),
            P(),
            P(CHAN, None),
            P(CHAN, None),
            P(None, CHAN),
            P(CHAN, None),
            P(FRAME),
            P(CHAN, FRAME),
        ),
        out_specs=(
            P(CHAN, FRAME),
            P(CHAN, FRAME),
            P(CHAN, FRAME),
            P(CHAN, FRAME),
            P(None, CHAN),
            P(CHAN),
            P(CHAN),
        ),
        check_vma=False,
    )
```

```python
import jax
import jax.numpy as jnp
from jax import lax
from jax.experimental import pallas as pl
from jax.experimental.pallas import tpu as pltpu
from jax.sharding import Mesh, PartitionSpec as P

eps = 1e-05
CHAN = ("x", "zh", "core")
FRAME = ("zl", "y")
SWAP = [(0, 1), (1, 0)]
f32 = jnp.float32
bf16 = jnp.bfloat16
VMEM = pl.BlockSpec(memory_space=pltpu.VMEM)
SMEM = pl.BlockSpec(memory_space=pltpu.SMEM)
OVER = (((1,), (1,)), ((), ()))


def swap(value, axis):
    return lax.ppermute(value, axis, SWAP)


def ordered(own, other, index, axis):
    return jnp.where(
        index == 0, jnp.stack([own, other], axis), jnp.stack([other, own], axis)
    )


def split_bf16(value):
    high = value.astype(bf16)
    return high, (value - high.astype(f32)).astype(bf16)


def shape(dims, dtype):
    return jax.ShapeDtypeStruct(dims, dtype)


def call(kernel, outs, scratch=(), specs=None):
    return pl.pallas_call(
        kernel,
        out_shape=outs,
        in_specs=specs,
        out_specs=tuple(VMEM for _ in outs),
        scratch_shapes=list(scratch),
        compiler_params=pltpu.CompilerParams(vmem_limit_bytes=24 << 20),
    )


STEPS = (0, 1, 3, 2)


def blocks_of(where_ref, own_refs, other_refs):
    zh, core, x = where_ref[0], where_ref[1], where_ref[3]
    for i, step in enumerate(STEPS):
        first = lax.rem(x + 4 - step, 4) * 4
        for far in range(2):
            side = zh if far == 0 else 1 - zh
            yield first + side * 2 + core, own_refs[i].at[far]
            yield first + side * 2 + 1 - core, other_refs[i].at[far]


def edges(inputs_hbm, upstream_hbm, mask_ref, right_ref, left_ref, ends_ref, sems):
    width, rows = inputs_hbm.shape
    starts = (rows - 128, 0)
    copies = []
    for i, start in enumerate(starts):
        for j, source in enumerate((inputs_hbm, upstream_hbm)):
            copies.append(
                pltpu.make_async_copy(
                    source.at[:, start : start + 128], ends_ref.at[i, j], sems.at[2 * i + j]
                )
            )
            copies[-1].start()
    for started in copies:
        started.wait()
    lane = lax.broadcasted_iota(jnp.int32, (width, 128), 1)
    low = lax.broadcasted_iota(jnp.int32, (16, 128), 1)

    def pack(i, own, moved, ref):
        up = pltpu.roll(ends_ref[i, 1].astype(f32), 64, 1)
        ref[:width] = jnp.where(
            own(lane), ends_ref[i, 0].astype(f32), jnp.where(moved(lane), up, 0.0)
        ).astype(bf16)
        mask = mask_ref[:, starts[i] : starts[i] + 128].astype(f32)
        ref[width:] = jnp.where(own(low), jnp.broadcast_to(mask, (16, 128)), 0.0).astype(bf16)

    pack(0, lambda i: i >= 98, lambda i: (i >= 49) & (i < 64), right_ref)
    pack(1, lambda i: i < 30, lambda i: (i >= 64) & (i < 79), left_ref)


def middle(
    where_ref, own0, own1, own2, own3, other0, other1, other2, other3, small_hbm, weight_hbm, project_hbm, flipped_hbm, mask_hbm,
    mixed_out, part0_out, part1_out, part2_out, part3_out, stats_out,
    small_ref, weight_ref, project_ref, flipped_ref, mask_ref,
    taps_ref, mixed_ref, grads_ref, stats_ref, normed_ref, full_ref, both_ref, act_ref, kernel_ref,
    proj_ref, grad_ref, moved_ref, back_ref, sems,
):
    model = weight_ref.shape[1]
    own_refs, other_refs = (own0, own1, own2, own3), (other0, other1, other2, other3)
    width = own0.shape[1]
    lanes = normed_ref.shape[2]
    rows = mixed_ref.shape[2]
    taps = taps_ref.shape[0]
    count = 0

    def copy(source, target):
        nonlocal count
        started = pltpu.make_async_copy(source, target, sems.at[count])
        started.start()
        count += 1
        return started

    small_copy = copy(small_hbm, small_ref)
    mask_copy = copy(mask_hbm, mask_ref)
    project_copy = copy(project_hbm, project_ref)
    weight_copy = copy(weight_hbm, weight_ref)
    flipped_copy = copy(flipped_hbm, flipped_ref)
    small_copy.wait()
    for k in range(taps):
        taps_ref[k] = jnp.broadcast_to(small_ref[:width, 34 + k : 35 + k], (width, 128))
    total = jnp.zeros((8, lanes), f32)
    square = jnp.zeros((8, lanes), f32)
    for place, block in blocks_of(where_ref, own_refs, other_refs):
        x = block[:, :lanes].astype(f32).reshape(width // 8, 8, lanes)
        total = total + jnp.sum(x, axis=0)
        square = square + jnp.sum(x * x, axis=0)
        full_ref[place, :, :rows] = block[:, lanes:]
        full_ref[place, :, rows:] = pltpu.roll(
            block[:, rows:lanes].astype(f32), 64, 1
        ).astype(bf16)
    row_mean = jnp.sum(total, axis=0, keepdims=True) / model
    row_var = jnp.sum(square, axis=0, keepdims=True) / model - row_mean * row_mean
    inv_std = lax.rsqrt(row_var + eps)
    stats_ref[...] = jnp.concatenate(
        [row_mean, inv_std, jnp.zeros((6, lanes), f32)], axis=0
    )
    finished = [copy(stats_ref, stats_out)]
    for i, (place, block) in enumerate(blocks_of(where_ref, own_refs, other_refs)):
        centred = (block[:, :lanes].astype(f32) - row_mean) * inv_std
        normed_ref[place] = (
            centred * small_ref[:width, i : i + 1] + small_ref[:width, 16 + i : 17 + i]
        ).astype(bf16)
    project_copy.wait()
    grad_ref[...] = jnp.dot(
        project_ref[...], full_ref[...].reshape(model, lanes), preferred_element_type=f32
    )
    weight_copy.wait()
    proj_ref[...] = jnp.dot(
        weight_ref[...], normed_ref[...].reshape(model, lanes), preferred_element_type=f32
    )
    mask_copy.wait()
    group = 16
    lane = lax.broadcasted_iota(jnp.int32, (group, 128), 1)
    inside = lax.broadcasted_iota(jnp.int32, (group, lanes), 1) < rows

    def channels(step, carry):
        first = pl.multiple_of(step * group, group)
        mine = pl.ds(first, group)
        after = pl.ds(pl.multiple_of(width + first, group), group)
        value = proj_ref[mine, :]
        gate = jax.nn.sigmoid(proj_ref[after, :])
        keep = mask_ref[...]
        glu = (value * gate * keep).astype(bf16).astype(f32)

        def shifted(x, by):
            return pltpu.roll(x, by % lanes, 1) if by % lanes else x

        def tap(k):
            return jnp.concatenate([taps_ref[k, mine, :]] * (lanes // 128), axis=1)

        def spread(fine, sign):
            result = None
            for a in range(4):
                part = None
                for b in range(8):
                    if 8 * a + b < taps:
                        term = tap(8 * a + b) * fine[b]
                        part = term if part is None else part + term
                part = shifted(part, sign * (8 * a - 8))
                result = part if result is None else result + part
            return result

        for b in range(8):
            moved_ref[b] = shifted(glu, 7 - b)
        conv = spread(moved_ref, -1)
        sig = jax.nn.sigmoid(conv)
        act_ref[mine, :] = (conv * sig)[:, :rows].astype(bf16)
        act_grad = grad_ref[mine, :].astype(bf16).astype(f32)
        grad = (act_grad * (sig + conv * sig * (1.0 - sig))).astype(bf16).astype(f32)
        for b in range(8):
            back_ref[b] = shifted(grad, b - 7)
        glu_grad = spread(back_ref, 1)[:, :rows]
        inner = jnp.where(inside, grad, 0.0)
        kernel = jnp.zeros((group, 128), f32)
        for a in range(4):
            here = shifted(inner, 8 * a - 8)
            for b in range(8):
                if 8 * a + b < taps:
                    seen = jnp.sum(here * moved_ref[b], axis=1, keepdims=True)
                    kernel = jnp.where(lane == 8 * a + b, seen, kernel)
        kernel_ref[mine, :] = kernel
        glu_grad = glu_grad * keep[:, :rows]
        gate = gate[:, :rows]
        both_ref[mine, :] = (glu_grad * gate).astype(bf16)
        both_ref[after, :] = (glu_grad * value[:, :rows] * gate * (1.0 - gate)).astype(bf16)
        return carry

    lax.fori_loop(0, width // group, channels, 0)
    both = both_ref[...]
    flipped_copy.wait()
    partial = jnp.dot(flipped_ref[...], both, preferred_element_type=f32).astype(bf16)
    partial = partial.reshape(4, 2, 2, width, rows)
    both = both.astype(f32)
    first = jnp.sum(both * small_ref[:, 32:33], axis=0, keepdims=True)
    second = jnp.sum(both * (proj_ref[:, :rows] - small_ref[:, 33:34]), axis=0, keepdims=True)
    first_high = first.astype(bf16).astype(f32)
    second_high = second.astype(bf16).astype(f32)
    row = lax.broadcasted_iota(jnp.int32, (16, rows), 0)
    extra = jnp.where(row == 0, first_high, 0.0)
    extra = jnp.where(row == 1, second_high, extra)
    extra = jnp.where(row == 2, first - first_high, extra)
    extra = jnp.where(row == 3, second - second_high, extra).astype(bf16)
    zh = where_ref[0]
    for x in range(4):
        for core in range(2):
            for side in range(2):
                start = pl.multiple_of(jnp.where(side == zh, width, 0), width)
                mixed_ref[x * 2 + core, pl.ds(start, width)] = partial[x, side, core]
            mixed_ref[x * 2 + core, 2 * width :] = extra
    finished.append(copy(mixed_ref, mixed_out))

    zero = jnp.zeros((width, rows), bf16)
    grads = lax.dot_general(
        normed_ref[:, :, :rows].reshape(model, rows),
        jnp.concatenate([zero, both_ref[...], zero], axis=0),
        OVER,
        preferred_element_type=f32,
    ) + lax.dot_general(
        full_ref[:, :, :rows].reshape(model, rows),
        jnp.concatenate([zero, zero, zero, act_ref[...]], axis=0),
        OVER,
        preferred_element_type=f32,
    )
    grads_ref[...] = grads.astype(bf16).reshape(grads_ref.shape)
    kernel = jnp.transpose(kernel_ref[...])[: grads_ref.shape[2]].astype(bf16)
    for zl in range(8):
        for y in range(4):
            grads_ref[zl, y, :, :width] = kernel
    for step, out in zip((0, 1, 3, 2), (part0_out, part1_out, part2_out, part3_out)):
        out[...] = grads_ref[:, lax.rem(where_ref[2] + step, 4)]
    for started in finished:
        started.wait()


def on_device(
    inputs,
    norm_gain,
    norm_bias,
    value_weight,
    gate_weight,
    conv_kernel,
    project_weight,
    frame_mask,
    upstream,
):
    width, rows = inputs.shape
    model = value_weight.shape[1]
    taps = conv_kernel.shape[0]
    lanes = rows + 128
    piece = model // 32
    zh = lax.axis_index("zh")
    core = lax.axis_index("core")
    y = lax.axis_index("y")
    zl = lax.axis_index("zl")
    offset = lax.axis_index(CHAN) * width
    x = lax.axis_index("x")
    where = jnp.stack([zh, core, y, x]).astype(jnp.int32)

    to_right, to_left = call(
        edges,
        (shape((width + 16, 128), bf16), shape((width + 16, 128), bf16)),
        scratch=(pltpu.VMEM((2, 2, width, 128), bf16), pltpu.SemaphoreType.DMA((4,))),
        specs=[pl.BlockSpec(memory_space=pltpu.HBM)] * 2 + [VMEM],
    )(
        pltpu.with_memory_space_constraint(inputs, pltpu.HBM),
        pltpu.with_memory_space_constraint(upstream, pltpu.HBM),
        frame_mask.reshape(1, rows),
    )
    edge = lax.ppermute(to_right, FRAME, [(i, i + 1) for i in range(31)]) + lax.ppermute(
        to_left, FRAME, [(i + 1, i) for i in range(31)]
    )

    weights = jnp.concatenate([value_weight, gate_weight])
    by_gain = jnp.sum(weights.astype(f32) * norm_gain[None, :], axis=1, keepdims=True)
    by_bias = jnp.sum(weights.astype(f32) * norm_bias[None, :], axis=1, keepdims=True)
    gain_local = lax.dynamic_slice_in_dim(norm_gain, offset, width, 0)[:, None]

    def columns_of(parameter):
        parameter = parameter.reshape(4, 2, 2, width)
        parameter = jnp.stack(
            [lax.dynamic_index_in_dim(parameter, (x + 4 - step) % 4, 0, False) for step in STEPS]
        )
        parameter = jnp.where(zh == 0, parameter, parameter[:, ::-1])
        parameter = jnp.where(core == 0, parameter, parameter[:, :, ::-1])
        return parameter.reshape(16, width).T

    small = jnp.concatenate([columns_of(norm_gain), columns_of(norm_bias)], axis=1)
    small = jnp.concatenate(
        [
            jnp.pad(small, ((0, width), (0, 0))),
            by_gain,
            by_bias,
            jnp.pad(conv_kernel.T, ((0, width), (0, 128 - 34 - taps))),
        ],
        axis=1,
    )
    early = (weights, weights.T, small, gain_local, where)

    held = jnp.concatenate([inputs, edge[:width], upstream], axis=1)
    keep = jnp.concatenate([frame_mask.astype(f32)[None, :], edge[width : width + 1].astype(f32)], axis=1)
    came = swap(held, "zh")
    came, keep, early = lax.optimization_barrier((came, keep, early))
    weights, flipped, small, gain_local, where = early
    far_inputs = came[:, :rows]
    pair = jnp.stack([held, came])
    own = [pair] + [
        lax.ppermute(pair, "x", [(i, (i + step) % 4) for i in range(4)]) for step in STEPS[1:]
    ]
    other = [swap(block, "core") for block in own]
    piece_shape = (8, piece, 4 * width)
    operands = (small, weights, project_weight, flipped, keep)
    mixed, *pieces, stats = pl.pallas_call(
        middle,
        out_shape=(
            pltpu.HBM((8, 2 * width + 16, rows), bf16),
            *(pltpu.VMEM(piece_shape, bf16) for _ in range(4)),
            pltpu.HBM((8, lanes), f32),
        ),
        in_specs=[SMEM] + [VMEM] * 8 + [pl.BlockSpec(memory_space=pltpu.HBM)] * len(operands),
        out_specs=tuple(pl.BlockSpec(memory_space=pltpu.HBM if i in (0, 5) else pltpu.VMEM) for i in range(6)),
        scratch_shapes=[pltpu.VMEM(operand.shape, operand.dtype) for operand in operands]
        + [
            pltpu.VMEM((taps, width, 128), f32),
            pltpu.VMEM((8, 2 * width + 16, rows), bf16),
            pltpu.VMEM((8, 4, piece, 4 * width), bf16),
            pltpu.VMEM((8, lanes), f32),
            pltpu.VMEM((16, width, lanes), bf16),
            pltpu.VMEM((16, width, lanes), bf16),
            pltpu.VMEM((2 * width, rows), bf16),
            pltpu.VMEM((width, rows), bf16),
            pltpu.VMEM((width, 128), f32),
            pltpu.VMEM((2 * width, lanes), f32),
            pltpu.VMEM((width, lanes), f32),
            pltpu.VMEM((8, 16, lanes), f32),
            pltpu.VMEM((8, 16, lanes), f32),
            pltpu.SemaphoreType.DMA((20,)),
        ],
        compiler_params=pltpu.CompilerParams(vmem_limit_bytes=26 << 20),
    )(where, *own, *other, *(pltpu.with_memory_space_constraint(operand, pltpu.HBM) for operand in operands))

    mixed = lax.all_to_all(mixed, ("x", "core"), 0, 0, tiled=True)

    parts = [
        lax.ppermute(sent, "y", [(i, (i + step) % 4) for i in range(4)])
        for step, sent in zip((1, 3, 2), pieces[1:])
    ]
    total = pieces[0].astype(f32)
    for part in parts:
        total = total + part.astype(f32)

    side = zl % 2
    total = total.reshape(4, 2, piece, 4 * width)
    sent = lax.dynamic_slice_in_dim(total, 1 - side, 1, 1)[:, 0].astype(bf16)
    total = lax.dynamic_slice_in_dim(total, side, 1, 1)[:, 0]
    sent, mixed = lax.optimization_barrier((sent, mixed))
    total = total + lax.ppermute(sent, "zl", [(i, i ^ 1) for i in range(8)]).astype(f32)

    mixed = jnp.sum(mixed.astype(f32), axis=0)
    near = mixed[width : 2 * width]
    inv_std = stats[1:2, :rows]
    centred = (inputs.astype(f32) - stats[0:1, :rows]) * inv_std
    centred_far = (far_inputs.astype(f32) - stats[0:1, :rows]) * inv_std
    near_tail = jnp.stack([jnp.sum(near * centred, axis=1), jnp.sum(near, axis=1)])
    far_tail = jnp.stack([jnp.sum(mixed[:width] * centred_far, axis=1), jnp.sum(mixed[:width], axis=1)])
    tail, near = lax.optimization_barrier((ordered(near_tail, far_tail, zh, 0), near))
    far_sums = mixed[2 * width : 2 * width + 2] + mixed[2 * width + 2 : 2 * width + 4]
    sent_high, sent_low = split_bf16(far_sums)
    far = jnp.concatenate(
        [mixed[:width].astype(bf16), sent_high, sent_low, jnp.zeros((12, rows), bf16)]
    )
    came = swap(far, "zh").astype(f32)

    tail = lax.all_to_all(
        jnp.broadcast_to(tail[None], (32, 2, 2, width)).reshape(64, 2, width),
        FRAME + ("zh",), 0, 0, tiled=True,
    )

    normed_grad = near + came[:width]
    kept = far[width : width + 4].astype(f32)
    sums = (kept[:2] + kept[2:] + came[width : width + 2] + came[width + 2 : width + 4]) / model
    total, normed_grad = lax.optimization_barrier((total, normed_grad))
    inputs_grad = (
        upstream.astype(f32)
        + inv_std * (normed_grad * gain_local - sums[0:1] - centred * sums[1:2])
    ).astype(bf16)

    for size in (2, 4):
        side = (zl // size) % 2
        total = total.reshape(4 // size, 2, piece, 4 * width)
        sent = lax.dynamic_slice_in_dim(total, 1 - side, 1, 1)[:, 0].astype(bf16)
        total = lax.dynamic_slice_in_dim(total, side, 1, 1)[:, 0]
        total = total + lax.ppermute(sent, "zl", [(i, i ^ size) for i in range(8)]).astype(f32)
    grads = total[0]
    tail, grads = lax.optimization_barrier((tail, grads))
    tail = jnp.sum(tail, axis=0)
    kernel_grad = grads[:taps, :width]
    value_grad = grads[:, width : 2 * width].T
    gate_grad = grads[:, 2 * width : 3 * width].T
    project_grad = grads[:, 3 * width :].T
    return (inputs_grad, value_grad, gate_grad, project_grad, kernel_grad, tail[0], tail[1])


def solution(mesh):
    split = Mesh(mesh.devices.reshape(8, 4, 4, 2, 2), FRAME + CHAN)
    return jax.shard_map(
        on_device,
        mesh=split,
        in_specs=(
            P(CHAN, FRAME),
            P(),
            P(),
            P(CHAN, None),
            P(CHAN, None),
            P(None, CHAN),
            P(CHAN, None),
            P(FRAME),
            P(CHAN, FRAME),
        ),
        out_specs=(
            P(CHAN, FRAME),
            P(CHAN, FRAME),
            P(CHAN, FRAME),
            P(CHAN, FRAME),
            P(None, CHAN),
            P(CHAN),
            P(CHAN),
        ),
        check_vma=False,
    )
```

```python
import jax
import jax.numpy as jnp
from jax import lax
from jax.experimental import pallas as pl
from jax.experimental.pallas import tpu as pltpu
from jax.sharding import Mesh, PartitionSpec as P

eps = 1e-05
CHAN = ("x", "zh", "core")
FRAME = ("zl", "y")
SWAP = [(0, 1), (1, 0)]
f32 = jnp.float32
bf16 = jnp.bfloat16
VMEM = pl.BlockSpec(memory_space=pltpu.VMEM)
SMEM = pl.BlockSpec(memory_space=pltpu.SMEM)
OVER = (((1,), (1,)), ((), ()))


def swap(value, axis):
    return lax.ppermute(value, axis, SWAP)


def over_x(pair):
    return lax.all_to_all(
        jnp.broadcast_to(pair[None], (4,) + pair.shape), "x", 0, 0, tiled=True
    )


def ordered(own, other, index, axis):
    return jnp.where(
        index == 0, jnp.stack([own, other], axis), jnp.stack([other, own], axis)
    )


def split_bf16(value):
    high = value.astype(bf16)
    return high, (value - high.astype(f32)).astype(bf16)


def shape(dims, dtype):
    return jax.ShapeDtypeStruct(dims, dtype)


def call(kernel, outs, scratch=(), specs=None):
    return pl.pallas_call(
        kernel,
        out_shape=outs,
        in_specs=specs,
        out_specs=tuple(VMEM for _ in outs),
        scratch_shapes=list(scratch),
        compiler_params=pltpu.CompilerParams(vmem_limit_bytes=24 << 20),
    )


def blocks_of(where_ref, own_ref, other_ref):
    zh, core = where_ref[0], where_ref[1]
    for x in range(4):
        for far in range(2):
            side = zh if far == 0 else 1 - zh
            yield x * 4 + side * 2 + core, own_ref.at[x, far]
            yield x * 4 + side * 2 + 1 - core, other_ref.at[x, far]


def edges(inputs_hbm, upstream_hbm, mask_ref, right_ref, left_ref, ends_ref, sems):
    width, rows = inputs_hbm.shape
    starts = (rows - 128, 0)
    copies = []
    for i, start in enumerate(starts):
        for j, source in enumerate((inputs_hbm, upstream_hbm)):
            copies.append(
                pltpu.make_async_copy(
                    source.at[:, start : start + 128], ends_ref.at[i, j], sems.at[2 * i + j]
                )
            )
            copies[-1].start()
    for started in copies:
        started.wait()
    lane = lax.broadcasted_iota(jnp.int32, (width, 128), 1)
    low = lax.broadcasted_iota(jnp.int32, (16, 128), 1)

    def pack(i, own, moved, ref):
        up = pltpu.roll(ends_ref[i, 1].astype(f32), 64, 1)
        ref[:width] = jnp.where(
            own(lane), ends_ref[i, 0].astype(f32), jnp.where(moved(lane), up, 0.0)
        ).astype(bf16)
        mask = mask_ref[:, starts[i] : starts[i] + 128].astype(f32)
        ref[width:] = jnp.where(own(low), jnp.broadcast_to(mask, (16, 128)), 0.0).astype(bf16)

    pack(0, lambda i: i >= 98, lambda i: (i >= 49) & (i < 64), right_ref)
    pack(1, lambda i: i < 30, lambda i: (i >= 64) & (i < 79), left_ref)


def middle(
    where_ref, own_hbm, other_hbm, small_hbm, weight_hbm, project_hbm, flipped_hbm, mask_hbm,
    mixed_out, part0_out, part1_out, part2_out, part3_out, stats_out,
    own_ref, other_ref, small_ref, weight_ref, project_ref, flipped_ref, mask_ref,
    taps_ref, mixed_ref, grads_ref, stats_ref, normed_ref, full_ref, both_ref, act_ref, kernel_ref,
    proj_ref, grad_ref, moved_ref, back_ref, sems,
):
    model = weight_ref.shape[1]
    width = own_ref.shape[2]
    lanes = normed_ref.shape[2]
    rows = mixed_ref.shape[2]
    taps = taps_ref.shape[0]
    count = 0

    def copy(source, target):
        nonlocal count
        started = pltpu.make_async_copy(source, target, sems.at[count])
        started.start()
        count += 1
        return started

    small_copy = copy(small_hbm, small_ref)
    blocks = [
        copy(source.at[x], target.at[x])
        for x in range(4)
        for source, target in ((own_hbm, own_ref), (other_hbm, other_ref))
    ]
    mask_copy = copy(mask_hbm, mask_ref)
    project_copy = copy(project_hbm, project_ref)
    weight_copy = copy(weight_hbm, weight_ref)
    flipped_copy = copy(flipped_hbm, flipped_ref)
    small_copy.wait()
    for k in range(taps):
        taps_ref[k] = jnp.broadcast_to(small_ref[:width, 34 + k : 35 + k], (width, 128))
    total = jnp.zeros((8, lanes), f32)
    square = jnp.zeros((8, lanes), f32)
    for i, (place, block) in enumerate(blocks_of(where_ref, own_ref, other_ref)):
        if i % 4 == 0:
            blocks[i // 2].wait()
            blocks[i // 2 + 1].wait()
        x = block[:, :lanes].astype(f32).reshape(width // 8, 8, lanes)
        total = total + jnp.sum(x, axis=0)
        square = square + jnp.sum(x * x, axis=0)
        full_ref[place, :, :rows] = block[:, lanes:]
        full_ref[place, :, rows:] = pltpu.roll(
            block[:, rows:lanes].astype(f32), 64, 1
        ).astype(bf16)
    row_mean = jnp.sum(total, axis=0, keepdims=True) / model
    row_var = jnp.sum(square, axis=0, keepdims=True) / model - row_mean * row_mean
    inv_std = lax.rsqrt(row_var + eps)
    stats_ref[...] = jnp.concatenate(
        [row_mean, inv_std, jnp.zeros((6, lanes), f32)], axis=0
    )
    finished = [copy(stats_ref, stats_out)]
    for i, (place, block) in enumerate(blocks_of(where_ref, own_ref, other_ref)):
        centred = (block[:, :lanes].astype(f32) - row_mean) * inv_std
        normed_ref[place] = (
            centred * small_ref[:width, i : i + 1] + small_ref[:width, 16 + i : 17 + i]
        ).astype(bf16)
    project_copy.wait()
    grad_ref[...] = jnp.dot(
        project_ref[...], full_ref[...].reshape(model, lanes), preferred_element_type=f32
    )
    weight_copy.wait()
    proj_ref[...] = jnp.dot(
        weight_ref[...], normed_ref[...].reshape(model, lanes), preferred_element_type=f32
    )
    mask_copy.wait()
    group = 32
    lane = lax.broadcasted_iota(jnp.int32, (group, 128), 1)
    inside = lax.broadcasted_iota(jnp.int32, (group, lanes), 1) < rows

    def channels(step, carry):
        first = pl.multiple_of(step * group, group)
        mine = pl.ds(first, group)
        after = pl.ds(pl.multiple_of(width + first, group), group)
        value = proj_ref[mine, :]
        gate = jax.nn.sigmoid(proj_ref[after, :])
        keep = mask_ref[...]
        glu = (value * gate * keep).astype(bf16).astype(f32)

        def shifted(x, by):
            return pltpu.roll(x, by % lanes, 1) if by % lanes else x

        def tap(k):
            return jnp.concatenate([taps_ref[k, mine, :]] * (lanes // 128), axis=1)

        def spread(fine, sign):
            result = None
            for a in range(4):
                part = None
                for b in range(8):
                    if 8 * a + b < taps:
                        term = tap(8 * a + b) * fine[b]
                        part = term if part is None else part + term
                part = shifted(part, sign * (8 * a - 8))
                result = part if result is None else result + part
            return result

        for b in range(8):
            moved_ref[b] = shifted(glu, 7 - b)
        conv = spread(moved_ref, -1)
        sig = jax.nn.sigmoid(conv)
        act_ref[mine, :] = (conv * sig)[:, :rows].astype(bf16)
        act_grad = grad_ref[mine, :].astype(bf16).astype(f32)
        grad = (act_grad * (sig + conv * sig * (1.0 - sig))).astype(bf16).astype(f32)
        for b in range(8):
            back_ref[b] = shifted(grad, b - 7)
        glu_grad = spread(back_ref, 1)[:, :rows]
        inner = jnp.where(inside, grad, 0.0)
        kernel = jnp.zeros((group, 128), f32)
        for a in range(4):
            here = shifted(inner, 8 * a - 8)
            for b in range(8):
                if 8 * a + b < taps:
                    seen = jnp.sum(here * moved_ref[b], axis=1, keepdims=True)
                    kernel = jnp.where(lane == 8 * a + b, seen, kernel)
        kernel_ref[mine, :] = kernel
        glu_grad = glu_grad * keep[:, :rows]
        gate = gate[:, :rows]
        both_ref[mine, :] = (glu_grad * gate).astype(bf16)
        both_ref[after, :] = (glu_grad * value[:, :rows] * gate * (1.0 - gate)).astype(bf16)
        return carry

    lax.fori_loop(0, width // group, channels, 0)
    both = both_ref[...]
    flipped_copy.wait()
    partial = jnp.dot(flipped_ref[...], both, preferred_element_type=f32).astype(bf16)
    partial = partial.reshape(4, 2, 2, width, rows)
    both = both.astype(f32)
    first = jnp.sum(both * small_ref[:, 32:33], axis=0, keepdims=True)
    second = jnp.sum(both * (proj_ref[:, :rows] - small_ref[:, 33:34]), axis=0, keepdims=True)
    first_high = first.astype(bf16).astype(f32)
    second_high = second.astype(bf16).astype(f32)
    row = lax.broadcasted_iota(jnp.int32, (16, rows), 0)
    extra = jnp.where(row == 0, first_high, 0.0)
    extra = jnp.where(row == 1, second_high, extra)
    extra = jnp.where(row == 2, first - first_high, extra)
    extra = jnp.where(row == 3, second - second_high, extra).astype(bf16)
    zh = where_ref[0]
    for x in range(4):
        for core in range(2):
            for side in range(2):
                start = pl.multiple_of(jnp.where(side == zh, width, 0), width)
                mixed_ref[x * 2 + core, pl.ds(start, width)] = partial[x, side, core]
            mixed_ref[x * 2 + core, 2 * width :] = extra
    finished.append(copy(mixed_ref, mixed_out))

    piece = grads_ref.shape[2]
    kernel = jnp.transpose(kernel_ref[...])[:piece]
    kernel = jnp.concatenate([kernel, jnp.zeros((piece, 128 - width), f32)], axis=1)
    lane = lax.broadcasted_iota(jnp.int32, (piece, 128), 1)
    for source, factor, start, by, first in (
        (normed_ref, both_ref, 0, 64, 64),
        (full_ref, act_ref, 256, 32, 96),
    ):
        rest = -factor.shape[0] % 128
        part = lax.dot_general(
            source[:, :, :rows].reshape(model, rows),
            jnp.concatenate([factor[...], jnp.zeros((rest, rows), bf16)], axis=0),
            OVER,
            preferred_element_type=f32,
        )
        size = part.shape[1]
        part = part.reshape(8, 4, piece, size)
        taps_here = jnp.where(lane >= first, pltpu.roll(kernel, by, 1), 0.0)
        if size > 128:
            grads_ref[:, :, :, start : start + size - 128] = part[..., : size - 128].astype(bf16)
        grads_ref[:, :, :, start + size - 128 : start + size] = (
            part[..., size - 128 :] + taps_here
        ).astype(bf16)
    for step, out in zip((0, 1, 3, 2), (part0_out, part1_out, part2_out, part3_out)):
        out[...] = grads_ref[:, lax.rem(where_ref[2] + step, 4)]
    for started in finished:
        started.wait()


def on_device(
    inputs,
    norm_gain,
    norm_bias,
    value_weight,
    gate_weight,
    conv_kernel,
    project_weight,
    frame_mask,
    upstream,
):
    width, rows = inputs.shape
    model = value_weight.shape[1]
    taps = conv_kernel.shape[0]
    lanes = rows + 128
    piece = model // 32
    zh = lax.axis_index("zh")
    core = lax.axis_index("core")
    y = lax.axis_index("y")
    zl = lax.axis_index("zl")
    offset = lax.axis_index(CHAN) * width
    where = jnp.stack([zh, core, y]).astype(jnp.int32)

    to_right, to_left = call(
        edges,
        (shape((width + 16, 128), bf16), shape((width + 16, 128), bf16)),
        scratch=(pltpu.VMEM((2, 2, width, 128), bf16), pltpu.SemaphoreType.DMA((4,))),
        specs=[pl.BlockSpec(memory_space=pltpu.HBM)] * 2 + [VMEM],
    )(
        pltpu.with_memory_space_constraint(inputs, pltpu.HBM),
        pltpu.with_memory_space_constraint(upstream, pltpu.HBM),
        frame_mask.reshape(1, rows),
    )
    edge = lax.ppermute(to_right, FRAME, [(i, i + 1) for i in range(31)]) + lax.ppermute(
        to_left, FRAME, [(i + 1, i) for i in range(31)]
    )

    weights = jnp.concatenate([value_weight, gate_weight])
    by_gain = jnp.sum(weights.astype(f32) * norm_gain[None, :], axis=1, keepdims=True)
    by_bias = jnp.sum(weights.astype(f32) * norm_bias[None, :], axis=1, keepdims=True)
    gain_local = lax.dynamic_slice_in_dim(norm_gain, offset, width, 0)[:, None]

    def columns_of(parameter):
        parameter = parameter.reshape(4, 2, 2, width)
        parameter = jnp.where(zh == 0, parameter, parameter[:, ::-1])
        parameter = jnp.where(core == 0, parameter, parameter[:, :, ::-1])
        return parameter.reshape(16, width).T

    small = jnp.concatenate([columns_of(norm_gain), columns_of(norm_bias)], axis=1)
    small = jnp.concatenate(
        [
            jnp.pad(small, ((0, width), (0, 0))),
            by_gain,
            by_bias,
            jnp.pad(conv_kernel.T, ((0, width), (0, 128 - 34 - taps))),
        ],
        axis=1,
    )
    early = (weights, weights.T, small, gain_local, where)

    held = jnp.concatenate([inputs, edge[:width], upstream], axis=1)
    keep = jnp.concatenate([frame_mask.astype(f32)[None, :], edge[width : width + 1].astype(f32)], axis=1)
    came = swap(held, "zh")
    came, keep, early = lax.optimization_barrier((came, keep, early))
    weights, flipped, small, gain_local, where = early
    far_inputs = came[:, :rows]
    own = over_x(jnp.stack([held, came]))
    other = swap(own, "core")
    piece_shape = (8, piece, 4 * width)
    operands = (own, other, small, weights, project_weight, flipped, keep)
    mixed, *pieces, stats = pl.pallas_call(
        middle,
        out_shape=(
            pltpu.HBM((8, 2 * width + 16, rows), bf16),
            *(pltpu.VMEM(piece_shape, bf16) for _ in range(4)),
            pltpu.HBM((8, lanes), f32),
        ),
        in_specs=[SMEM] + [pl.BlockSpec(memory_space=pltpu.HBM)] * len(operands),
        out_specs=tuple(pl.BlockSpec(memory_space=pltpu.HBM if i in (0, 5) else pltpu.VMEM) for i in range(6)),
        scratch_shapes=[pltpu.VMEM(operand.shape, operand.dtype) for operand in operands]
        + [
            pltpu.VMEM((taps, width, 128), f32),
            pltpu.VMEM((8, 2 * width + 16, rows), bf16),
            pltpu.VMEM((8, 4, piece, 4 * width), bf16),
            pltpu.VMEM((8, lanes), f32),
            pltpu.VMEM((16, width, lanes), bf16),
            pltpu.VMEM((16, width, lanes), bf16),
            pltpu.VMEM((2 * width, rows), bf16),
            pltpu.VMEM((width, rows), bf16),
            pltpu.VMEM((width, 128), f32),
            pltpu.VMEM((2 * width, lanes), f32),
            pltpu.VMEM((width, lanes), f32),
            pltpu.VMEM((8, 32, lanes), f32),
            pltpu.VMEM((8, 32, lanes), f32),
            pltpu.SemaphoreType.DMA((20,)),
        ],
        compiler_params=pltpu.CompilerParams(vmem_limit_bytes=40 << 20),
    )(where, *(pltpu.with_memory_space_constraint(operand, pltpu.HBM) for operand in operands))

    mixed = lax.all_to_all(mixed, ("x", "core"), 0, 0, tiled=True)

    parts = [
        lax.ppermute(sent, "y", [(i, (i + step) % 4) for i in range(4)])
        for step, sent in zip((1, 3, 2), pieces[1:])
    ]
    total = pieces[0].astype(f32)
    for part in parts:
        total = total + part.astype(f32)

    side = zl % 2
    total = total.reshape(4, 2, piece, 4 * width)
    sent = lax.dynamic_slice_in_dim(total, 1 - side, 1, 1)[:, 0].astype(bf16)
    total = lax.dynamic_slice_in_dim(total, side, 1, 1)[:, 0]
    sent, mixed = lax.optimization_barrier((sent, mixed))
    total = total + lax.ppermute(sent, "zl", [(i, i ^ 1) for i in range(8)]).astype(f32)

    mixed = jnp.sum(mixed.astype(f32), axis=0)
    near = mixed[width : 2 * width]
    inv_std = stats[1:2, :rows]
    centred = (inputs.astype(f32) - stats[0:1, :rows]) * inv_std
    centred_far = (far_inputs.astype(f32) - stats[0:1, :rows]) * inv_std
    near_tail = jnp.stack([jnp.sum(near * centred, axis=1), jnp.sum(near, axis=1)])
    far_tail = jnp.stack([jnp.sum(mixed[:width] * centred_far, axis=1), jnp.sum(mixed[:width], axis=1)])
    tail, near = lax.optimization_barrier((ordered(near_tail, far_tail, zh, 0), near))
    far_sums = mixed[2 * width : 2 * width + 2] + mixed[2 * width + 2 : 2 * width + 4]
    sent_high, sent_low = split_bf16(far_sums)
    far = jnp.concatenate(
        [mixed[:width].astype(bf16), sent_high, sent_low, jnp.zeros((12, rows), bf16)]
    )
    came = swap(far, "zh").astype(f32)

    tail = lax.all_to_all(
        jnp.broadcast_to(tail[None], (32, 2, 2, width)).reshape(64, 2, width),
        FRAME + ("zh",), 0, 0, tiled=True,
    )

    normed_grad = near + came[:width]
    kept = far[width : width + 4].astype(f32)
    sums = (kept[:2] + kept[2:] + came[width : width + 2] + came[width + 2 : width + 4]) / model
    total, normed_grad = lax.optimization_barrier((total, normed_grad))
    inputs_grad = (
        upstream.astype(f32)
        + inv_std * (normed_grad * gain_local - sums[0:1] - centred * sums[1:2])
    ).astype(bf16)

    for size in (2, 4):
        side = (zl // size) % 2
        total = total.reshape(4 // size, 2, piece, 4 * width)
        sent = lax.dynamic_slice_in_dim(total, 1 - side, 1, 1)[:, 0].astype(bf16)
        total = lax.dynamic_slice_in_dim(total, side, 1, 1)[:, 0]
        total = total + lax.ppermute(sent, "zl", [(i, i ^ size) for i in range(8)]).astype(f32)
    grads = total[0]
    tail, grads = lax.optimization_barrier((tail, grads))
    tail = jnp.sum(tail, axis=0)
    kernel_grad = jnp.concatenate([grads[:taps, 192:256], grads[:taps, 352:384]], axis=1)
    value_grad = grads[:, :width].T
    gate_grad = grads[:, width : 2 * width].T
    project_grad = grads[:, 256 : 256 + width].T
    return (inputs_grad, value_grad, gate_grad, project_grad, kernel_grad, tail[0], tail[1])


def solution(mesh):
    split = Mesh(mesh.devices.reshape(8, 4, 4, 2, 2), FRAME + CHAN)
    return jax.shard_map(
        on_device,
        mesh=split,
        in_specs=(
            P(CHAN, FRAME),
            P(),
            P(),
            P(CHAN, None),
            P(CHAN, None),
            P(None, CHAN),
            P(CHAN, None),
            P(FRAME),
            P(CHAN, FRAME),
        ),
        out_specs=(
            P(CHAN, FRAME),
            P(CHAN, FRAME),
            P(CHAN, FRAME),
            P(CHAN, FRAME),
            P(None, CHAN),
            P(CHAN),
            P(CHAN),
        ),
        check_vma=False,
    )
```

```python
import jax
import jax.numpy as jnp
from jax import lax
from jax.experimental import pallas as pl
from jax.experimental.pallas import tpu as pltpu
from jax.sharding import Mesh, PartitionSpec as P

eps = 1e-05
CHAN = ("x", "zh", "core")
FRAME = ("zl", "y")
SWAP = [(0, 1), (1, 0)]
f32 = jnp.float32
bf16 = jnp.bfloat16
VMEM = pl.BlockSpec(memory_space=pltpu.VMEM)
SMEM = pl.BlockSpec(memory_space=pltpu.SMEM)
OVER = (((1,), (1,)), ((), ()))


def swap(value, axis):
    return lax.ppermute(value, axis, SWAP)


def over_x(pair):
    return lax.all_to_all(
        jnp.broadcast_to(pair[None], (4,) + pair.shape), "x", 0, 0, tiled=True
    )


def ordered(own, other, index, axis):
    return jnp.where(
        index == 0, jnp.stack([own, other], axis), jnp.stack([other, own], axis)
    )


def split_bf16(value):
    high = value.astype(bf16)
    return high, (value - high.astype(f32)).astype(bf16)


def shape(dims, dtype):
    return jax.ShapeDtypeStruct(dims, dtype)


def call(kernel, outs, scratch=(), specs=None):
    return pl.pallas_call(
        kernel,
        out_shape=outs,
        in_specs=specs,
        out_specs=tuple(VMEM for _ in outs),
        scratch_shapes=list(scratch),
        compiler_params=pltpu.CompilerParams(vmem_limit_bytes=24 << 20),
    )


def blocks_of(where_ref, own_ref, other_ref):
    zh, core = where_ref[0], where_ref[1]
    for x in range(4):
        for far in range(2):
            side = zh if far == 0 else 1 - zh
            yield x * 4 + side * 2 + core, own_ref.at[x, far]
            yield x * 4 + side * 2 + 1 - core, other_ref.at[x, far]


def edges(inputs_hbm, upstream_hbm, mask_ref, right_ref, left_ref, ends_ref, sems):
    width, rows = inputs_hbm.shape
    starts = (rows - 128, 0)
    copies = []
    for i, start in enumerate(starts):
        for j, source in enumerate((inputs_hbm, upstream_hbm)):
            copies.append(
                pltpu.make_async_copy(
                    source.at[:, start : start + 128], ends_ref.at[i, j], sems.at[2 * i + j]
                )
            )
            copies[-1].start()
    for started in copies:
        started.wait()
    lane = lax.broadcasted_iota(jnp.int32, (width, 128), 1)
    low = lax.broadcasted_iota(jnp.int32, (16, 128), 1)

    def pack(i, own, moved, ref):
        up = pltpu.roll(ends_ref[i, 1].astype(f32), 64, 1)
        ref[:width] = jnp.where(
            own(lane), ends_ref[i, 0].astype(f32), jnp.where(moved(lane), up, 0.0)
        ).astype(bf16)
        mask = mask_ref[pl.ds(starts[i], 128)].reshape(1, 128).astype(f32)
        ref[width:] = jnp.where(own(low), jnp.broadcast_to(mask, (16, 128)), 0.0).astype(bf16)

    pack(0, lambda i: i >= 98, lambda i: (i >= 49) & (i < 64), right_ref)
    pack(1, lambda i: i < 30, lambda i: (i >= 64) & (i < 79), left_ref)


def middle(
    where_ref, own_hbm, other_hbm, small_hbm, weight_hbm, project_hbm, flipped_hbm, mask_hbm,
    mixed_out, part0_out, part1_out, part2_out, part3_out, stats_out,
    own_ref, other_ref, small_ref, weight_ref, project_ref, flipped_ref, mask_ref,
    taps_ref, mixed_ref, grads_ref, stats_ref, normed_ref, full_ref, both_ref, act_ref, kernel_ref,
    proj_ref, grad_ref, moved_ref, back_ref, sems,
):
    model = weight_ref.shape[1]
    width = own_ref.shape[2]
    lanes = normed_ref.shape[2]
    rows = mixed_ref.shape[2]
    taps = taps_ref.shape[0]
    count = 0

    def copy(source, target):
        nonlocal count
        started = pltpu.make_async_copy(source, target, sems.at[count])
        started.start()
        count += 1
        return started

    small_copy = copy(small_hbm, small_ref)
    blocks = [
        copy(source.at[x], target.at[x])
        for x in range(4)
        for source, target in ((own_hbm, own_ref), (other_hbm, other_ref))
    ]
    mask_copy = copy(mask_hbm, mask_ref)
    project_copy = copy(project_hbm, project_ref)
    weight_copy = copy(weight_hbm, weight_ref)
    flipped_copy = copy(flipped_hbm, flipped_ref)
    small_copy.wait()
    for k in range(taps):
        taps_ref[k] = jnp.broadcast_to(small_ref[:width, 34 + k : 35 + k], (width, 128))
    total = jnp.zeros((8, lanes), f32)
    square = jnp.zeros((8, lanes), f32)
    for i, (place, block) in enumerate(blocks_of(where_ref, own_ref, other_ref)):
        if i % 4 == 0:
            blocks[i // 2].wait()
            blocks[i // 2 + 1].wait()
        x = block[:, :lanes].astype(f32).reshape(width // 8, 8, lanes)
        total = total + jnp.sum(x, axis=0)
        square = square + jnp.sum(x * x, axis=0)
        full_ref[place, :, :rows] = block[:, lanes:]
        full_ref[place, :, rows:] = pltpu.roll(
            block[:, rows:lanes].astype(f32), 64, 1
        ).astype(bf16)
    row_mean = jnp.sum(total, axis=0, keepdims=True) / model
    row_var = jnp.sum(square, axis=0, keepdims=True) / model - row_mean * row_mean
    inv_std = lax.rsqrt(row_var + eps)
    stats_ref[...] = jnp.concatenate(
        [row_mean, inv_std, jnp.zeros((6, lanes), f32)], axis=0
    )
    finished = [copy(stats_ref, stats_out)]
    for i, (place, block) in enumerate(blocks_of(where_ref, own_ref, other_ref)):
        centred = (block[:, :lanes].astype(f32) - row_mean) * inv_std
        normed_ref[place] = (
            centred * small_ref[:width, i : i + 1] + small_ref[:width, 16 + i : 17 + i]
        ).astype(bf16)
    project_copy.wait()
    grad_ref[...] = jnp.dot(
        project_ref[...], full_ref[...].reshape(model, lanes), preferred_element_type=f32
    )
    weight_copy.wait()
    proj_ref[...] = jnp.dot(
        weight_ref[...], normed_ref[...].reshape(model, lanes), preferred_element_type=f32
    )
    mask_copy.wait()
    group = 32
    lane = lax.broadcasted_iota(jnp.int32, (group, 128), 1)
    inside = lax.broadcasted_iota(jnp.int32, (group, lanes), 1) < rows

    def channels(step, carry):
        first = pl.multiple_of(step * group, group)
        mine = pl.ds(first, group)
        after = pl.ds(pl.multiple_of(width + first, group), group)
        value = proj_ref[mine, :]
        gate = jax.nn.sigmoid(proj_ref[after, :])
        keep = mask_ref[...]
        glu = (value * gate * keep).astype(bf16).astype(f32)

        def shifted(x, by):
            return pltpu.roll(x, by % lanes, 1) if by % lanes else x

        def tap(k):
            return jnp.concatenate([taps_ref[k, mine, :]] * (lanes // 128), axis=1)

        def spread(fine, sign):
            result = None
            for a in range(4):
                part = None
                for b in range(8):
                    if 8 * a + b < taps:
                        term = tap(8 * a + b) * fine[b]
                        part = term if part is None else part + term
                part = shifted(part, sign * (8 * a - 8))
                result = part if result is None else result + part
            return result

        for b in range(8):
            moved_ref[b] = shifted(glu, 7 - b)
        conv = spread(moved_ref, -1)
        sig = jax.nn.sigmoid(conv)
        act_ref[mine, :] = (conv * sig)[:, :rows].astype(bf16)
        act_grad = grad_ref[mine, :].astype(bf16).astype(f32)
        grad = (act_grad * (sig + conv * sig * (1.0 - sig))).astype(bf16).astype(f32)
        for b in range(8):
            back_ref[b] = shifted(grad, b - 7)
        glu_grad = spread(back_ref, 1)[:, :rows]
        inner = jnp.where(inside, grad, 0.0)
        kernel = jnp.zeros((group, 128), f32)
        for a in range(4):
            here = shifted(inner, 8 * a - 8)
            for b in range(8):
                if 8 * a + b < taps:
                    seen = jnp.sum(here * moved_ref[b], axis=1, keepdims=True)
                    kernel = jnp.where(lane == 8 * a + b, seen, kernel)
        kernel_ref[mine, :] = kernel
        glu_grad = glu_grad * keep[:, :rows]
        gate = gate[:, :rows]
        both_ref[mine, :] = (glu_grad * gate).astype(bf16)
        both_ref[after, :] = (glu_grad * value[:, :rows] * gate * (1.0 - gate)).astype(bf16)
        return carry

    lax.fori_loop(0, width // group, channels, 0)
    both = both_ref[...]
    flipped_copy.wait()
    partial = jnp.dot(flipped_ref[...], both, preferred_element_type=f32).astype(bf16)
    partial = partial.reshape(4, 2, 2, width, rows)
    both = both.astype(f32)
    first = jnp.sum(both * small_ref[:, 32:33], axis=0, keepdims=True)
    second = jnp.sum(both * (proj_ref[:, :rows] - small_ref[:, 33:34]), axis=0, keepdims=True)
    first_high = first.astype(bf16).astype(f32)
    second_high = second.astype(bf16).astype(f32)
    row = lax.broadcasted_iota(jnp.int32, (16, rows), 0)
    extra = jnp.where(row == 0, first_high, 0.0)
    extra = jnp.where(row == 1, second_high, extra)
    extra = jnp.where(row == 2, first - first_high, extra)
    extra = jnp.where(row == 3, second - second_high, extra).astype(bf16)
    zh = where_ref[0]
    for x in range(4):
        for core in range(2):
            for side in range(2):
                start = pl.multiple_of(jnp.where(side == zh, width, 0), width)
                mixed_ref[x * 2 + core, pl.ds(start, width)] = partial[x, side, core]
            mixed_ref[x * 2 + core, 2 * width :] = extra
    finished.append(copy(mixed_ref, mixed_out))

    piece = grads_ref.shape[2]
    kernel = jnp.transpose(kernel_ref[...])[:piece]
    kernel = jnp.concatenate([kernel, jnp.zeros((piece, 128 - width), f32)], axis=1)
    lane = lax.broadcasted_iota(jnp.int32, (piece, 128), 1)
    for source, factor, start, by, first in (
        (normed_ref, both_ref, 0, 64, 64),
        (full_ref, act_ref, 256, 32, 96),
    ):
        rest = -factor.shape[0] % 128
        part = lax.dot_general(
            source[:, :, :rows].reshape(model, rows),
            jnp.concatenate([factor[...], jnp.zeros((rest, rows), bf16)], axis=0),
            OVER,
            preferred_element_type=f32,
        )
        size = part.shape[1]
        part = part.reshape(8, 4, piece, size)
        taps_here = jnp.where(lane >= first, pltpu.roll(kernel, by, 1), 0.0)
        if size > 128:
            grads_ref[:, :, :, start : start + size - 128] = part[..., : size - 128].astype(bf16)
        grads_ref[:, :, :, start + size - 128 : start + size] = (
            part[..., size - 128 :] + taps_here
        ).astype(bf16)
    for step, out in zip((0, 1, 3, 2), (part0_out, part1_out, part2_out, part3_out)):
        out[...] = grads_ref[:, lax.rem(where_ref[2] + step, 4)]
    for started in finished:
        started.wait()


def on_device(
    inputs,
    norm_gain,
    norm_bias,
    value_weight,
    gate_weight,
    conv_kernel,
    project_weight,
    frame_mask,
    upstream,
):
    width, rows = inputs.shape
    model = value_weight.shape[1]
    taps = conv_kernel.shape[0]
    lanes = rows + 128
    piece = model // 32
    zh = lax.axis_index("zh")
    core = lax.axis_index("core")
    y = lax.axis_index("y")
    zl = lax.axis_index("zl")
    offset = lax.axis_index(CHAN) * width
    where = jnp.stack([zh, core, y]).astype(jnp.int32)

    to_right, to_left = call(
        edges,
        (shape((width + 16, 128), bf16), shape((width + 16, 128), bf16)),
        scratch=(pltpu.VMEM((2, 2, width, 128), bf16), pltpu.SemaphoreType.DMA((4,))),
        specs=[pl.BlockSpec(memory_space=pltpu.HBM)] * 2 + [VMEM],
    )(
        pltpu.with_memory_space_constraint(inputs, pltpu.HBM),
        pltpu.with_memory_space_constraint(upstream, pltpu.HBM),
        frame_mask,
    )
    edge = lax.ppermute(to_right, FRAME, [(i, i + 1) for i in range(31)]) + lax.ppermute(
        to_left, FRAME, [(i + 1, i) for i in range(31)]
    )

    weights = jnp.concatenate([value_weight, gate_weight])
    by_gain = jnp.sum(weights.astype(f32) * norm_gain[None, :], axis=1, keepdims=True)
    by_bias = jnp.sum(weights.astype(f32) * norm_bias[None, :], axis=1, keepdims=True)
    gain_local = lax.dynamic_slice_in_dim(norm_gain, offset, width, 0)[:, None]

    def columns_of(parameter):
        parameter = parameter.reshape(4, 2, 2, width)
        parameter = jnp.where(zh == 0, parameter, parameter[:, ::-1])
        parameter = jnp.where(core == 0, parameter, parameter[:, :, ::-1])
        return parameter.reshape(16, width).T

    small = jnp.concatenate([columns_of(norm_gain), columns_of(norm_bias)], axis=1)
    small = jnp.concatenate(
        [
            jnp.pad(small, ((0, width), (0, 0))),
            by_gain,
            by_bias,
            jnp.pad(conv_kernel.T, ((0, width), (0, 128 - 34 - taps))),
        ],
        axis=1,
    )
    early = (weights, weights.T, small, gain_local, where)

    held = jnp.concatenate([inputs, edge[:width], upstream], axis=1)
    keep = jnp.concatenate([frame_mask.astype(f32)[None, :], edge[width : width + 1].astype(f32)], axis=1)
    came = swap(held, "zh")
    came, keep, early = lax.optimization_barrier((came, keep, early))
    weights, flipped, small, gain_local, where = early
    far_inputs = came[:, :rows]
    own = over_x(jnp.stack([held, came]))
    other = swap(own, "core")
    piece_shape = (8, piece, 4 * width)
    operands = (own, other, small, weights, project_weight, flipped, keep)
    mixed, *pieces, stats = pl.pallas_call(
        middle,
        out_shape=(
            pltpu.HBM((8, 2 * width + 16, rows), bf16),
            *(pltpu.VMEM(piece_shape, bf16) for _ in range(4)),
            pltpu.HBM((8, lanes), f32),
        ),
        in_specs=[SMEM] + [pl.BlockSpec(memory_space=pltpu.HBM)] * len(operands),
        out_specs=tuple(pl.BlockSpec(memory_space=pltpu.HBM if i in (0, 5) else pltpu.VMEM) for i in range(6)),
        scratch_shapes=[pltpu.VMEM(operand.shape, operand.dtype) for operand in operands]
        + [
            pltpu.VMEM((taps, width, 128), f32),
            pltpu.VMEM((8, 2 * width + 16, rows), bf16),
            pltpu.VMEM((8, 4, piece, 4 * width), bf16),
            pltpu.VMEM((8, lanes), f32),
            pltpu.VMEM((16, width, lanes), bf16),
            pltpu.VMEM((16, width, lanes), bf16),
            pltpu.VMEM((2 * width, rows), bf16),
            pltpu.VMEM((width, rows), bf16),
            pltpu.VMEM((width, 128), f32),
            pltpu.VMEM((2 * width, lanes), f32),
            pltpu.VMEM((width, lanes), f32),
            pltpu.VMEM((8, 32, lanes), f32),
            pltpu.VMEM((8, 32, lanes), f32),
            pltpu.SemaphoreType.DMA((20,)),
        ],
        compiler_params=pltpu.CompilerParams(vmem_limit_bytes=40 << 20),
    )(where, *(pltpu.with_memory_space_constraint(operand, pltpu.HBM) for operand in operands))

    mixed = lax.all_to_all(mixed, ("x", "core"), 0, 0, tiled=True)

    parts = [
        lax.ppermute(sent, "y", [(i, (i + step) % 4) for i in range(4)])
        for step, sent in zip((1, 3, 2), pieces[1:])
    ]
    total = pieces[0].astype(f32)
    for part in parts:
        total = total + part.astype(f32)

    side = zl % 2
    total = total.reshape(4, 2, piece, 4 * width)
    sent = lax.dynamic_slice_in_dim(total, 1 - side, 1, 1)[:, 0].astype(bf16)
    total = lax.dynamic_slice_in_dim(total, side, 1, 1)[:, 0]
    sent, mixed = lax.optimization_barrier((sent, mixed))
    total = total + lax.ppermute(sent, "zl", [(i, i ^ 1) for i in range(8)]).astype(f32)

    mixed = jnp.sum(mixed.astype(f32), axis=0)
    near = mixed[width : 2 * width]
    inv_std = stats[1:2, :rows]
    centred = (inputs.astype(f32) - stats[0:1, :rows]) * inv_std
    centred_far = (far_inputs.astype(f32) - stats[0:1, :rows]) * inv_std
    near_tail = jnp.stack([jnp.sum(near * centred, axis=1), jnp.sum(near, axis=1)])
    far_tail = jnp.stack([jnp.sum(mixed[:width] * centred_far, axis=1), jnp.sum(mixed[:width], axis=1)])
    tail, near = lax.optimization_barrier((ordered(near_tail, far_tail, zh, 0), near))
    far_sums = mixed[2 * width : 2 * width + 2] + mixed[2 * width + 2 : 2 * width + 4]
    sent_high, sent_low = split_bf16(far_sums)
    far = jnp.concatenate(
        [mixed[:width].astype(bf16), sent_high, sent_low, jnp.zeros((12, rows), bf16)]
    )
    came = swap(far, "zh").astype(f32)

    tail = lax.all_to_all(
        jnp.broadcast_to(tail[None], (32, 2, 2, width)).reshape(64, 2, width),
        FRAME + ("zh",), 0, 0, tiled=True,
    )

    normed_grad = near + came[:width]
    kept = far[width : width + 4].astype(f32)
    sums = (kept[:2] + kept[2:] + came[width : width + 2] + came[width + 2 : width + 4]) / model
    total, normed_grad = lax.optimization_barrier((total, normed_grad))
    inputs_grad = (
        upstream.astype(f32)
        + inv_std * (normed_grad * gain_local - sums[0:1] - centred * sums[1:2])
    ).astype(bf16)

    for size in (2, 4):
        side = (zl // size) % 2
        total = total.reshape(4 // size, 2, piece, 4 * width)
        sent = lax.dynamic_slice_in_dim(total, 1 - side, 1, 1)[:, 0].astype(bf16)
        total = lax.dynamic_slice_in_dim(total, side, 1, 1)[:, 0]
        total = total + lax.ppermute(sent, "zl", [(i, i ^ size) for i in range(8)]).astype(f32)
    grads = total[0]
    tail, grads = lax.optimization_barrier((tail, grads))
    tail = jnp.sum(tail, axis=0)
    kernel_grad = jnp.concatenate([grads[:taps, 192:256], grads[:taps, 352:384]], axis=1)
    value_grad = grads[:, :width].T
    gate_grad = grads[:, width : 2 * width].T
    project_grad = grads[:, 256 : 256 + width].T
    return (inputs_grad, value_grad, gate_grad, project_grad, kernel_grad, tail[0], tail[1])


def solution(mesh):
    split = Mesh(mesh.devices.reshape(8, 4, 4, 2, 2), FRAME + CHAN)
    return jax.shard_map(
        on_device,
        mesh=split,
        in_specs=(
            P(CHAN, FRAME),
            P(),
            P(),
            P(CHAN, None),
            P(CHAN, None),
            P(None, CHAN),
            P(CHAN, None),
            P(FRAME),
            P(CHAN, FRAME),
        ),
        out_specs=(
            P(CHAN, FRAME),
            P(CHAN, FRAME),
            P(CHAN, FRAME),
            P(CHAN, FRAME),
            P(None, CHAN),
            P(CHAN),
            P(CHAN),
        ),
        check_vma=False,
    )
```
